32 devices in a mesh: group: 2 (over y), tm: 4 (over z), tensor: 2 (over x), dp: 2 (over core).
Axes of the slice: x: 2, y: 2, z: 4, core: 2. Of those that a mesh axis runs over, the one named last changes fastest.
Arguments:
- frames_in: bfloat16 [4, 3072, 1024], P(('group', 'dp'), 'tm', 'tensor'), parts along dimension 0, may hold values from -6 to 6
- in_proj: bfloat16 [2, 1024, 1024], P(None, None, 'tensor'), may hold values from -0.1875 to 0.1875
- log_rates: float32 [8, 8], P(None, 'tensor'), as said below
- angles: float32 [8, 8], P(None, 'tensor'), may hold values from -3.140625 to 3.140625
- residues: float32 [2, 8, 1024], P(None, None, 'tensor'), may hold values from -3 to 3
- skip_gain: float32 [1024], P('tensor'), may hold values from -3 to 3
- lengths: int32 [4, 4], P(('group', 'dp')), parts along dimension 0, may hold values from 1 to 1536, 3072 in all within a row
- grad_out: bfloat16 [4, 3072, 1024], P(('group', 'dp'), 'tm', 'tensor'), parts along dimension 0, may hold values from -6 to 6
Outputs:
- mixed: bfloat16 [4, 3072, 1024], P(('group', 'dp'), 'tm', 'tensor'), parts along dimension 0
- input_grad: bfloat16 [4, 3072, 1024], P(('group', 'dp'), 'tm', 'tensor'), parts along dimension 0
- proj_grad: float32 [4, 1024, 1024], P('group', None, 'tensor'), parts along dimension 0
- residue_grad: float32 [4, 8, 1024], P('group', None, 'tensor'), parts along dimension 0
- skip_grad: float32 [2048], P(('group', 'tensor')), parts along dimension 0
The draws below stay inside these ranges and needn't reach their ends.
There are 2 independent parts, one for each index of `group`. The reference program is written for one: setup_inputs(seed, part) draws one part's arguments, and reference() takes and returns one part's arrays. A program takes and returns all parts, laid end to end along the dimension named above; an argument that names none is the same for every part. Nothing has to cross between parts.
Inputs may be any that keep to these rules, and one draw needn't show every extreme that they name: Each clip has at least one frame; the lengths of a stream sum to 3072. `log_rates`: each entry lies between the logarithms of 0.1 / 3072 and 0.08.
All inputs are finite; a program needn't handle non-finite values.
Results may differ from the reference program's by a relative error of at most 0.0058.
Values may be sent and summed in bfloat16 or wider, within the bound.
A program may use at most 128 MiB of HBM per device.

```python
import math
import jax
import jax.numpy as jnp
import numpy as np
from jax import lax

HEADS = 8
HEAD_DIM = 128
WIDTH = 1024
MODES = 8
BLOCK_LEN = 128
CLIPS = 4
FRAMES = 3072
STREAMS = 2


def draw_log_rates(key, part):
    key_mask, key_slow, key_fast = jax.random.split(jax.random.fold_in(key, 7), 3)
    slow_share = 0.5
    slow_rates = jax.random.uniform(key_slow, (MODES, HEADS), jnp.float32, math.log(0.1 / FRAMES), math.log(1.0 / FRAMES))
    fast_rates = jax.random.uniform(key_fast, (MODES, HEADS), jnp.float32, math.log(0.03), math.log(0.08))
    picker = jax.random.uniform(key_mask, (MODES, HEADS), jnp.float32)
    return jnp.where(picker < slow_share, slow_rates, fast_rates)


def block_scale(rng, shape, pieces, smallest, largest):
    def one(dim, blocks):
        heights = jax.random.uniform(jax.random.fold_in(jax.random.fold_in(rng, 6), dim), (blocks,), jnp.float32, smallest / len(pieces), largest / len(pieces))
        return jnp.repeat(jnp.exp(heights), shape[dim] // blocks).reshape((-1,) + (1,) * (len(shape) - dim - 1))

    level = one(*pieces[0])
    for cut in pieces[1:]:
        level = level * one(*cut)
    return level


def split_up(number_of, total, limit, lean):
    loads = [(1 << 20) // math.isqrt(rank ** lean) + 1 for rank in range(2, number_of + 1)]
    rest, given = total - limit - (number_of - 1), [1] * (number_of - 1)
    while rest > 0:
        candidates = [i for i in range(number_of - 1) if given[i] < limit]
        mass, budget = sum([loads[i] for i in candidates]), rest
        for i in candidates:
            extra = min(limit - given[i], max(1, budget * loads[i] // mass), rest)
            given[i] = given[i] + extra
            rest = rest - extra
    return np.array([limit] + given)


def uneven(stream_key, count, total, most, slope):
    if count == 2:
        one = jax.random.randint(stream_key, (), max(1, total - most), min(most, total - 1) + 1)
        return jnp.stack([one, total - one])
    tallies = jnp.asarray(split_up(count, total, most, slope), jnp.int32)
    twos = (count - 1) // 2
    source_of, taker = tallies[1:1 + 2 * twos:2], tallies[2:2 + 2 * twos:2]
    slack = jnp.minimum(source_of - 1, most - taker)
    shifted = jax.random.randint(jax.random.fold_in(stream_key, 1), (twos,), 0, 1 << 20) % (slack + 1)
    tallies = tallies.at[1:1 + 2 * twos:2].set(source_of - shifted).at[2:2 + 2 * twos:2].set(taker + shifted)
    return tallies[jax.random.permutation(jax.random.fold_in(stream_key, 2), count)]


def noise(stream_key, dims, width, bound, cuts=(), kind=jnp.bfloat16):
    values = width * jax.random.normal(stream_key, dims, jnp.float32)
    if cuts:
        values = values * block_scale(stream_key, dims, cuts, -0.22, 0.18)
    return jnp.clip(values, -bound, bound).astype(kind)


def setup_inputs(seed: int = 0, part: int = 0) -> dict:
    keys = jax.random.split(jax.random.key(seed), 9)
    part_splits = jax.random.split(jax.random.fold_in(keys[8], part), 9)
    frames_in = noise(part_splits[0], (STREAMS, FRAMES, WIDTH), 1.0, 6.0, ((0, 2), (1, 4), (2, 2)))
    in_proj = noise(keys[1], (2, WIDTH, WIDTH), WIDTH ** -0.5, 0.1875, ((2, 2),))
    log_rates = draw_log_rates(jax.random.fold_in(keys[8], 71), part)
    angles = jnp.clip(jax.random.uniform(keys[3], (MODES, HEADS), jnp.float32, -3.140625, 3.140625), -3.140625, 3.140625)
    residues = noise(keys[4], (2, MODES, WIDTH), 0.5, 3.0, ((2, 2),), jnp.float32)
    skip_gain = noise(keys[5], (WIDTH,), 0.5, 3.0, ((0, 2),), jnp.float32)
    lengths = jax.vmap(lambda own: uneven(own, CLIPS, FRAMES, FRAMES // 2, 2))(jax.random.split(part_splits[6], STREAMS)).reshape((STREAMS, CLIPS)).astype(jnp.int32)
    grad_out = noise(part_splits[7], (STREAMS, FRAMES, WIDTH), 1.0, 6.0, ((0, 2), (1, 4), (2, 2)))
    return {"frames_in": frames_in, "in_proj": in_proj, "log_rates": log_rates, "angles": angles, "residues": residues, "skip_gain": skip_gain, "lengths": lengths, "grad_out": grad_out}


def pole_terms(log_rates, angles):
    decay_rate = jnp.exp(log_rates)
    magnitude = jnp.exp(-decay_rate)
    weight = jnp.sqrt(-jnp.expm1(-2.0 * decay_rate))
    return (magnitude * jnp.cos(angles), magnitude * jnp.sin(angles), weight)

def long_conv(signal, coeffs, skip_vec, pole_real, pole_imag, weight, keep_mask):
    streams, frames, features = signal.shape
    coefficient_real = coeffs[0].reshape(MODES, HEADS, HEAD_DIM) * weight[:, :, None]
    coefficient_imaginary = coeffs[1].reshape(MODES, HEADS, HEAD_DIM) * weight[:, :, None]
    skip_row = skip_vec.reshape(HEADS, HEAD_DIM)
    blocks = frames // BLOCK_LEN
    inputs = signal.reshape(streams, blocks, BLOCK_LEN, HEADS, HEAD_DIM).transpose(1, 2, 0, 3, 4)
    resets = keep_mask.reshape(streams, blocks, BLOCK_LEN).transpose(1, 2, 0)
    real_part = pole_real[None, :, :, None]
    imag_part = pole_imag[None, :, :, None]

    def frame_step(carried, element):
        state_re, state_im = carried
        current, kept = element
        factor = kept[:, None, None, None]
        next_re = factor * (real_part * state_re - imag_part * state_im) + current[:, None]
        next_im = factor * (real_part * state_im + imag_part * state_re)
        output = skip_row * current + lax.optimization_barrier(jnp.sum(coefficient_real * next_re - coefficient_imaginary * next_im, axis=1))
        return ((next_re, next_im), output)

    def block_step(carried, element):
        return lax.scan(frame_step, carried, element)
    initial = jnp.zeros((streams, MODES, HEADS, HEAD_DIM), jnp.float32)
    _, outputs = lax.scan(jax.checkpoint(block_step), (initial, initial), (inputs, resets))
    return outputs.transpose(2, 0, 1, 3, 4).reshape(streams, frames, features)

def reference(frames_in, in_proj, log_rates, angles, residues, skip_gain, lengths, grad_out):
    inputs32 = frames_in.astype(jnp.float32)
    weights32 = in_proj.astype(jnp.float32)
    query_rows = jnp.einsum('bfd,dc->bfc', inputs32, weights32[0]).astype(jnp.bfloat16)
    signal = jnp.einsum('bfd,dc->bfc', inputs32, weights32[1]).astype(jnp.bfloat16)
    pole_real, pole_imag, weight = pole_terms(log_rates, angles)
    clip_start = (jnp.cumsum(lengths, axis=1) - lengths).astype(jnp.int32)
    frame_ids = jnp.arange(FRAMES, dtype=jnp.int32)
    is_start = jnp.any(frame_ids[None, :, None] == clip_start[:, None, :], axis=2)
    keep_mask = jnp.where(is_start, 0.0, 1.0).astype(jnp.float32)

    def convolve(signal32, coeffs, skip_vec):
        return long_conv(signal32, coeffs, skip_vec, pole_real, pole_imag, weight, keep_mask)
    long_out, pullback = jax.vjp(convolve, signal.astype(jnp.float32), residues, skip_gain)
    query32 = query_rows.astype(jnp.float32)
    upstream = grad_out.astype(jnp.float32)
    mixed = (query32 * long_out).astype(jnp.bfloat16)
    grad_long = upstream * query32
    grad_query = (upstream * long_out).astype(jnp.bfloat16)
    grad_signal, grad_coeffs, grad_skip = pullback(grad_long)
    grad_value = grad_signal.astype(jnp.bfloat16)
    query_grad32 = grad_query.astype(jnp.float32)
    value_grad32 = grad_value.astype(jnp.float32)
    input_grad = (jnp.einsum('bfc,dc->bfd', query_grad32, weights32[0]) + jnp.einsum('bfc,dc->bfd', value_grad32, weights32[1])).astype(jnp.bfloat16)
    norm_scale = 1.0 / math.sqrt(FRAMES * STREAMS)
    proj_grad = jnp.stack([jnp.einsum('bfd,bfc->dc', inputs32, query_grad32), jnp.einsum('bfd,bfc->dc', inputs32, value_grad32)]) * norm_scale
    return (mixed, input_grad, proj_grad, grad_coeffs * norm_scale, grad_skip * norm_scale)
```

```python
import functools
import math

import jax
import jax.numpy as jnp
from jax import lax
from jax.experimental import pallas as pl
from jax.experimental.pallas import tpu as pltpu
from jax.sharding import PartitionSpec as P

F32 = jnp.float32
BF16 = jnp.bfloat16
MESH = pl.DeviceIdType.MESH
Q = 16
B = 128
STEP = 64


def dot(a, b):
    return jnp.dot(a, b, preferred_element_type=F32)


def dot_nt(a, b):
    return lax.dot_general(a, b, (((1,), (1,)), ((), ())), preferred_element_type=F32)


def flag(cond):
    return jnp.where(cond, 1.0, 0.0).astype(F32)


def rows_at(start, size, step=8):
    return pl.ds(pl.multiple_of(start, step), size)


class Chain:
    def __init__(self, axis, acc, snd, upb, inb, tot, sems, steps, nch, size, half, tot_rows, core):
        n, z = lax.axis_size(axis), lax.axis_index(axis)
        self.axis, self.n = axis, n
        left = z < n // 2
        self.side = jnp.where(left, 0, 1)
        self.inward = jnp.where(left, z + 1, z - 1)
        self.outward = jnp.clip(jnp.where(left, z - 1, z + 1), 0, n - 1)
        self.depth = jnp.where(left, n // 2 - 1 - z, z - n // 2)
        self.root = self.depth == 0
        self.inner = self.depth > 0
        self.has_out = self.depth < n // 2 - 1
        self.no_out = self.depth == n // 2 - 1
        self.acc, self.snd, self.upb, self.inb, self.tot = acc, snd, upb, inb, tot
        (self.up_s, self.up_r, self.in_r, self.ti_s, self.to_s, self.tot_r, self.dp_s, self.dp_r) = sems
        self.steps, self.nch, self.size, self.half, self.tot_rows, self.core = steps, nch, size, half, tot_rows, core
        self.wire = snd.dtype

    def off(self, far):
        return jnp.where(self.side == far, 0, self.half // 2)

    def row(self, s, far):
        r = (s // self.nch) * self.half + self.off(far) + (s % self.nch) * self.size
        return rows_at(r, self.size)

    def total_row(self, s, far, core):
        r = (s // self.nch) * self.tot_rows + core * self.half + self.off(far) + (s % self.nch) * self.size
        return rows_at(r, self.size)

    def copy(self, src, dst, send, recv, to):
        return pltpu.make_async_remote_copy(
            src_ref=src, dst_ref=dst, send_sem=send, recv_sem=recv, device_id=to, device_id_type=MESH
        )

    def up_copy(self, s, far):
        r = self.row(s, far)
        return self.copy(self.snd.at[r], self.upb.at[r], self.up_s.at[far, s], self.up_r.at[far, s], {self.axis: self.inward})

    def in_copy(self, s):
        r = self.row(s, 1)
        dst = self.inb.at[rows_at(s * self.size, self.size)]
        return self.copy(self.snd.at[r], dst, self.up_s.at[1, s], self.in_r.at[s], {self.axis: self.inward})

    def across_copy(self, s):
        r = self.total_row(s, 0, self.core)
        return self.copy(self.tot.at[r], self.tot.at[r], self.ti_s.at[s], self.tot_r.at[1, s], {self.axis: self.inward})

    def out_copy(self, s, far):
        r = self.total_row(s, far, self.core)
        return self.copy(
            self.tot.at[r], self.tot.at[r], self.to_s.at[far, s], self.tot_r.at[far, s], {self.axis: self.outward}
        )

    def dp_copy(self, s, far, core):
        r = self.total_row(s, far, core)
        return self.copy(
            self.tot.at[r], self.tot.at[r], self.dp_s.at[far, s], self.dp_r.at[far, s], {"dp": 1 - self.core}
        )

    def gathered(self, s, far):
        @pl.when(self.has_out)
        def _():
            r = self.row(s, far)
            self.up_copy(s, far).wait_recv()
            self.acc[r] = self.acc[r] + self.upb[r].astype(F32)

    def up_far(self, s):
        self.gathered(s, 1)
        r = self.row(s, 1)
        self.snd[r] = self.acc[r].astype(self.wire)

        @pl.when(self.inner)
        def _():
            self.up_copy(s, 1).start()

        @pl.when(self.root)
        def _():
            self.in_copy(s).start()

    def up_near(self, s):
        self.gathered(s, 0)
        r = self.row(s, 0)

        @pl.when(self.inner)
        def _():
            self.snd[r] = self.acc[r].astype(self.wire)
            self.up_copy(s, 0).start()

        @pl.when(self.root)
        def _():
            self.in_copy(s).wait_recv()
            total = self.acc[r] + self.inb[rows_at(s * self.size, self.size)].astype(F32)
            self.tot[self.total_row(s, 0, self.core)] = total.astype(self.wire)
            self.across_copy(s).start()
            self.dp_copy(s, 0, self.core).start()

            @pl.when(self.has_out)
            def _():
                self.out_copy(s, 0).start()

    def down(self, s, far):
        def go():
            self.out_copy(s, far).wait_recv()

            @pl.when(self.has_out)
            def _():
                self.out_copy(s, far).start()

            self.dp_copy(s, far, self.core).start()

        if far:
            go()
        else:
            pl.when(self.inner)(go)

    def finish(self, s):
        for far in (0, 1):
            self.dp_copy(s, far, self.core).wait_send()
            self.dp_copy(s, far, 1 - self.core).wait_recv()

            @pl.when(self.has_out)
            def _():
                self.out_copy(s, far).wait_send()

            @pl.when(self.inner)
            def _():
                self.up_copy(s, far).wait_send()

        @pl.when(self.root)
        def _():
            self.in_copy(s).wait_send()
            self.across_copy(s).wait_send()


def layer_kernel(
    cfg,
    lens_ref, rates_ref, angles_ref, resid_ref, skip_ref, frames_ref, proj_ref, up_hbm,
    mixed_out, ig_out, pg_out, res_out, skip_out,
    feat, feat_t, proj, up, q_s, x_scr, g_scr, y_scr, gx_scr, xb_s, gb_s, gm_s, y_loc, gx_loc, gq, gv, mixed_v,
    a1_s, a2_s, bt_s, b1_s, b2_s, colp_s, colh_s, pk_s, pos_s, pstep_s, w_s, k_s, wgt_s,
    ma1_s, ma2_s, keep_s, km_s, mb1_s, mb2_s,
    u_s, d_s, lead_s, g_end, r_s, rc_s, ent_s, lea_s, endf_r, endb_r,
    pacc, psnd, dpsnd, dprcv, upb, inb, tot, macc, msnd, mdps, mdpr, mupb, minb, mtot, igs, igr, iga,
    loc_sem, f_s, f_r, ef_s, ef_r, eb_s, eb_r, dps_s, dps_r, ig_s, ig_r, md_s, md_r, out_sem,
    *chain_sems,
):
    clips, M, H, R, C, D, norm = cfg
    nb = R // B
    n, z = lax.axis_size("tm"), lax.axis_index("tm")
    nt, t_me = lax.axis_size("tensor"), lax.axis_index("tensor")
    core = lax.axis_index("dp")
    first = z * R
    share = D // nt
    half = D // 2
    big_sems, small_sems = chain_sems[:8], chain_sems[8:]
    nch = half // 2 // STEP
    big = Chain("tm", pacc, psnd, upb, inb, tot, big_sems, 2 * nch, nch, STEP, half, D, core)
    small = Chain("tm", macc, msnd, mupb, minb, mtot, small_sems, 1, 1, 8, 16, 32, core)

    clip_starts = [jnp.int32(0)]
    for k in range(clips - 1):
        clip_starts.append(clip_starts[-1] + lens_ref[0, k])

    def seg(frame):
        total = jnp.where(frame >= clip_starts[0], 1, 0)
        for k in range(1, clips):
            total = total + jnp.where(frame >= clip_starts[k], 1, 0)
        return total

    mine = pl.ds(pl.multiple_of(t_me * C, 128), C)
    own_in = pltpu.make_async_copy(frames_ref, feat.at[:, mine], loc_sem.at[0])
    proj_in = pltpu.make_async_copy(proj_ref, proj, loc_sem.at[1])
    up_in = pltpu.make_async_copy(up_hbm, up, loc_sem.at[2])
    own_in.start()
    proj_in.start()
    up_in.start()

    barrier = pltpu.get_barrier_semaphore()
    for k in range(1, nt):
        pl.semaphore_signal(barrier, inc=1, device_id={"tensor": lax.rem(t_me + k, nt)}, device_id_type=MESH)
    pl.semaphore_signal(barrier, inc=1, device_id={"dp": 1 - core}, device_id_type=MESH)
    for k in range(1, n):
        pl.semaphore_signal(barrier, inc=1, device_id={"tm": lax.rem(z + k, n)}, device_id_type=MESH)
    pl.semaphore_wait(barrier, nt + n - 1)

    def feature_copy(k, b, sender):
        rows = rows_at(b * B, B)
        cols = pl.ds(pl.multiple_of(sender * C, 128), C)
        return pltpu.make_async_remote_copy(
            src_ref=frames_ref.at[rows], dst_ref=feat.at[rows, cols], send_sem=f_s.at[k - 1, b],
            recv_sem=f_r.at[k - 1, b], device_id={"tensor": lax.rem(t_me + k, nt)}, device_id_type=MESH,
        )

    for b in range(nb):
        for k in range(1, nt):
            feature_copy(k, b, t_me).start()

    lane = lax.broadcasted_iota(jnp.int32, (8, 128), 1)
    sub = lax.broadcasted_iota(jnp.int32, (8, 128), 0)
    lanef = lane.astype(F32)
    in_chunk = lane % Q
    chunk = lane // Q
    all_decay = jnp.exp(rates_ref[...])
    head_id = lax.broadcasted_iota(jnp.int32, (M, H), 1)

    def tables(h, _):
        pick = head_id == h
        d = jnp.sum(jnp.where(pick, all_decay, 0.0), axis=1, keepdims=True)
        a = jnp.sum(jnp.where(pick, angles_ref[...], 0.0), axis=1, keepdims=True)

        def powers(lag, dd=d, aa=a):
            size = jnp.exp(-dd * lag)
            return size * jnp.cos(aa * lag), size * jnp.sin(aa * lag)

        pos_re, pos_im = powers(lanef)
        nxt_re, nxt_im = powers(lanef + 1.0)
        neg_re, neg_im = powers(-lanef - 1.0)
        end_re, end_im = powers(127.0 - lanef)
        far_re, far_im = powers(128.0 - lanef)
        b1_re, b1_im = powers((in_chunk + 1).astype(F32))
        b2_re, b2_im = powers((Q - in_chunk).astype(F32))
        pos_s[h, 0], pos_s[h, 1] = pos_re, pos_im
        for i, lag in enumerate((1.0, float(B), float(R))):
            pr, pi = powers(jnp.full((M, 128), lag, F32))
            pstep_s[h, i, 0], pstep_s[h, i, 1] = pr, pi
        y = 2.0 * d
        series = y * (1.0 - y / 2 * (1.0 - y / 3 * (1.0 - y / 4 * (1.0 - y / 5 * (1.0 - y / 6 * (1.0 - y / 7))))))
        wgt = jnp.sqrt(jnp.where(y < 0.25, series, 1.0 - jnp.exp(-y)))
        wgt = jnp.broadcast_to(wgt, (M, 128))
        wgt_s[h] = wgt
        wr, wi = resid_ref[0, h] * wgt, resid_ref[1, h] * wgt
        w_s[h, 0], w_s[h, 1] = wr, wi
        for k in range(Q):
            tap = jnp.sum(wr * pos_re[:, k : k + 1] - wi * pos_im[:, k : k + 1], axis=0, keepdims=True)
            if k == 0:
                tap = tap + skip_ref[h]
            k_s[h, k] = jnp.broadcast_to(tap, (8, 128))
        a1r, a1i, a2r, a2i, btr, bti, b2r, b2i = [], [], [], [], [], [], [], []
        subf = sub.astype(F32) * Q
        for m in range(M):
            one = slice(m, m + 1)
            pr, pi = powers(subf, d[one], a[one])
            pk_s[h, 0, m * 8 : m * 8 + 8], pk_s[h, 1, m * 8 : m * 8 + 8] = pr, pi
            back_re, back_im = powers(-subf - float(Q), d[one], a[one])
            fr, fi = neg_re[one], neg_im[one]
            past = lane < sub * Q
            a1r.append(jnp.where(past, pr * fr - pi * fi, 0.0))
            a1i.append(jnp.where(past, pr * fi + pi * fr, 0.0))
            fr, fi = pos_re[one], pos_im[one]
            later = lane >= (sub + 1) * Q
            a2r.append(jnp.where(later, back_re * fr - back_im * fi, 0.0))
            a2i.append(jnp.where(later, back_re * fi + back_im * fr, 0.0))
            here = chunk == sub
            btr.append(jnp.where(here, b1_re[one], 0.0))
            bti.append(jnp.where(here, b1_im[one], 0.0))
            b2r.append(jnp.where(here, b2_re[one], 0.0))
            b2i.append(jnp.where(here, b2_im[one], 0.0))
        a1_s[h] = jnp.concatenate(a1r + a1i + [end_re, end_im], axis=0).astype(BF16)
        a2_s[h] = jnp.concatenate(a2r + a2i + [pos_re, pos_im], axis=0).astype(BF16)
        bt = jnp.concatenate(btr + bti, axis=0)
        bt_s[h] = bt.astype(BF16)
        b1_s[h] = bt.T.astype(BF16)
        b2_s[h] = jnp.concatenate(b2r + b2i, axis=0).T.astype(BF16)
        pad = [jnp.zeros((128 - 2 * M, 128), F32)]
        colp_s[h] = jnp.concatenate([nxt_re, nxt_im] + pad, axis=0).T.astype(BF16)
        colh_s[h] = jnp.concatenate([far_re, far_im] + pad, axis=0).T.astype(BF16)
        return 0

    lax.fori_loop(0, H, tables, 0)
    u_s[...] = jnp.zeros_like(u_s)
    r_s[...] = jnp.zeros_like(r_s)
    rc_s[...] = jnp.zeros_like(rc_s)
    own_in.wait()
    proj_in.wait()
    up_in.wait()

    def head(b, keep_block, h):
        rows = rows_at(b * B, B)
        xs = [x_scr[h, pl.ds(i, 8, stride=Q), :] for i in range(Q)]
        gs = [g_scr[h, pl.ds(i, 8, stride=Q), :] for i in range(Q)]
        held, corr = [], [None] * Q
        for i in range(Q):
            if i:
                kept = keep_s[i]
                held = [v * kept for v in held]
            held.append(xs[i])
            acc = None
            for s in range(i + 1):
                lag = i - s
                term = k_s[h, lag] * held[s]
                acc = term if acc is None else acc + term
                both = gs[i] * held[s]
                corr[lag] = both if corr[lag] is None else corr[lag] + both
            y_scr[h, pl.ds(i, 8, stride=Q), :] = acc
        for lag in range(Q):
            r_s[h, lag] += corr[lag]
        held = []
        for s in reversed(range(Q)):
            if s < Q - 1:
                kept = keep_s[s + 1]
                held = [v * kept for v in held]
            held = [gs[s]] + held
            acc = None
            for lag in range(Q - s):
                term = k_s[h, lag] * held[lag]
                acc = term if acc is None else acc + term
            gx_scr[h, pl.ds(s, 8, stride=Q), :] = acc

        states = dot(a1_s[h] * ma1_s[...], xb_s[h])
        leads = dot(bt_s[h], gm_s[h])
        adj = dot(a2_s[h] * ma2_s[...], gb_s[h])
        kept = km_s[...]
        vr, vi, ar, ai = [], [], [], []
        for m in range(M):
            re, im = slice(m * 8, m * 8 + 8), slice(64 + m * 8, 72 + m * 8)
            pr, pi = pk_s[h, 0, re] * kept, pk_s[h, 1, re] * kept
            ur, ui = u_s[h, m : m + 1, :], u_s[h, M + m : M + m + 1, :]
            sr = states[re] + (pr * ur - pi * ui)
            si = states[im] + (pr * ui + pi * ur)
            lr, li = leads[re], leads[im]
            rc_s[h, m] += sr * lr - si * li
            rc_s[h, M + m] += sr * li + si * lr
            wr, wi = w_s[h, 0, m : m + 1, :], w_s[h, 1, m : m + 1, :]
            vr.append(wr * sr - wi * si)
            vi.append(-(wr * si + wi * sr))
            ar.append(wr * adj[re] - wi * adj[im])
            ai.append(-(wr * adj[im] + wi * adj[re]))
        v = jnp.concatenate(vr + vi, axis=0).astype(BF16)
        y_loc[h, rows, :] = y_scr[h] + mb1_s[...] * dot(b1_s[h], v)
        v = jnp.concatenate(ar + ai, axis=0).astype(BF16)
        gx_loc[h, rows, :] = gx_scr[h] + mb2_s[...] * dot(b2_s[h], v)
        lead_s[b, h] = adj[128:]
        pr, pi = pstep_s[h, 1, 0] * keep_block, pstep_s[h, 1, 1] * keep_block
        ur, ui = u_s[h, :M, :], u_s[h, M:, :]
        u_s[h, :M, :] = states[128 : 128 + M] + (pr * ur - pi * ui)
        u_s[h, M:, :] = states[128 + M :] + (pr * ui + pi * ur)

    col = lax.broadcasted_iota(jnp.int32, (B, 128), 0)

    def block(b, _):
        begin = first + b * B
        rows = rows_at(b * B, B)
        seg_t = seg(begin + lane)
        same = flag(seg_t == seg(begin + sub * Q - 1))
        ma1_s[...] = jnp.concatenate([same] * 16 + [flag(seg_t == seg(begin + B - 1))] * 2, axis=0).astype(BF16)
        same = flag(seg_t == seg(begin + (sub + 1) * Q))
        ma2_s[...] = jnp.concatenate([same] * 16 + [flag(seg_t == seg(begin))] * 2, axis=0).astype(BF16)
        km_s[...] = flag(seg(begin + sub * Q - 1) == seg(begin - 1))
        for i in range(Q):
            at = begin + sub * Q + i
            keep_s[i] = flag(seg(at) == seg(at - 1))
        seg_c = seg(begin + col)
        mb1_s[...] = flag(seg_c == seg(begin + (col // Q) * Q - 1))
        mb2_s[...] = flag(seg_c == seg(begin + (col // Q + 1) * Q))
        keep_block = flag(seg(begin + B - 1) == seg(begin - 1))

        for k in range(1, nt):
            feature_copy(k, b, lax.rem(t_me - k + nt, nt)).wait_recv()
        fb = feat[rows, :]
        query = dot(fb, proj[0]).astype(BF16)
        signal = dot(fb, proj[1]).astype(BF16)
        q_s[rows, :] = query
        g = query.astype(F32) * up[rows, :].astype(F32)
        signal32 = signal.astype(F32)
        for h in range(H):
            cols = slice(h * 128, h * 128 + 128)
            x_scr[h] = signal32[:, cols]
            g_scr[h] = g[:, cols]
            xb_s[h] = signal[:, cols]
            gb_s[h] = g[:, cols].astype(BF16)
            gm_s[h] = (g[:, cols] * mb1_s[...]).astype(BF16)
        feat_t[b] = fb.T

        def one(h, _):
            head(b, keep_block, h)
            return 0

        lax.fori_loop(0, H, one, 0)
        return 0

    lax.fori_loop(0, nb, block, 0)

    def turned(h, which, re, im, kept):
        pr, pi = pstep_s[h, which, 0] * kept, pstep_s[h, which, 1] * kept
        return pr * re - pi * im, pr * im + pi * re

    def reverse_scan(start, store):
        state = start
        for b in reversed(range(nb)):
            begin = first + b * B
            kept = flag(seg(begin) == seg(begin + B))
            following = []
            for h in range(H):
                re, im = state[h]
                if store:
                    g_end[b, h, :M, :], g_end[b, h, M:, :] = re, im
                tr, ti = turned(h, 1, re, im, kept)
                following.append((lead_s[b, h, :M, :] + tr, lead_s[b, h, M:, :] + ti))
            state = following
        return state

    zero = jnp.zeros((M, 128), F32)
    ends = reverse_scan([(zero, zero)] * H, False)
    for h in range(H):
        d_s[h, :M, :], d_s[h, M:, :] = ends[h]

    def end_copy(src, dst, send, recv, slot, to):
        return pltpu.make_async_remote_copy(
            src_ref=src, dst_ref=dst.at[slot], send_sem=send.at[to], recv_sem=recv.at[slot],
            device_id={"tm": to}, device_id_type=MESH,
        )

    def forward_copy(slot, to):
        return end_copy(u_s, endf_r, ef_s, ef_r, slot, to)

    def backward_copy(slot, to):
        return end_copy(d_s, endb_r, eb_s, eb_r, slot, to)

    def send_ends(to, _):
        @pl.when(to > z)
        def _():
            forward_copy(z, to).start()

        @pl.when(to < z)
        def _():
            backward_copy(z, to).start()

        return 0

    lax.fori_loop(0, n, send_ends, 0)
    ent_s[...] = jnp.zeros_like(ent_s)
    lea_s[...] = jnp.zeros_like(lea_s)

    def enter(src, _):
        @pl.when(src < z)
        def _():
            forward_copy(src, z).wait_recv()
            kept = flag(seg(src * R - 1) == seg(src * R + R - 1))
            for h in range(H):
                tr, ti = turned(h, 2, ent_s[h, :M, :], ent_s[h, M:, :], kept)
                ent_s[h, :M, :] = endf_r[src, h, :M, :] + tr
                ent_s[h, M:, :] = endf_r[src, h, M:, :] + ti

        return 0

    lax.fori_loop(0, n, enter, 0)

    def weigh(h, re, im):
        wr, wi = w_s[h, 0], w_s[h, 1]
        pad = [jnp.zeros((128 - 2 * M, 128), F32)]
        return jnp.concatenate([wr * re - wi * im, -(wr * im + wi * re)] + pad, axis=0).astype(BF16)

    kept_first = flag(seg(first) == seg(first - 1))
    for h in range(H):
        lr, li = turned(h, 0, d_s[h, :M, :], d_s[h, M:, :], kept_first)
        er, ei = ent_s[h, :M, :], ent_s[h, M:, :]
        re, im = [], []
        for m in range(M):
            re.append(jnp.sum(rc_s[h, m], axis=0, keepdims=True))
            im.append(jnp.sum(rc_s[h, M + m], axis=0, keepdims=True))
        re = jnp.concatenate(re, axis=0) + er * lr - ei * li
        im = jnp.concatenate(im, axis=0) + er * li + ei * lr
        for lag in range(Q):
            r = jnp.sum(r_s[h, lag], axis=0, keepdims=True)
            if lag == 0:
                skip_row = r
            re = re + pos_s[h, 0, :, lag : lag + 1] * r
            im = im + pos_s[h, 1, :, lag : lag + 1] * r
        cols = slice(h * 128, h * 128 + 128)
        scale = wgt_s[h] * norm
        terms = jnp.concatenate([re * scale, -im * scale, skip_row * norm, jnp.zeros((15, 128), F32)], axis=0)
        own = rows_at(core * 16, 16)
        mdps[:, cols] = jnp.where(core == 0, terms[16:], terms[:16])
        macc[:, cols] = jnp.where(core == 0, terms[:16], terms[16:])

    def enter_block(b, _):
        begin = first + b * B
        rows = rows_at(b * B, B)
        kept = flag(seg(begin + col) == seg(first - 1))
        for h in range(H):
            cols = slice(h * 128, h * 128 + 128)
            er, ei = ent_s[h, :M, :], ent_s[h, M:, :]
            y = y_loc[h, rows, :] + kept * dot(colp_s[h], weigh(h, er, ei))
            mixed_v[rows, cols] = (q_s[rows, cols].astype(F32) * y).astype(BF16)
            gq[rows, cols] = (up[rows, cols].astype(F32) * y).astype(BF16)
            ent_s[h, :M, :], ent_s[h, M:, :] = turned(h, 1, er, ei, 1.0)
        return 0

    lax.fori_loop(0, nb, enter_block, 0)
    mixed_copy = pltpu.make_async_copy(mixed_v, mixed_out, out_sem.at[0])
    mixed_copy.start()

    quarter = half // 2

    def partner_copy(k, far):
        r = rows_at(k * half + big.off(far), quarter)
        return pltpu.make_async_remote_copy(
            src_ref=dpsnd.at[r], dst_ref=dprcv.at[r], send_sem=dps_s.at[k, far], recv_sem=dps_r.at[k, far],
            device_id={"dp": 1 - core}, device_id_type=MESH,
        )

    def transposed(start):
        return jnp.concatenate([feat_t[b, rows_at(start, quarter), :] for b in range(nb)], axis=1)

    def gradient(k, other):
        for far in (1, 0):
            r = rows_at(k * half + big.off(far), quarter)
            dpsnd[r] = (dot(transposed((1 - core) * half + big.off(far)), other[...]) * norm).astype(BF16)
            partner_copy(k, far).start()
        for far in (1, 0):
            r = rows_at(k * half + big.off(far), quarter)
            pacc[r] = dot(transposed(core * half + big.off(far)), other[...]) * norm

    def join_partner(k):
        for far in (1, 0):
            r = rows_at(k * half + big.off(far), quarter)
            partner_copy(k, far).wait_recv()
            pacc[r] = pacc[r] + dprcv[r].astype(F32)

    def early(k):
        @pl.when(big.no_out & big.inner)
        def _():
            def go(i, _):
                big.up_far(k * nch + i)
                big.up_near(k * nch + i)
                return 0

            lax.fori_loop(0, nch, go, 0)

    gradient(0, gq)
    small_partner = pltpu.make_async_remote_copy(
        src_ref=mdps, dst_ref=mdpr, send_sem=md_s, recv_sem=md_r, device_id={"dp": 1 - core}, device_id_type=MESH
    )
    small_partner.start()

    def leave(i, _):
        src = n - 1 - i

        @pl.when(src > z)
        def _():
            backward_copy(src, z).wait_recv()
            kept = flag(seg(src * R) == seg(src * R + R))
            for h in range(H):
                tr, ti = turned(h, 2, lea_s[h, :M, :], lea_s[h, M:, :], kept)
                lea_s[h, :M, :] = endb_r[src, h, :M, :] + tr
                lea_s[h, M:, :] = endb_r[src, h, M:, :] + ti

        return 0

    join_partner(0)
    early(0)
    lax.fori_loop(0, n, leave, 0)
    reverse_scan([(lea_s[h, :M, :], lea_s[h, M:, :]) for h in range(H)], True)

    def ig_copy(k, b, sender):
        rows = rows_at(b * B, B)
        return pltpu.make_async_remote_copy(
            src_ref=igs.at[k - 1, rows], dst_ref=igr.at[k - 1, rows], send_sem=ig_s.at[k - 1, b],
            recv_sem=ig_r.at[k - 1, b], device_id={"tensor": lax.rem(t_me + k, nt)}, device_id_type=MESH,
        )

    def leave_block(b, _):
        begin = first + b * B
        rows = rows_at(b * B, B)
        kept = flag(seg(begin + col) == seg(begin + B))
        for h in range(H):
            cols = slice(h * 128, h * 128 + 128)
            gr, gi = g_end[b, h, :M, :], g_end[b, h, M:, :]
            gx = gx_loc[h, rows, :] + kept * dot(colh_s[h], weigh(h, gr, gi))
            gv[rows, cols] = gx.astype(BF16)
        for k in range(1, nt):
            to = lax.rem(t_me + k, nt)
            part = rows_at(to * share, share)
            igs[k - 1, rows, :] = (
                dot_nt(gq[rows, :], proj[0, part, :]) + dot_nt(gv[rows, :], proj[1, part, :])
            ).astype(BF16)
            ig_copy(k, b, t_me).start()
        return 0

    lax.fori_loop(0, nb, leave_block, 0)
    gradient(1, gv)
    small_partner.wait_recv()
    macc[...] = macc[...] + mdpr[...]
    join_partner(1)
    early(1)

    @pl.when(small.no_out & small.inner)
    def _():
        small.up_far(0)
        small.up_near(0)

    def ig_own(b, _):
        rows = rows_at(b * B, B)
        part = rows_at(t_me * share, share)
        iga[rows, :] = dot_nt(gq[rows, :], proj[0, part, :]) + dot_nt(gv[rows, :], proj[1, part, :])
        return 0

    lax.fori_loop(0, nb, ig_own, 0)

    steps = 2 * nch
    middle = big.has_out | big.root

    def sum_step(s, _):
        @pl.when(middle & (s < steps))
        def _():
            big.up_far(s)

        @pl.when(middle & (s >= 1) & (s < steps + 1))
        def _():
            big.up_near(s - 1)

        @pl.when(s >= 2)
        def _():
            big.down(s - 2, 1)
            big.down(s - 2, 0)

        return 0

    lax.fori_loop(0, steps + 2, sum_step, 0)

    @pl.when(small.has_out | small.root)
    def _():
        small.up_far(0)
        small.up_near(0)

    small.down(0, 1)
    small.down(0, 0)

    def ig_rest(b, _):
        rows = rows_at(b * B, B)
        total = iga[rows, :]
        for k in range(1, nt):
            ig_copy(k, b, t_me).wait_recv()
            total = total + igr[k - 1, rows, :].astype(F32)
        gv[rows, :share] = total.astype(BF16)
        return 0

    lax.fori_loop(0, nb, ig_rest, 0)
    ig_out_copy = pltpu.make_async_copy(gv.at[:, :share], ig_out, out_sem.at[1])
    ig_out_copy.start()

    def finish(s, _):
        big.finish(s)
        return 0

    lax.fori_loop(0, steps, finish, 0)
    pg_copy = pltpu.make_async_copy(tot, pg_out, out_sem.at[2])
    pg_copy.start()
    small.finish(0)
    res_copy = pltpu.make_async_copy(mtot.at[pl.ds(0, 2 * M)], res_out, out_sem.at[3])
    skip_copy = pltpu.make_async_copy(mtot.at[pl.ds(2 * M, 8)], skip_out, out_sem.at[4])
    res_copy.start()
    skip_copy.start()

    for b in range(nb):
        for k in range(1, nt):
            feature_copy(k, b, t_me).wait_send()
            ig_copy(k, b, t_me).wait_send()
    for k in range(2):
        for far in (1, 0):
            partner_copy(k, far).wait_send()
    small_partner.wait_send()

    def sent(to, _):
        @pl.when(to > z)
        def _():
            forward_copy(z, to).wait_send()

        @pl.when(to < z)
        def _():
            backward_copy(z, to).wait_send()

        return 0

    lax.fori_loop(0, n, sent, 0)
    mixed_copy.wait()
    ig_out_copy.wait()
    pg_copy.wait()
    res_copy.wait()
    skip_copy.wait()


def shards(frames_in, in_proj, log_rates, angles, residues, skip_gain, lengths, grad_out):
    R, C = frames_in.shape[1:]
    D = in_proj.shape[1]
    M, H = log_rates.shape
    clips = lengths.shape[1]
    n, nt = lax.axis_size("tm"), lax.axis_size("tensor")
    nb = R // B
    norm = 1.0 / math.sqrt(R * n * lax.axis_size("dp"))
    half = D // 2
    nch = half // 2 // STEP
    share = D // nt
    resid = residues.reshape(2, M, H, 128).transpose(0, 2, 1, 3)
    skip = skip_gain.reshape(H, 1, 128)
    vm, dma = pltpu.VMEM, pltpu.SemaphoreType.DMA

    def chain_sems(steps):
        return [dma((2, steps)), dma((2, steps)), dma((steps,)), dma((steps,)), dma((2, steps)), dma((2, steps)),
                dma((2, steps)), dma((2, steps))]

    scratch = [
        vm((R, D), BF16), vm((nb, D, B), BF16), vm((2, D, C), BF16), vm((R, C), BF16), vm((R, C), BF16),
        vm((H, B, 128), F32), vm((H, B, 128), F32), vm((H, B, 128), F32), vm((H, B, 128), F32),
        vm((H, B, 128), BF16), vm((H, B, 128), BF16), vm((H, B, 128), BF16),
        vm((H, R, 128), F32), vm((H, R, 128), F32), vm((R, C), BF16), vm((R, C), BF16), vm((R, C), BF16),
        vm((H, 144, 128), BF16), vm((H, 144, 128), BF16), vm((H, 128, 128), BF16), vm((H, 128, 128), BF16),
        vm((H, 128, 128), BF16), vm((H, 128, 128), BF16), vm((H, 128, 128), BF16),
        vm((H, 2, 8 * M, 128), F32), vm((H, 2, M, 128), F32), vm((H, 3, 2, M, 128), F32), vm((H, 2, M, 128), F32),
        vm((H, Q, 8, 128), F32), vm((H, M, 128), F32),
        vm((144, 128), BF16), vm((144, 128), BF16), vm((Q, 8, 128), F32), vm((8, 128), F32), vm((B, 128), F32),
        vm((B, 128), F32),
        vm((H, 2 * M, 128), F32), vm((H, 2 * M, 128), F32), vm((nb, H, 2 * M, 128), F32), vm((nb, H, 2 * M, 128), F32),
        vm((H, Q, 8, 128), F32), vm((H, 2 * M, 8, 128), F32), vm((H, 2 * M, 128), F32), vm((H, 2 * M, 128), F32),
        vm((n, H, 2 * M, 128), F32), vm((n, H, 2 * M, 128), F32),
        vm((2 * half, C), F32), vm((2 * half, C), BF16), vm((2 * half, C), BF16), vm((2 * half, C), BF16),
        vm((2 * half, C), BF16), vm((half, C), BF16), vm((2 * D, C), BF16),
        vm((16, C), F32), vm((16, C), F32), vm((16, C), F32), vm((16, C), F32), vm((16, C), F32), vm((8, C), F32),
        vm((32, C), F32),
        vm((nt - 1, R, share), BF16), vm((nt - 1, R, share), BF16), vm((R, share), F32),
        dma((3,)), dma((nt - 1, nb)), dma((nt - 1, nb)), dma((n,)), dma((n,)), dma((n,)), dma((n,)),
        dma((2, 2)), dma((2, 2)), dma((nt - 1, nb)), dma((nt - 1, nb)), dma, dma, dma((5,)),
    ] + chain_sems(2 * nch) + chain_sems(1)
    vmem = pl.BlockSpec(memory_space=pltpu.VMEM)
    anywhere = pl.BlockSpec(memory_space=pl.ANY)
    mixed, ig, pg, res, skips = pl.pallas_call(
        functools.partial(layer_kernel, (clips, M, H, R, C, D, norm)),
        out_shape=[
            jax.ShapeDtypeStruct((R, C), BF16), jax.ShapeDtypeStruct((R, share), BF16),
            jax.ShapeDtypeStruct((2 * D, C), BF16), jax.ShapeDtypeStruct((2 * M, C), F32),
            jax.ShapeDtypeStruct((8, C), F32),
        ],
        in_specs=[pl.BlockSpec(memory_space=pltpu.SMEM)] + [vmem] * 4 + [anywhere] * 3,
        out_specs=[anywhere] * 5,
        scratch_shapes=scratch,
        compiler_params=pltpu.CompilerParams(
            collective_id=0, has_side_effects=True, vmem_limit_bytes=56 << 20
        ),
        name="layer",
    )(lengths, log_rates, angles, resid, skip, frames_in[0], in_proj, grad_out[0])
    proj_grad = pg.reshape(2, D, C).astype(F32)
    return mixed[None], ig[None], proj_grad, res.reshape(2, M, C), skips[0]


def solution(mesh):
    in_specs = (
        P(("group", "dp"), "tm", "tensor"),
        P(None, None, "tensor"),
        P(None, "tensor"),
        P(None, "tensor"),
        P(None, None, "tensor"),
        P("tensor"),
        P(("group", "dp"), None),
        P(("group", "dp"), "tm", "tensor"),
    )
    out_specs = (
        P(("group", "dp"), "tm", "tensor"),
        P(("group", "dp"), "tm", "tensor"),
        P("group", None, "tensor"),
        P("group", None, "tensor"),
        P(("group", "tensor")),
    )
    return jax.shard_map(shards, mesh=mesh, in_specs=in_specs, out_specs=out_specs, check_vma=False)
```

```python
import functools
import math

import jax
import jax.numpy as jnp
from jax import lax
from jax.experimental import pallas as pl
from jax.experimental.pallas import tpu as pltpu
from jax.sharding import PartitionSpec as P

F32 = jnp.float32
BF16 = jnp.bfloat16
MESH = pl.DeviceIdType.MESH
Q = 16
B = 128
LAG = 2
GROUP = 4
STEP = 64


def dot(a, b):
    return jnp.dot(a, b, preferred_element_type=F32)


def dot_nt(a, b):
    return lax.dot_general(a, b, (((1,), (1,)), ((), ())), preferred_element_type=F32)


def flag(cond):
    return jnp.where(cond, 1.0, 0.0).astype(F32)


def rows_at(start, size, step=8):
    return pl.ds(pl.multiple_of(start, step), size)


class Chain:
    def __init__(self, acc, also, snd, upb, inb, tot, sems, nch, size, half, tot_rows, group, core):
        n, z = lax.axis_size("tm"), lax.axis_index("tm")
        left = z < n // 2
        self.inward = jnp.where(left, z + 1, z - 1)
        self.outward = jnp.clip(jnp.where(left, z - 1, z + 1), 0, n - 1)
        depth = jnp.where(left, n // 2 - 1 - z, z - n // 2)
        self.root = depth == 0
        self.inner = depth > 0
        self.has_out = depth < n // 2 - 1
        self.no_out = depth == n // 2 - 1
        self.acc, self.also, self.snd, self.upb, self.inb, self.tot = acc, also, snd, upb, inb, tot
        (self.up_s, self.up_r, self.in_r, self.to_s, self.tot_r, self.dp_s, self.dp_r) = sems
        self.nch, self.size, self.half, self.tot_rows, self.group, self.core = nch, size, half, tot_rows, group, core
        self.wire = snd.dtype

    def row(self, s):
        return rows_at(s * self.size, self.size)

    def total_row(self, s, core, count=1):
        r = (s // self.nch) * self.tot_rows + core * self.half + (s % self.nch) * self.size
        return rows_at(r, self.size * count)

    def copy(self, src, dst, send, recv, to):
        return pltpu.make_async_remote_copy(
            src_ref=src, dst_ref=dst, send_sem=send, recv_sem=recv, device_id=to, device_id_type=MESH
        )

    def up_copy(self, s):
        r = self.row(s)
        return self.copy(self.snd.at[r], self.upb.at[r], self.up_s.at[s], self.up_r.at[s], {"tm": self.inward})

    def in_copy(self, s):
        r = self.row(s)
        return self.copy(self.snd.at[r], self.inb.at[r], self.up_s.at[s], self.in_r.at[s], {"tm": self.inward})

    def out_copy(self, s):
        r = self.total_row(s, self.core)
        return self.copy(self.tot.at[r], self.tot.at[r], self.to_s.at[s], self.tot_r.at[s], {"tm": self.outward})

    def dp_copy(self, g, core):
        r = self.total_row(g * self.group, core, self.group)
        return self.copy(self.tot.at[r], self.tot.at[r], self.dp_s.at[g], self.dp_r.at[g], {"dp": 1 - self.core})

    def up(self, s):
        r = self.row(s)

        @pl.when(self.no_out)
        def _():
            self.snd[r] = (self.acc[r] + self.also[r].astype(F32)).astype(self.wire)

        @pl.when(self.has_out)
        def _():
            self.up_copy(s).wait_recv()
            self.snd[r] = (self.acc[r] + self.also[r].astype(F32) + self.upb[r].astype(F32)).astype(self.wire)

        @pl.when(self.inner)
        def _():
            self.up_copy(s).start()

        @pl.when(self.root)
        def _():
            self.in_copy(s).start()

    def down(self, s):
        @pl.when(self.root)
        def _():
            r = self.row(s)
            self.in_copy(s).wait_recv()
            self.tot[self.total_row(s, self.core)] = (self.snd[r].astype(F32) + self.inb[r].astype(F32)).astype(self.wire)

        @pl.when(self.inner)
        def _():
            self.out_copy(s).wait_recv()

        @pl.when(self.has_out)
        def _():
            self.out_copy(s).start()

        @pl.when(s % self.group == self.group - 1)
        def _():
            self.dp_copy(s // self.group, self.core).start()

    def finish(self, g):
        self.dp_copy(g, self.core).wait_send()
        self.dp_copy(g, 1 - self.core).wait_recv()
        for i in range(self.group):
            s = g * self.group + i

            @pl.when(self.has_out)
            def _():
                self.out_copy(s).wait_send()

            self.up_copy(s).wait_send()


def layer_kernel(
    cfg,
    lens_ref, rates_ref, angles_ref, resid_ref, skip_ref, frames_ref, proj_ref, up_hbm,
    mixed_out, ig_out, pg_out, res_out, skip_out,
    feat, feat_t, proj, up, q_s, x_scr, g_scr, y_scr, gx_scr, xb_s, gb_s, gm_s, y_loc, gx_loc, gq, gv, mixed_v,
    a1_s, a2_s, bt_s, b1_s, b2_s, colp_s, colh_s, pk_s, pos_s, pstep_s, w_s, k_s, wgt_s,
    ma1_s, ma2_s, keep_s, km_s, mb1_s, mb2_s,
    u_s, d_s, lead_s, g_end, r_s, rc_s, ent_s, lea_s, endf_r, endb_r,
    pacc, psnd, dpsnd, dprcv, upb, inb, tot, macc, msnd, mdps, mdpr, mupb, minb, mtot, igs, igr, iga,
    loc_sem, f_s, f_r, ef_s, ef_r, eb_s, eb_r, dps_s, dps_r, ig_s, ig_r, md_s, md_r, out_sem,
    *chain_sems,
):
    clips, M, H, R, C, D, norm = cfg
    nb = R // B
    n, z = lax.axis_size("tm"), lax.axis_index("tm")
    nt, t_me = lax.axis_size("tensor"), lax.axis_index("tensor")
    core = lax.axis_index("dp")
    first = z * R
    share = D // nt
    half = D // 2
    big_sems, small_sems = chain_sems[:7], chain_sems[7:]
    nch = half // STEP
    big = Chain(pacc, dprcv, psnd, upb, inb, tot, big_sems, nch, STEP, half, D, GROUP, core)
    small = Chain(macc, mdpr, msnd, mupb, minb, mtot, small_sems, 1, 16, 16, 32, 1, core)

    clip_starts = [jnp.int32(0)]
    for k in range(clips - 1):
        clip_starts.append(clip_starts[-1] + lens_ref[0, k])

    def seg(frame):
        total = jnp.where(frame >= clip_starts[0], 1, 0)
        for k in range(1, clips):
            total = total + jnp.where(frame >= clip_starts[k], 1, 0)
        return total

    mine = pl.ds(pl.multiple_of(t_me * C, 128), C)
    own_in = pltpu.make_async_copy(frames_ref, feat.at[:, mine], loc_sem.at[0])
    proj_in = pltpu.make_async_copy(proj_ref, proj, loc_sem.at[1])
    up_in = pltpu.make_async_copy(up_hbm, up, loc_sem.at[2])
    own_in.start()
    proj_in.start()
    up_in.start()

    barrier = pltpu.get_barrier_semaphore()
    for k in range(1, nt):
        pl.semaphore_signal(barrier, inc=1, device_id={"tensor": lax.rem(t_me + k, nt)}, device_id_type=MESH)
    pl.semaphore_signal(barrier, inc=1, device_id={"dp": 1 - core}, device_id_type=MESH)
    for k in range(1, n):
        pl.semaphore_signal(barrier, inc=1, device_id={"tm": lax.rem(z + k, n)}, device_id_type=MESH)
    pl.semaphore_wait(barrier, nt + n - 1)

    def feature_copy(k, b, sender):
        rows = rows_at(b * B, B)
        cols = pl.ds(pl.multiple_of(sender * C, 128), C)
        return pltpu.make_async_remote_copy(
            src_ref=frames_ref.at[rows], dst_ref=feat.at[rows, cols], send_sem=f_s.at[k - 1, b],
            recv_sem=f_r.at[k - 1, b], device_id={"tensor": lax.rem(t_me + k, nt)}, device_id_type=MESH,
        )

    for b in range(nb):
        for k in range(1, nt):
            feature_copy(k, b, t_me).start()

    lane = lax.broadcasted_iota(jnp.int32, (8, 128), 1)
    sub = lax.broadcasted_iota(jnp.int32, (8, 128), 0)
    lanef = lane.astype(F32)
    in_chunk = lane % Q
    chunk = lane // Q
    square = lax.broadcasted_iota(jnp.int32, (M, M), 0) == lax.broadcasted_iota(jnp.int32, (M, M), 1)

    def tables(h, _):
        d = jnp.exp(jnp.sum(jnp.where(square, rates_ref[pl.ds(h, 1), :], 0.0), axis=1, keepdims=True))
        a = jnp.sum(jnp.where(square, angles_ref[pl.ds(h, 1), :], 0.0), axis=1, keepdims=True)

        def powers(lag, dd=d, aa=a):
            size = jnp.exp(-dd * lag)
            return size * jnp.cos(aa * lag), size * jnp.sin(aa * lag)

        pos_re, pos_im = powers(lanef)
        nxt_re, nxt_im = powers(lanef + 1.0)
        neg_re, neg_im = powers(-lanef - 1.0)
        end_re, end_im = powers(127.0 - lanef)
        far_re, far_im = powers(128.0 - lanef)
        b1_re, b1_im = powers((in_chunk + 1).astype(F32))
        b2_re, b2_im = powers((Q - in_chunk).astype(F32))
        pos_s[h, 0], pos_s[h, 1] = pos_re, pos_im
        for i, lag in enumerate((1.0, float(B), float(R))):
            pr, pi = powers(jnp.full((M, 128), lag, F32))
            pstep_s[h, i, 0], pstep_s[h, i, 1] = pr, pi
        y = 2.0 * d
        series = y * (1.0 - y / 2 * (1.0 - y / 3 * (1.0 - y / 4 * (1.0 - y / 5 * (1.0 - y / 6 * (1.0 - y / 7))))))
        wgt = jnp.sqrt(jnp.where(y < 0.25, series, 1.0 - jnp.exp(-y)))
        wgt = jnp.broadcast_to(wgt, (M, 128))
        wgt_s[h] = wgt
        wr, wi = resid_ref[0, h] * wgt, resid_ref[1, h] * wgt
        w_s[h, 0], w_s[h, 1] = wr, wi
        for k in range(Q):
            tap = jnp.sum(wr * pos_re[:, k : k + 1] - wi * pos_im[:, k : k + 1], axis=0, keepdims=True)
            if k == 0:
                tap = tap + skip_ref[h]
            k_s[h, k] = jnp.broadcast_to(tap, (8, 128))
        a1r, a1i, a2r, a2i, btr, bti, b2r, b2i = [], [], [], [], [], [], [], []
        subf = sub.astype(F32) * Q
        for m in range(M):
            one = slice(m, m + 1)
            pr, pi = powers(subf, d[one], a[one])
            pk_s[h, 0, m * 8 : m * 8 + 8], pk_s[h, 1, m * 8 : m * 8 + 8] = pr, pi
            back_re, back_im = powers(-subf - float(Q), d[one], a[one])
            fr, fi = neg_re[one], neg_im[one]
            past = lane < sub * Q
            a1r.append(jnp.where(past, pr * fr - pi * fi, 0.0))
            a1i.append(jnp.where(past, pr * fi + pi * fr, 0.0))
            fr, fi = pos_re[one], pos_im[one]
            later = lane >= (sub + 1) * Q
            a2r.append(jnp.where(later, back_re * fr - back_im * fi, 0.0))
            a2i.append(jnp.where(later, back_re * fi + back_im * fr, 0.0))
            here = chunk == sub
            btr.append(jnp.where(here, b1_re[one], 0.0))
            bti.append(jnp.where(here, b1_im[one], 0.0))
            b2r.append(jnp.where(here, b2_re[one], 0.0))
            b2i.append(jnp.where(here, b2_im[one], 0.0))
        a1_s[h] = jnp.concatenate(a1r + a1i + [end_re, end_im], axis=0).astype(BF16)
        a2_s[h] = jnp.concatenate(a2r + a2i + [pos_re, pos_im], axis=0).astype(BF16)
        bt = jnp.concatenate(btr + bti, axis=0)
        bt_s[h] = bt.astype(BF16)
        b1_s[h] = bt.T.astype(BF16)
        b2_s[h] = jnp.concatenate(b2r + b2i, axis=0).T.astype(BF16)
        pad = [jnp.zeros((128 - 2 * M, 128), F32)]
        colp_s[h] = jnp.concatenate([nxt_re, nxt_im] + pad, axis=0).T.astype(BF16)
        colh_s[h] = jnp.concatenate([far_re, far_im] + pad, axis=0).T.astype(BF16)
        return 0

    lax.fori_loop(0, H, tables, 0)
    u_s[...] = jnp.zeros_like(u_s)
    r_s[...] = jnp.zeros_like(r_s)
    rc_s[...] = jnp.zeros_like(rc_s)
    own_in.wait()
    proj_in.wait()
    up_in.wait()

    def head(b, keep_block, h):
        rows = rows_at(b * B, B)
        xs = [x_scr[h, pl.ds(i, 8, stride=Q), :] for i in range(Q)]
        gs = [g_scr[h, pl.ds(i, 8, stride=Q), :] for i in range(Q)]
        held, corr = [], [None] * Q
        for i in range(Q):
            if i:
                kept = keep_s[i]
                held = [v * kept for v in held]
            held.append(xs[i])
            acc = None
            for s in range(i + 1):
                lag = i - s
                term = k_s[h, lag] * held[s]
                acc = term if acc is None else acc + term
                both = gs[i] * held[s]
                corr[lag] = both if corr[lag] is None else corr[lag] + both
            y_scr[h, pl.ds(i, 8, stride=Q), :] = acc
        for lag in range(Q):
            r_s[h, lag] += corr[lag]
        held = []
        for s in reversed(range(Q)):
            if s < Q - 1:
                kept = keep_s[s + 1]
                held = [v * kept for v in held]
            held = [gs[s]] + held
            acc = None
            for lag in range(Q - s):
                term = k_s[h, lag] * held[lag]
                acc = term if acc is None else acc + term
            gx_scr[h, pl.ds(s, 8, stride=Q), :] = acc

        states = dot(a1_s[h] * ma1_s[...], xb_s[h])
        leads = dot(bt_s[h], gm_s[h])
        adj = dot(a2_s[h] * ma2_s[...], gb_s[h])
        kept = km_s[...]
        vr, vi, ar, ai = [], [], [], []
        for m in range(M):
            re, im = slice(m * 8, m * 8 + 8), slice(64 + m * 8, 72 + m * 8)
            pr, pi = pk_s[h, 0, re] * kept, pk_s[h, 1, re] * kept
            ur, ui = u_s[h, m : m + 1, :], u_s[h, M + m : M + m + 1, :]
            sr = states[re] + (pr * ur - pi * ui)
            si = states[im] + (pr * ui + pi * ur)
            lr, li = leads[re], leads[im]
            rc_s[h, m] += sr * lr - si * li
            rc_s[h, M + m] += sr * li + si * lr
            wr, wi = w_s[h, 0, m : m + 1, :], w_s[h, 1, m : m + 1, :]
            vr.append(wr * sr - wi * si)
            vi.append(-(wr * si + wi * sr))
            ar.append(wr * adj[re] - wi * adj[im])
            ai.append(-(wr * adj[im] + wi * adj[re]))
        v = jnp.concatenate(vr + vi, axis=0).astype(BF16)
        y_loc[h, rows, :] = y_scr[h] + mb1_s[...] * dot(b1_s[h], v)
        v = jnp.concatenate(ar + ai, axis=0).astype(BF16)
        gx_loc[h, rows, :] = gx_scr[h] + mb2_s[...] * dot(b2_s[h], v)
        lead_s[b, h] = adj[128:]
        pr, pi = pstep_s[h, 1, 0] * keep_block, pstep_s[h, 1, 1] * keep_block
        ur, ui = u_s[h, :M, :], u_s[h, M:, :]
        u_s[h, :M, :] = states[128 : 128 + M] + (pr * ur - pi * ui)
        u_s[h, M:, :] = states[128 + M :] + (pr * ui + pi * ur)

    col = lax.broadcasted_iota(jnp.int32, (B, 128), 0)

    def block(b, _):
        begin = first + b * B
        rows = rows_at(b * B, B)
        seg_t = seg(begin + lane)
        same = flag(seg_t == seg(begin + sub * Q - 1))
        ma1_s[...] = jnp.concatenate([same] * 16 + [flag(seg_t == seg(begin + B - 1))] * 2, axis=0).astype(BF16)
        same = flag(seg_t == seg(begin + (sub + 1) * Q))
        ma2_s[...] = jnp.concatenate([same] * 16 + [flag(seg_t == seg(begin))] * 2, axis=0).astype(BF16)
        km_s[...] = flag(seg(begin + sub * Q - 1) == seg(begin - 1))
        for i in range(Q):
            at = begin + sub * Q + i
            keep_s[i] = flag(seg(at) == seg(at - 1))
        seg_c = seg(begin + col)
        mb1_s[...] = flag(seg_c == seg(begin + (col // Q) * Q - 1))
        mb2_s[...] = flag(seg_c == seg(begin + (col // Q + 1) * Q))
        keep_block = flag(seg(begin + B - 1) == seg(begin - 1))

        for k in range(1, nt):
            feature_copy(k, b, lax.rem(t_me - k + nt, nt)).wait_recv()
        fb = feat[rows, :]
        query = dot(fb, proj[0]).astype(BF16)
        signal = dot(fb, proj[1]).astype(BF16)
        q_s[rows, :] = query
        g = query.astype(F32) * up[rows, :].astype(F32)
        signal32 = signal.astype(F32)
        for h in range(H):
            cols = slice(h * 128, h * 128 + 128)
            x_scr[h] = signal32[:, cols]
            g_scr[h] = g[:, cols]
            xb_s[h] = signal[:, cols]
            gb_s[h] = g[:, cols].astype(BF16)
            gm_s[h] = (g[:, cols] * mb1_s[...]).astype(BF16)
        feat_t[b] = fb.T

        for h in range(H):
            head(b, keep_block, h)
        return 0

    lax.fori_loop(0, nb, block, 0)

    def turned(h, which, re, im, kept):
        pr, pi = pstep_s[h, which, 0] * kept, pstep_s[h, which, 1] * kept
        return pr * re - pi * im, pr * im + pi * re

    def reverse_scan(start, store):
        state = start
        for b in reversed(range(nb)):
            begin = first + b * B
            kept = flag(seg(begin) == seg(begin + B))
            following = []
            for h in range(H):
                re, im = state[h]
                if store:
                    g_end[b, h, :M, :], g_end[b, h, M:, :] = re, im
                tr, ti = turned(h, 1, re, im, kept)
                following.append((lead_s[b, h, :M, :] + tr, lead_s[b, h, M:, :] + ti))
            state = following
        return state

    zero = jnp.zeros((M, 128), F32)
    ends = reverse_scan([(zero, zero)] * H, False)
    for h in range(H):
        d_s[h, :M, :], d_s[h, M:, :] = ends[h]

    def end_copy(src, dst, send, recv, slot, to):
        return pltpu.make_async_remote_copy(
            src_ref=src, dst_ref=dst.at[slot], send_sem=send.at[to], recv_sem=recv.at[slot],
            device_id={"tm": to}, device_id_type=MESH,
        )

    def forward_copy(slot, to):
        return end_copy(u_s, endf_r, ef_s, ef_r, slot, to)

    def backward_copy(slot, to):
        return end_copy(d_s, endb_r, eb_s, eb_r, slot, to)

    def send_ends(to, _):
        @pl.when(to > z)
        def _():
            forward_copy(z, to).start()

        @pl.when(to < z)
        def _():
            backward_copy(z, to).start()

        return 0

    lax.fori_loop(0, n, send_ends, 0)
    ent_s[...] = jnp.zeros_like(ent_s)
    lea_s[...] = jnp.zeros_like(lea_s)

    def enter(src, _):
        @pl.when(src < z)
        def _():
            forward_copy(src, z).wait_recv()
            kept = flag(seg(src * R - 1) == seg(src * R + R - 1))
            for h in range(H):
                tr, ti = turned(h, 2, ent_s[h, :M, :], ent_s[h, M:, :], kept)
                ent_s[h, :M, :] = endf_r[src, h, :M, :] + tr
                ent_s[h, M:, :] = endf_r[src, h, M:, :] + ti

        return 0

    lax.fori_loop(0, n, enter, 0)

    def weigh(h, re, im):
        wr, wi = w_s[h, 0], w_s[h, 1]
        pad = [jnp.zeros((128 - 2 * M, 128), F32)]
        return jnp.concatenate([wr * re - wi * im, -(wr * im + wi * re)] + pad, axis=0).astype(BF16)

    kept_first = flag(seg(first) == seg(first - 1))
    for h in range(H):
        lr, li = turned(h, 0, d_s[h, :M, :], d_s[h, M:, :], kept_first)
        er, ei = ent_s[h, :M, :], ent_s[h, M:, :]
        re, im = [], []
        for m in range(M):
            re.append(jnp.sum(rc_s[h, m], axis=0, keepdims=True))
            im.append(jnp.sum(rc_s[h, M + m], axis=0, keepdims=True))
        re = jnp.concatenate(re, axis=0) + er * lr - ei * li
        im = jnp.concatenate(im, axis=0) + er * li + ei * lr
        for lag in range(Q):
            r = jnp.sum(r_s[h, lag], axis=0, keepdims=True)
            if lag == 0:
                skip_row = r
            re = re + pos_s[h, 0, :, lag : lag + 1] * r
            im = im + pos_s[h, 1, :, lag : lag + 1] * r
        cols = slice(h * 128, h * 128 + 128)
        scale = wgt_s[h] * norm
        terms = jnp.concatenate([re * scale, -im * scale, skip_row * norm, jnp.zeros((15, 128), F32)], axis=0)
        own = rows_at(core * 16, 16)
        mdps[:, cols] = jnp.where(core == 0, terms[16:], terms[:16])
        macc[:, cols] = jnp.where(core == 0, terms[:16], terms[16:])

    def enter_block(b, _):
        begin = first + b * B
        rows = rows_at(b * B, B)
        kept = flag(seg(begin + col) == seg(first - 1))
        for h in range(H):
            cols = slice(h * 128, h * 128 + 128)
            er, ei = ent_s[h, :M, :], ent_s[h, M:, :]
            y = y_loc[h, rows, :] + kept * dot(colp_s[h], weigh(h, er, ei))
            mixed_v[rows, cols] = (q_s[rows, cols].astype(F32) * y).astype(BF16)
            gq[rows, cols] = (up[rows, cols].astype(F32) * y).astype(BF16)
            ent_s[h, :M, :], ent_s[h, M:, :] = turned(h, 1, er, ei, 1.0)
        return 0

    lax.fori_loop(0, nb, enter_block, 0)
    mixed_copy = pltpu.make_async_copy(mixed_v, mixed_out, out_sem.at[0])
    mixed_copy.start()

    quarter = half // 2

    def partner_copy(k, i):
        r = rows_at(k * half + i * quarter, quarter)
        return pltpu.make_async_remote_copy(
            src_ref=dpsnd.at[r], dst_ref=dprcv.at[r], send_sem=dps_s.at[k, i], recv_sem=dps_r.at[k, i],
            device_id={"dp": 1 - core}, device_id_type=MESH,
        )

    def transposed(start):
        return jnp.concatenate([feat_t[b, rows_at(start, quarter), :] for b in range(nb)], axis=1)

    def gradient(k, other):
        for i in range(2):
            r = rows_at(k * half + i * quarter, quarter)
            dpsnd[r] = (dot(transposed((1 - core) * half + i * quarter), other[...]) * norm).astype(BF16)
            partner_copy(k, i).start()
        for i in range(2):
            r = rows_at(k * half + i * quarter, quarter)
            pacc[r] = dot(transposed(core * half + i * quarter), other[...]) * norm
            partner_copy(k, i).wait_recv()

            @pl.when(big.no_out)
            def _():
                def go(j, _):
                    big.up(k * nch + i * (nch // 2) + j)
                    return 0

                lax.fori_loop(0, nch // 2, go, 0)

    gradient(0, gq)
    small_partner = pltpu.make_async_remote_copy(
        src_ref=mdps, dst_ref=mdpr, send_sem=md_s, recv_sem=md_r, device_id={"dp": 1 - core}, device_id_type=MESH
    )
    small_partner.start()

    def leave(i, _):
        src = n - 1 - i

        @pl.when(src > z)
        def _():
            backward_copy(src, z).wait_recv()
            kept = flag(seg(src * R) == seg(src * R + R))
            for h in range(H):
                tr, ti = turned(h, 2, lea_s[h, :M, :], lea_s[h, M:, :], kept)
                lea_s[h, :M, :] = endb_r[src, h, :M, :] + tr
                lea_s[h, M:, :] = endb_r[src, h, M:, :] + ti

        return 0

    lax.fori_loop(0, n, leave, 0)
    reverse_scan([(lea_s[h, :M, :], lea_s[h, M:, :]) for h in range(H)], True)

    def ig_copy(k, b, sender):
        rows = rows_at(b * B, B)
        return pltpu.make_async_remote_copy(
            src_ref=igs.at[k - 1, rows], dst_ref=igr.at[k - 1, rows], send_sem=ig_s.at[k - 1, b],
            recv_sem=ig_r.at[k - 1, b], device_id={"tensor": lax.rem(t_me + k, nt)}, device_id_type=MESH,
        )

    def leave_block(b, _):
        begin = first + b * B
        rows = rows_at(b * B, B)
        kept = flag(seg(begin + col) == seg(begin + B))
        for h in range(H):
            cols = slice(h * 128, h * 128 + 128)
            gr, gi = g_end[b, h, :M, :], g_end[b, h, M:, :]
            gx = gx_loc[h, rows, :] + kept * dot(colh_s[h], weigh(h, gr, gi))
            gv[rows, cols] = gx.astype(BF16)
        for k in range(1, nt):
            to = lax.rem(t_me + k, nt)
            part = rows_at(to * share, share)
            igs[k - 1, rows, :] = (
                dot_nt(gq[rows, :], proj[0, part, :]) + dot_nt(gv[rows, :], proj[1, part, :])
            ).astype(BF16)
            ig_copy(k, b, t_me).start()
        return 0

    def ig_own(b, _):
        rows = rows_at(b * B, B)
        part = rows_at(t_me * share, share)
        iga[rows, :] = dot_nt(gq[rows, :], proj[0, part, :]) + dot_nt(gv[rows, :], proj[1, part, :])
        return 0

    steps = 2 * nch
    def sum_step(s, _):
        @pl.when(big.has_out & (s < steps))
        def _():
            big.up(s)

        @pl.when(s >= LAG)
        def _():
            big.down(s - LAG)

        return 0

    def mixture(b, _):
        leave_block(b, 0)
        sum_step(b, 0)
        return 0

    def ig_rest(b, _):
        rows = rows_at(b * B, B)
        total = iga[rows, :]
        for k in range(1, nt):
            ig_copy(k, b, t_me).wait_recv()
            total = total + igr[k - 1, rows, :].astype(F32)
        gv[rows, :share] = total.astype(BF16)
        return 0

    def finish(s, _):
        big.finish(s)
        return 0

    def pg_copy(k):
        r = pl.ds(k * D, D)
        return pltpu.make_async_copy(tot.at[r], pg_out.at[r], out_sem.at[2 + k])

    lax.fori_loop(0, nb, mixture, 0)
    gradient(1, gv)
    small_partner.wait_recv()
    pl.when(small.no_out)(lambda: small.up(0))
    lax.fori_loop(nb, nch, sum_step, 0)
    lax.fori_loop(0, nb, ig_own, 0)
    lax.fori_loop(nch, steps - 2, sum_step, 0)
    lax.fori_loop(0, nch // GROUP, finish, 0)
    pg_copy(0).start()
    pl.when(small.has_out)(lambda: small.up(0))
    lax.fori_loop(steps - 2, steps, sum_step, 0)
    small.down(0)
    lax.fori_loop(0, nb, ig_rest, 0)
    ig_out_copy = pltpu.make_async_copy(gv.at[:, :share], ig_out, out_sem.at[1])
    ig_out_copy.start()
    lax.fori_loop(steps, steps + LAG, sum_step, 0)
    small.finish(0)
    res_copy = pltpu.make_async_copy(mtot.at[pl.ds(0, 2 * M)], res_out, out_sem.at[4])
    skip_copy = pltpu.make_async_copy(mtot.at[pl.ds(2 * M, 8)], skip_out, out_sem.at[5])
    res_copy.start()
    skip_copy.start()
    lax.fori_loop(nch // GROUP, steps // GROUP, finish, 0)
    pg_copy(1).start()

    for b in range(nb):
        for k in range(1, nt):
            feature_copy(k, b, t_me).wait_send()
            ig_copy(k, b, t_me).wait_send()
    for k in range(2):
        for i in range(2):
            partner_copy(k, i).wait_send()
    small_partner.wait_send()

    def sent(to, _):
        @pl.when(to > z)
        def _():
            forward_copy(z, to).wait_send()

        @pl.when(to < z)
        def _():
            backward_copy(z, to).wait_send()

        return 0

    lax.fori_loop(0, n, sent, 0)
    mixed_copy.wait()
    ig_out_copy.wait()
    pg_copy(0).wait()
    pg_copy(1).wait()
    res_copy.wait()
    skip_copy.wait()


def assemble_kernel(mixed, ig, pg, res, skips, mixed_o, ig_o, pg_o, res_o, skip_o, narrow, wide, b0, b1, b2, b3, in_s, out_s):
    parts = narrow.shape[0]
    rows = narrow.shape[1]
    through = ((mixed, b0, mixed_o), (ig, b1, ig_o), (res, b2, res_o), (skips, b3, skip_o))
    loads = [pltpu.make_async_copy(pg.at[pl.ds(i * rows, rows)], narrow.at[i], in_s.at[i]) for i in range(parts)]
    stores = [pltpu.make_async_copy(wide.at[i], pg_o.at[pl.ds(i * rows, rows)], out_s.at[i]) for i in range(parts)]
    for i, (src, buf, dst) in enumerate(through):
        loads.append(pltpu.make_async_copy(src, buf, in_s.at[parts + i]))
        kept = buf if buf.shape == dst.shape else buf.at[pl.ds(0, dst.shape[0])]
        stores.append(pltpu.make_async_copy(kept, dst, out_s.at[parts + i]))
    for copy in loads:
        copy.start()
    for i in range(len(loads)):
        loads[i].wait()
        if i < parts:
            wide[i] = narrow[i].astype(F32)
        stores[i].start()
    for copy in stores:
        copy.wait()


def shards(frames_in, in_proj, log_rates, angles, residues, skip_gain, lengths, grad_out):
    R, C = frames_in.shape[1:]
    D = in_proj.shape[1]
    M, H = log_rates.shape
    clips = lengths.shape[1]
    n, nt = lax.axis_size("tm"), lax.axis_size("tensor")
    nb = R // B
    norm = 1.0 / math.sqrt(R * n * lax.axis_size("dp"))
    half = D // 2
    nch = half // STEP
    share = D // nt
    resid = residues.reshape(2, M, H, 128).transpose(0, 2, 1, 3)
    skip = skip_gain.reshape(H, 1, 128)
    vm, dma = pltpu.VMEM, pltpu.SemaphoreType.DMA

    def chain_sems(steps, group):
        return [dma((steps,))] * 5 + [dma((steps // group,))] * 2

    scratch = [
        vm((R, D), BF16), vm((nb, D, B), BF16), vm((2, D, C), BF16), vm((R, C), BF16), vm((R, C), BF16),
        vm((H, B, 128), F32), vm((H, B, 128), F32), vm((H, B, 128), F32), vm((H, B, 128), F32),
        vm((H, B, 128), BF16), vm((H, B, 128), BF16), vm((H, B, 128), BF16),
        vm((H, R, 128), F32), vm((H, R, 128), F32), vm((R, C), BF16), vm((R, C), BF16), vm((R, C), BF16),
        vm((H, 144, 128), BF16), vm((H, 144, 128), BF16), vm((H, 128, 128), BF16), vm((H, 128, 128), BF16),
        vm((H, 128, 128), BF16), vm((H, 128, 128), BF16), vm((H, 128, 128), BF16),
        vm((H, 2, 8 * M, 128), F32), vm((H, 2, M, 128), F32), vm((H, 3, 2, M, 128), F32), vm((H, 2, M, 128), F32),
        vm((H, Q, 8, 128), F32), vm((H, M, 128), F32),
        vm((144, 128), BF16), vm((144, 128), BF16), vm((Q, 8, 128), F32), vm((8, 128), F32), vm((B, 128), F32),
        vm((B, 128), F32),
        vm((H, 2 * M, 128), F32), vm((H, 2 * M, 128), F32), vm((nb, H, 2 * M, 128), F32), vm((nb, H, 2 * M, 128), F32),
        vm((H, Q, 8, 128), F32), vm((H, 2 * M, 8, 128), F32), vm((H, 2 * M, 128), F32), vm((H, 2 * M, 128), F32),
        vm((n, H, 2 * M, 128), F32), vm((n, H, 2 * M, 128), F32),
        vm((2 * half, C), F32), vm((2 * half, C), BF16), vm((2 * half, C), BF16), vm((2 * half, C), BF16),
        vm((2 * half, C), BF16), vm((2 * half, C), BF16), vm((2 * D, C), BF16),
        vm((16, C), F32), vm((16, C), F32), vm((16, C), F32), vm((16, C), F32), vm((16, C), F32), vm((16, C), F32),
        vm((32, C), F32),
        vm((nt - 1, R, share), BF16), vm((nt - 1, R, share), BF16), vm((R, share), F32),
        dma((3,)), dma((nt - 1, nb)), dma((nt - 1, nb)), dma((n,)), dma((n,)), dma((n,)), dma((n,)),
        dma((2, 2)), dma((2, 2)), dma((nt - 1, nb)), dma((nt - 1, nb)), dma, dma, dma((6,)),
    ] + chain_sems(2 * nch, GROUP) + chain_sems(1, 1)
    vmem = pl.BlockSpec(memory_space=pltpu.VMEM)
    anywhere = pl.BlockSpec(memory_space=pl.ANY)
    mixed, ig, pg, res, skips = pl.pallas_call(
        functools.partial(layer_kernel, (clips, M, H, R, C, D, norm)),
        out_shape=[
            jax.ShapeDtypeStruct((R, C), BF16), jax.ShapeDtypeStruct((R, share), BF16),
            jax.ShapeDtypeStruct((2 * D, C), BF16), jax.ShapeDtypeStruct((2 * M, C), F32),
            jax.ShapeDtypeStruct((8, C), F32),
        ],
        in_specs=[pl.BlockSpec(memory_space=pltpu.SMEM)] + [vmem] * 4 + [anywhere] * 3,
        out_specs=[anywhere] * 5,
        scratch_shapes=scratch,
        compiler_params=pltpu.CompilerParams(
            collective_id=0, has_side_effects=True, vmem_limit_bytes=56 << 20
        ),
        name="layer",
    )(lengths, log_rates.T, angles.T, resid, skip, frames_in[0], in_proj, grad_out[0])
    parts = 8
    mixed, ig, pg, res, skips = pl.pallas_call(
        assemble_kernel,
        out_shape=[
            jax.ShapeDtypeStruct((R, C), BF16), jax.ShapeDtypeStruct((R, share), BF16),
            jax.ShapeDtypeStruct((2 * D, C), F32), jax.ShapeDtypeStruct((2 * M, C), F32),
            jax.ShapeDtypeStruct((1, C), F32),
        ],
        in_specs=[anywhere] * 5,
        out_specs=[anywhere] * 5,
        scratch_shapes=[
            vm((parts, 2 * D // parts, C), BF16), vm((parts, 2 * D // parts, C), F32), vm((R, C), BF16),
            vm((R, share), BF16), vm((2 * M, C), F32), vm((8, C), F32), dma((parts + 4,)), dma((parts + 4,)),
        ],
        compiler_params=pltpu.CompilerParams(vmem_limit_bytes=60 << 20),
        name="assemble",
    )(mixed, ig, pg, res, skips)
    return mixed[None], ig[None], pg.reshape(2, D, C), res.reshape(2, M, C), skips[0]


def solution(mesh):
    in_specs = (
        P(("group", "dp"), "tm", "tensor"),
        P(None, None, "tensor"),
        P(None, "tensor"),
        P(None, "tensor"),
        P(None, None, "tensor"),
        P("tensor"),
        P(("group", "dp"), None),
        P(("group", "dp"), "tm", "tensor"),
    )
    out_specs = (
        P(("group", "dp"), "tm", "tensor"),
        P(("group", "dp"), "tm", "tensor"),
        P("group", None, "tensor"),
        P("group", None, "tensor"),
        P(("group", "tensor")),
    )
    return jax.shard_map(shards, mesh=mesh, in_specs=in_specs, out_specs=out_specs, check_vma=False)
```

```python
import functools
import math

import jax
import jax.numpy as jnp
from jax import lax
from jax.experimental import pallas as pl
from jax.experimental.pallas import tpu as pltpu
from jax.sharding import PartitionSpec as P

F32 = jnp.float32
BF16 = jnp.bfloat16
AXES = ("group", "tm", "tensor", "dp")
MESH = pl.DeviceIdType.MESH
Q = 16
B = 128
LAG = 2
GROUP = 4
STEP = 64


def dot(a, b):
    return jnp.dot(a, b, preferred_element_type=F32)


def dot_nt(a, b):
    return lax.dot_general(a, b, (((1,), (1,)), ((), ())), preferred_element_type=F32)


def flag(cond):
    return jnp.where(cond, 1.0, 0.0).astype(F32)


def rows_at(start, size, step=8):
    return pl.ds(pl.multiple_of(start, step), size)


class Place:
    def __init__(self):
        self.at = {axis: lax.axis_index(axis) for axis in AXES}

    def __call__(self, **moved):
        return tuple(moved.get(axis, self.at[axis]) for axis in AXES)


class Chain:
    def __init__(self, place, acc, also, snd, upb, inb, tot, sems, nch, size, half, tot_rows, group, core):
        n, z = lax.axis_size("tm"), place.at["tm"]
        left = z < n // 2
        self.inward = place(tm=jnp.where(left, z + 1, z - 1))
        self.outward = place(tm=jnp.clip(jnp.where(left, z - 1, z + 1), 0, n - 1))
        self.partner = place(dp=1 - core)
        depth = jnp.where(left, n // 2 - 1 - z, z - n // 2)
        self.root = depth == 0
        self.inner = depth > 0
        self.has_out = depth < n // 2 - 1
        self.no_out = depth == n // 2 - 1
        self.acc, self.also, self.snd, self.upb, self.inb, self.tot = acc, also, snd, upb, inb, tot
        (self.up_s, self.up_r, self.in_r, self.to_s, self.tot_r, self.dp_s, self.dp_r) = sems
        self.nch, self.size, self.half, self.tot_rows, self.group, self.core = nch, size, half, tot_rows, group, core
        self.wire = snd.dtype

    def row(self, s):
        return rows_at(s * self.size, self.size)

    def total_row(self, s, core, count=1):
        r = (s // self.nch) * self.tot_rows + core * self.half + (s % self.nch) * self.size
        return rows_at(r, self.size * count)

    def copy(self, src, dst, send, recv, to):
        return pltpu.make_async_remote_copy(
            src_ref=src, dst_ref=dst, send_sem=send, recv_sem=recv, device_id=to, device_id_type=MESH
        )

    def up_copy(self, s):
        r = self.row(s)
        return self.copy(self.snd.at[r], self.upb.at[r], self.up_s.at[s], self.up_r.at[s], self.inward)

    def in_copy(self, s):
        r = self.row(s)
        return self.copy(self.snd.at[r], self.inb.at[r], self.up_s.at[s], self.in_r.at[s], self.inward)

    def out_copy(self, s):
        r = self.total_row(s, self.core)
        return self.copy(self.tot.at[r], self.tot.at[r], self.to_s.at[s], self.tot_r.at[s], self.outward)

    def dp_copy(self, g, core):
        r = self.total_row(g * self.group, core, self.group)
        return self.copy(self.tot.at[r], self.tot.at[r], self.dp_s.at[g], self.dp_r.at[g], self.partner)

    def up(self, s):
        r = self.row(s)

        @pl.when(self.no_out)
        def _():
            self.snd[r] = (self.acc[r] + self.also[r].astype(F32)).astype(self.wire)

        @pl.when(self.has_out)
        def _():
            self.up_copy(s).wait_recv()
            self.snd[r] = (self.acc[r] + self.also[r].astype(F32) + self.upb[r].astype(F32)).astype(self.wire)

        @pl.when(self.inner)
        def _():
            self.up_copy(s).start()

        @pl.when(self.root)
        def _():
            self.in_copy(s).start()

    def down(self, s):
        @pl.when(self.root)
        def _():
            r = self.row(s)
            self.in_copy(s).wait_recv()
            self.tot[self.total_row(s, self.core)] = (self.snd[r].astype(F32) + self.inb[r].astype(F32)).astype(self.wire)

        @pl.when(self.inner)
        def _():
            self.out_copy(s).wait_recv()

        @pl.when(self.has_out)
        def _():
            self.out_copy(s).start()

        @pl.when(s % self.group == self.group - 1)
        def _():
            self.dp_copy(s // self.group, self.core).start()

    def finish(self, g):
        self.dp_copy(g, self.core).wait_send()
        self.dp_copy(g, 1 - self.core).wait_recv()
        for i in range(self.group):
            s = g * self.group + i

            @pl.when(self.has_out)
            def _():
                self.out_copy(s).wait_send()

            self.up_copy(s).wait_send()


def layer_kernel(
    cfg,
    lens_ref, rates_ref, angles_ref, resid_ref, skip_ref, frames_ref, proj_ref, up_hbm,
    mixed_out, ig_out, pg_out, res_out, skip_out,
    feat, feat_t, proj, up, q_s, x_scr, g_scr, y_scr, gx_scr, xb_s, gb_s, gm_s, y_loc, gx_loc, gq, gv, mixed_v,
    a1_s, a2_s, bt_s, b1_s, b2_s, colp_s, colh_s, pk_s, pos_s, pstep_s, w_s, k_s, wgt_s,
    ma1_s, ma2_s, keep_s, km_s, mb1_s, mb2_s,
    u_s, d_s, lead_s, g_end, r_s, rc_s, ent_s, lea_s, endf_r, endb_r,
    pacc, psnd, dpsnd, dprcv, upb, inb, tot, macc, msnd, mdps, mdpr, mupb, minb, mtot, igs, igr, iga,
    loc_sem, f_s, f_r, ef_s, ef_r, eb_s, eb_r, dps_s, dps_r, ig_s, ig_r, md_s, md_r, out_sem,
    *chain_sems,
):
    clips, M, H, R, C, D, norm = cfg
    nb = R // B
    place = Place()
    n, z = lax.axis_size("tm"), place.at["tm"]
    nt, t_me = lax.axis_size("tensor"), place.at["tensor"]
    core = place.at["dp"]
    first = z * R
    share = D // nt
    half = D // 2
    big_sems, small_sems = chain_sems[:7], chain_sems[7:]
    nch = half // STEP
    big = Chain(place, pacc, dprcv, psnd, upb, inb, tot, big_sems, nch, STEP, half, D, GROUP, core)
    small = Chain(place, macc, mdpr, msnd, mupb, minb, mtot, small_sems, 1, 16, 16, 32, 1, core)

    clip_starts = [jnp.int32(0)]
    for k in range(clips - 1):
        clip_starts.append(clip_starts[-1] + lens_ref[0, k])

    def seg(frame):
        total = jnp.where(frame >= clip_starts[0], 1, 0)
        for k in range(1, clips):
            total = total + jnp.where(frame >= clip_starts[k], 1, 0)
        return total

    mine = pl.ds(pl.multiple_of(t_me * C, 128), C)
    own_in = pltpu.make_async_copy(frames_ref, feat.at[:, mine], loc_sem.at[0])
    proj_in = pltpu.make_async_copy(proj_ref, proj, loc_sem.at[1])
    up_in = pltpu.make_async_copy(up_hbm, up, loc_sem.at[2])
    own_in.start()
    proj_in.start()
    up_in.start()

    barrier = pltpu.get_barrier_semaphore()
    for k in range(1, nt):
        pl.semaphore_signal(barrier, inc=1, device_id=place(tensor=lax.rem(t_me + k, nt)), device_id_type=MESH)
    pl.semaphore_signal(barrier, inc=1, device_id=place(dp=1 - core), device_id_type=MESH)
    for k in range(1, n):
        pl.semaphore_signal(barrier, inc=1, device_id=place(tm=lax.rem(z + k, n)), device_id_type=MESH)
    pl.semaphore_wait(barrier, nt + n - 1)

    def feature_copy(k, b, sender):
        rows = rows_at(b * B, B)
        cols = pl.ds(pl.multiple_of(sender * C, 128), C)
        return pltpu.make_async_remote_copy(
            src_ref=frames_ref.at[rows], dst_ref=feat.at[rows, cols], send_sem=f_s.at[k - 1, b],
            recv_sem=f_r.at[k - 1, b], device_id=place(tensor=lax.rem(t_me + k, nt)), device_id_type=MESH,
        )

    for b in range(nb):
        for k in range(1, nt):
            feature_copy(k, b, t_me).start()

    lane = lax.broadcasted_iota(jnp.int32, (8, 128), 1)
    sub = lax.broadcasted_iota(jnp.int32, (8, 128), 0)
    lanef = lane.astype(F32)
    in_chunk = lane % Q
    chunk = lane // Q
    square = lax.broadcasted_iota(jnp.int32, (M, M), 0) == lax.broadcasted_iota(jnp.int32, (M, M), 1)

    def tables(h, _):
        d = jnp.exp(jnp.sum(jnp.where(square, rates_ref[pl.ds(h, 1), :], 0.0), axis=1, keepdims=True))
        a = jnp.sum(jnp.where(square, angles_ref[pl.ds(h, 1), :], 0.0), axis=1, keepdims=True)

        def powers(lag, dd=d, aa=a):
            size = jnp.exp(-dd * lag)
            return size * jnp.cos(aa * lag), size * jnp.sin(aa * lag)

        pos_re, pos_im = powers(lanef)
        nxt_re, nxt_im = powers(lanef + 1.0)
        neg_re, neg_im = powers(-lanef - 1.0)
        end_re, end_im = powers(127.0 - lanef)
        far_re, far_im = powers(128.0 - lanef)
        b1_re, b1_im = powers((in_chunk + 1).astype(F32))
        b2_re, b2_im = powers((Q - in_chunk).astype(F32))
        pos_s[h, 0], pos_s[h, 1] = pos_re, pos_im
        for i, lag in enumerate((1.0, float(B), float(R))):
            pr, pi = powers(jnp.full((M, 128), lag, F32))
            pstep_s[h, i, 0], pstep_s[h, i, 1] = pr, pi
        y = 2.0 * d
        series = y * (1.0 - y / 2 * (1.0 - y / 3 * (1.0 - y / 4 * (1.0 - y / 5 * (1.0 - y / 6 * (1.0 - y / 7))))))
        wgt = jnp.sqrt(jnp.where(y < 0.25, series, 1.0 - jnp.exp(-y)))
        wgt = jnp.broadcast_to(wgt, (M, 128))
        wgt_s[h] = wgt
        wr, wi = resid_ref[0, h] * wgt, resid_ref[1, h] * wgt
        w_s[h, 0], w_s[h, 1] = wr, wi
        for k in range(Q):
            tap = jnp.sum(wr * pos_re[:, k : k + 1] - wi * pos_im[:, k : k + 1], axis=0, keepdims=True)
            if k == 0:
                tap = tap + skip_ref[h]
            k_s[h, k] = jnp.broadcast_to(tap, (8, 128))
        a1r, a1i, a2r, a2i, btr, bti, b2r, b2i = [], [], [], [], [], [], [], []
        subf = sub.astype(F32) * Q
        for m in range(M):
            one = slice(m, m + 1)
            pr, pi = powers(subf, d[one], a[one])
            pk_s[h, 0, m * 8 : m * 8 + 8], pk_s[h, 1, m * 8 : m * 8 + 8] = pr, pi
            back_re, back_im = powers(-subf - float(Q), d[one], a[one])
            fr, fi = neg_re[one], neg_im[one]
            past = lane < sub * Q
            a1r.append(jnp.where(past, pr * fr - pi * fi, 0.0))
            a1i.append(jnp.where(past, pr * fi + pi * fr, 0.0))
            fr, fi = pos_re[one], pos_im[one]
            later = lane >= (sub + 1) * Q
            a2r.append(jnp.where(later, back_re * fr - back_im * fi, 0.0))
            a2i.append(jnp.where(later, back_re * fi + back_im * fr, 0.0))
            here = chunk == sub
            btr.append(jnp.where(here, b1_re[one], 0.0))
            bti.append(jnp.where(here, b1_im[one], 0.0))
            b2r.append(jnp.where(here, b2_re[one], 0.0))
            b2i.append(jnp.where(here, b2_im[one], 0.0))
        a1_s[h] = jnp.concatenate(a1r + a1i + [end_re, end_im], axis=0).astype(BF16)
        a2_s[h] = jnp.concatenate(a2r + a2i + [pos_re, pos_im], axis=0).astype(BF16)
        bt = jnp.concatenate(btr + bti, axis=0)
        bt_s[h] = bt.astype(BF16)
        b1_s[h] = bt.T.astype(BF16)
        b2_s[h] = jnp.concatenate(b2r + b2i, axis=0).T.astype(BF16)
        pad = [jnp.zeros((128 - 2 * M, 128), F32)]
        colp_s[h] = jnp.concatenate([nxt_re, nxt_im] + pad, axis=0).T.astype(BF16)
        colh_s[h] = jnp.concatenate([far_re, far_im] + pad, axis=0).T.astype(BF16)
        return 0

    lax.fori_loop(0, H, tables, 0)
    u_s[...] = jnp.zeros_like(u_s)
    r_s[...] = jnp.zeros_like(r_s)
    rc_s[...] = jnp.zeros_like(rc_s)
    own_in.wait()
    proj_in.wait()
    up_in.wait()

    def head(b, keep_block, h):
        rows = rows_at(b * B, B)
        xs = [x_scr[h, pl.ds(i, 8, stride=Q), :] for i in range(Q)]
        gs = [g_scr[h, pl.ds(i, 8, stride=Q), :] for i in range(Q)]
        held, corr = [], [None] * Q
        for i in range(Q):
            if i:
                kept = keep_s[i]
                held = [v * kept for v in held]
            held.append(xs[i])
            acc = None
            for s in range(i + 1):
                lag = i - s
                term = k_s[h, lag] * held[s]
                acc = term if acc is None else acc + term
                both = gs[i] * held[s]
                corr[lag] = both if corr[lag] is None else corr[lag] + both
            y_scr[h, pl.ds(i, 8, stride=Q), :] = acc
        for lag in range(Q):
            r_s[h, lag] += corr[lag]
        held = []
        for s in reversed(range(Q)):
            if s < Q - 1:
                kept = keep_s[s + 1]
                held = [v * kept for v in held]
            held = [gs[s]] + held
            acc = None
            for lag in range(Q - s):
                term = k_s[h, lag] * held[lag]
                acc = term if acc is None else acc + term
            gx_scr[h, pl.ds(s, 8, stride=Q), :] = acc

        states = dot(a1_s[h] * ma1_s[...], xb_s[h])
        leads = dot(bt_s[h], gm_s[h])
        adj = dot(a2_s[h] * ma2_s[...], gb_s[h])
        kept = km_s[...]
        vr, vi, ar, ai = [], [], [], []
        for m in range(M):
            re, im = slice(m * 8, m * 8 + 8), slice(64 + m * 8, 72 + m * 8)
            pr, pi = pk_s[h, 0, re] * kept, pk_s[h, 1, re] * kept
            ur, ui = u_s[h, m : m + 1, :], u_s[h, M + m : M + m + 1, :]
            sr = states[re] + (pr * ur - pi * ui)
            si = states[im] + (pr * ui + pi * ur)
            lr, li = leads[re], leads[im]
            rc_s[h, m] += sr * lr - si * li
            rc_s[h, M + m] += sr * li + si * lr
            wr, wi = w_s[h, 0, m : m + 1, :], w_s[h, 1, m : m + 1, :]
            vr.append(wr * sr - wi * si)
            vi.append(-(wr * si + wi * sr))
            ar.append(wr * adj[re] - wi * adj[im])
            ai.append(-(wr * adj[im] + wi * adj[re]))
        v = jnp.concatenate(vr + vi, axis=0).astype(BF16)
        y_loc[h, rows, :] = y_scr[h] + mb1_s[...] * dot(b1_s[h], v)
        v = jnp.concatenate(ar + ai, axis=0).astype(BF16)
        gx_loc[h, rows, :] = gx_scr[h] + mb2_s[...] * dot(b2_s[h], v)
        lead_s[b, h] = adj[128:]
        pr, pi = pstep_s[h, 1, 0] * keep_block, pstep_s[h, 1, 1] * keep_block
        ur, ui = u_s[h, :M, :], u_s[h, M:, :]
        u_s[h, :M, :] = states[128 : 128 + M] + (pr * ur - pi * ui)
        u_s[h, M:, :] = states[128 + M :] + (pr * ui + pi * ur)

    col = lax.broadcasted_iota(jnp.int32, (B, 128), 0)

    def block(b, _):
        begin = first + b * B
        rows = rows_at(b * B, B)
        seg_t = seg(begin + lane)
        same = flag(seg_t == seg(begin + sub * Q - 1))
        ma1_s[...] = jnp.concatenate([same] * 16 + [flag(seg_t == seg(begin + B - 1))] * 2, axis=0).astype(BF16)
        same = flag(seg_t == seg(begin + (sub + 1) * Q))
        ma2_s[...] = jnp.concatenate([same] * 16 + [flag(seg_t == seg(begin))] * 2, axis=0).astype(BF16)
        km_s[...] = flag(seg(begin + sub * Q - 1) == seg(begin - 1))
        for i in range(Q):
            at = begin + sub * Q + i
            keep_s[i] = flag(seg(at) == seg(at - 1))
        seg_c = seg(begin + col)
        mb1_s[...] = flag(seg_c == seg(begin + (col // Q) * Q - 1))
        mb2_s[...] = flag(seg_c == seg(begin + (col // Q + 1) * Q))
        keep_block = flag(seg(begin + B - 1) == seg(begin - 1))

        for k in range(1, nt):
            feature_copy(k, b, lax.rem(t_me - k + nt, nt)).wait_recv()
        fb = feat[rows, :]
        query = dot(fb, proj[0]).astype(BF16)
        signal = dot(fb, proj[1]).astype(BF16)
        q_s[rows, :] = query
        g = query.astype(F32) * up[rows, :].astype(F32)
        signal32 = signal.astype(F32)
        for h in range(H):
            cols = slice(h * 128, h * 128 + 128)
            x_scr[h] = signal32[:, cols]
            g_scr[h] = g[:, cols]
            xb_s[h] = signal[:, cols]
            gb_s[h] = g[:, cols].astype(BF16)
            gm_s[h] = (g[:, cols] * mb1_s[...]).astype(BF16)
        feat_t[b] = fb.T

        for h in range(H):
            head(b, keep_block, h)
        return 0

    lax.fori_loop(0, nb, block, 0)

    def turned(h, which, re, im, kept):
        pr, pi = pstep_s[h, which, 0] * kept, pstep_s[h, which, 1] * kept
        return pr * re - pi * im, pr * im + pi * re

    def reverse_scan(start, store):
        state = start
        for b in reversed(range(nb)):
            begin = first + b * B
            kept = flag(seg(begin) == seg(begin + B))
            following = []
            for h in range(H):
                re, im = state[h]
                if store:
                    g_end[b, h, :M, :], g_end[b, h, M:, :] = re, im
                tr, ti = turned(h, 1, re, im, kept)
                following.append((lead_s[b, h, :M, :] + tr, lead_s[b, h, M:, :] + ti))
            state = following
        return state

    zero = jnp.zeros((M, 128), F32)
    ends = reverse_scan([(zero, zero)] * H, False)
    for h in range(H):
        d_s[h, :M, :], d_s[h, M:, :] = ends[h]

    def end_copy(src, dst, send, recv, slot, to):
        return pltpu.make_async_remote_copy(
            src_ref=src, dst_ref=dst.at[slot], send_sem=send.at[to], recv_sem=recv.at[slot],
            device_id=place(tm=to), device_id_type=MESH,
        )

    def forward_copy(slot, to):
        return end_copy(u_s, endf_r, ef_s, ef_r, slot, to)

    def backward_copy(slot, to):
        return end_copy(d_s, endb_r, eb_s, eb_r, slot, to)

    def send_ends(to, _):
        @pl.when(to > z)
        def _():
            forward_copy(z, to).start()

        @pl.when(to < z)
        def _():
            backward_copy(z, to).start()

        return 0

    lax.fori_loop(0, n, send_ends, 0)
    ent_s[...] = jnp.zeros_like(ent_s)
    lea_s[...] = jnp.zeros_like(lea_s)

    def enter(src, _):
        @pl.when(src < z)
        def _():
            forward_copy(src, z).wait_recv()
            kept = flag(seg(src * R - 1) == seg(src * R + R - 1))
            for h in range(H):
                tr, ti = turned(h, 2, ent_s[h, :M, :], ent_s[h, M:, :], kept)
                ent_s[h, :M, :] = endf_r[src, h, :M, :] + tr
                ent_s[h, M:, :] = endf_r[src, h, M:, :] + ti

        return 0

    lax.fori_loop(0, n, enter, 0)

    def weigh(h, re, im):
        wr, wi = w_s[h, 0], w_s[h, 1]
        pad = [jnp.zeros((128 - 2 * M, 128), F32)]
        return jnp.concatenate([wr * re - wi * im, -(wr * im + wi * re)] + pad, axis=0).astype(BF16)

    kept_first = flag(seg(first) == seg(first - 1))
    for h in range(H):
        lr, li = turned(h, 0, d_s[h, :M, :], d_s[h, M:, :], kept_first)
        er, ei = ent_s[h, :M, :], ent_s[h, M:, :]
        re, im = [], []
        for m in range(M):
            re.append(jnp.sum(rc_s[h, m], axis=0, keepdims=True))
            im.append(jnp.sum(rc_s[h, M + m], axis=0, keepdims=True))
        re = jnp.concatenate(re, axis=0) + er * lr - ei * li
        im = jnp.concatenate(im, axis=0) + er * li + ei * lr
        for lag in range(Q):
            r = jnp.sum(r_s[h, lag], axis=0, keepdims=True)
            if lag == 0:
                skip_row = r
            re = re + pos_s[h, 0, :, lag : lag + 1] * r
            im = im + pos_s[h, 1, :, lag : lag + 1] * r
        cols = slice(h * 128, h * 128 + 128)
        scale = wgt_s[h] * norm
        terms = jnp.concatenate([re * scale, -im * scale, skip_row * norm, jnp.zeros((15, 128), F32)], axis=0)
        own = rows_at(core * 16, 16)
        mdps[:, cols] = jnp.where(core == 0, terms[16:], terms[:16])
        macc[:, cols] = jnp.where(core == 0, terms[:16], terms[16:])

    def enter_block(b, _):
        begin = first + b * B
        rows = rows_at(b * B, B)
        kept = flag(seg(begin + col) == seg(first - 1))
        for h in range(H):
            cols = slice(h * 128, h * 128 + 128)
            er, ei = ent_s[h, :M, :], ent_s[h, M:, :]
            y = y_loc[h, rows, :] + kept * dot(colp_s[h], weigh(h, er, ei))
            mixed_v[rows, cols] = (q_s[rows, cols].astype(F32) * y).astype(BF16)
            gq[rows, cols] = (up[rows, cols].astype(F32) * y).astype(BF16)
            ent_s[h, :M, :], ent_s[h, M:, :] = turned(h, 1, er, ei, 1.0)
        return 0

    lax.fori_loop(0, nb, enter_block, 0)
    mixed_copy = pltpu.make_async_copy(mixed_v, mixed_out, out_sem.at[0])
    mixed_copy.start()

    quarter = half // 2

    def partner_copy(k, i):
        r = rows_at(k * half + i * quarter, quarter)
        return pltpu.make_async_remote_copy(
            src_ref=dpsnd.at[r], dst_ref=dprcv.at[r], send_sem=dps_s.at[k, i], recv_sem=dps_r.at[k, i],
            device_id=place(dp=1 - core), device_id_type=MESH,
        )

    def transposed(start):
        return jnp.concatenate([feat_t[b, rows_at(start, quarter), :] for b in range(nb)], axis=1)

    def others_part(k, i, other):
        r = rows_at(k * half + i * quarter, quarter)
        dpsnd[r] = (dot(transposed((1 - core) * half + i * quarter), other[...]) * norm).astype(BF16)
        partner_copy(k, i).start()

    def own_part(k, i, other):
        r = rows_at(k * half + i * quarter, quarter)
        pacc[r] = dot(transposed(core * half + i * quarter), other[...]) * norm
        partner_copy(k, i).wait_recv()

        @pl.when(big.no_out)
        def _():
            def go(j, _):
                big.up(k * nch + i * (nch // 2) + j)
                return 0

            lax.fori_loop(0, nch // 2, go, 0)

    others_part(0, 0, gq)
    others_part(0, 1, gq)
    own_part(0, 0, gq)
    own_part(0, 1, gq)
    small_partner = pltpu.make_async_remote_copy(
        src_ref=mdps, dst_ref=mdpr, send_sem=md_s, recv_sem=md_r, device_id=place(dp=1 - core), device_id_type=MESH
    )
    small_partner.start()

    def leave(i, _):
        src = n - 1 - i

        @pl.when(src > z)
        def _():
            backward_copy(src, z).wait_recv()
            kept = flag(seg(src * R) == seg(src * R + R))
            for h in range(H):
                tr, ti = turned(h, 2, lea_s[h, :M, :], lea_s[h, M:, :], kept)
                lea_s[h, :M, :] = endb_r[src, h, :M, :] + tr
                lea_s[h, M:, :] = endb_r[src, h, M:, :] + ti

        return 0

    lax.fori_loop(0, n, leave, 0)
    reverse_scan([(lea_s[h, :M, :], lea_s[h, M:, :]) for h in range(H)], True)

    def ig_copy(k, b, sender):
        rows = rows_at(b * B, B)
        return pltpu.make_async_remote_copy(
            src_ref=igs.at[k - 1, rows], dst_ref=igr.at[k - 1, rows], send_sem=ig_s.at[k - 1, b],
            recv_sem=ig_r.at[k - 1, b], device_id=place(tensor=lax.rem(t_me + k, nt)), device_id_type=MESH,
        )

    def leave_block(b, _):
        begin = first + b * B
        rows = rows_at(b * B, B)
        kept = flag(seg(begin + col) == seg(begin + B))
        for h in range(H):
            cols = slice(h * 128, h * 128 + 128)
            gr, gi = g_end[b, h, :M, :], g_end[b, h, M:, :]
            gx = gx_loc[h, rows, :] + kept * dot(colh_s[h], weigh(h, gr, gi))
            gv[rows, cols] = gx.astype(BF16)
        for k in range(1, nt):
            to = lax.rem(t_me + k, nt)
            part = rows_at(to * share, share)
            igs[k - 1, rows, :] = (
                dot_nt(gq[rows, :], proj[0, part, :]) + dot_nt(gv[rows, :], proj[1, part, :])
            ).astype(BF16)
            ig_copy(k, b, t_me).start()
        return 0

    def ig_own(b, _):
        rows = rows_at(b * B, B)
        part = rows_at(t_me * share, share)
        iga[rows, :] = dot_nt(gq[rows, :], proj[0, part, :]) + dot_nt(gv[rows, :], proj[1, part, :])
        return 0

    steps = 2 * nch
    def middle_step(s, _=None):
        @pl.when(big.has_out & (s < steps))
        def _():
            big.up(s)

        @pl.when(big.has_out & (s >= LAG))
        def _():
            big.down(s - LAG)

        return 0

    def end_step(s, _):
        @pl.when(big.no_out)
        def _():
            big.down(s)

        return 0

    def ig_rest(b, _):
        rows = rows_at(b * B, B)
        total = iga[rows, :]
        for k in range(1, nt):
            ig_copy(k, b, t_me).wait_recv()
            total = total + igr[k - 1, rows, :].astype(F32)
        gv[rows, :share] = total.astype(BF16)
        return 0

    def finish(s, _):
        big.finish(s)
        return 0

    def pg_copy(k):
        r = pl.ds(k * D, D)
        return pltpu.make_async_copy(tot.at[r], pg_out.at[r], out_sem.at[2 + k])

    work = [functools.partial(lax.fori_loop, b, min(b + 2, nb), leave_block, 0) for b in range(1, nb, 2)]
    work += [functools.partial(others_part, 1, i, gv) for i in range(2)]
    work += [functools.partial(own_part, 1, i, gv) for i in range(2)]
    work += [functools.partial(lax.fori_loop, b, min(b + 3, nb), ig_own, 0) for b in range(0, nb, 3)]
    leave_block(0, 0)
    for s, item in enumerate(work):
        middle_step(s)
        item()
    lax.fori_loop(len(work), steps - 2, middle_step, 0)
    small_partner.wait_recv()
    pl.when(small.no_out)(lambda: small.up(0))
    lax.fori_loop(0, nch, end_step, 0)
    lax.fori_loop(0, nch // GROUP, finish, 0)
    pg_copy(0).start()
    pl.when(small.has_out)(lambda: small.up(0))
    lax.fori_loop(steps - 2, steps, middle_step, 0)
    small.down(0)
    lax.fori_loop(0, nb, ig_rest, 0)
    ig_out_copy = pltpu.make_async_copy(gv.at[:, :share], ig_out, out_sem.at[1])
    ig_out_copy.start()
    lax.fori_loop(steps, steps + LAG, middle_step, 0)
    lax.fori_loop(nch, steps, end_step, 0)
    small.finish(0)
    res_copy = pltpu.make_async_copy(mtot.at[pl.ds(0, 2 * M)], res_out, out_sem.at[4])
    skip_copy = pltpu.make_async_copy(mtot.at[pl.ds(2 * M, 8)], skip_out, out_sem.at[5])
    res_copy.start()
    skip_copy.start()
    lax.fori_loop(nch // GROUP, steps // GROUP, finish, 0)
    pg_copy(1).start()

    for b in range(nb):
        for k in range(1, nt):
            feature_copy(k, b, t_me).wait_send()
            ig_copy(k, b, t_me).wait_send()
    for k in range(2):
        for i in range(2):
            partner_copy(k, i).wait_send()
    small_partner.wait_send()

    def sent(to, _):
        @pl.when(to > z)
        def _():
            forward_copy(z, to).wait_send()

        @pl.when(to < z)
        def _():
            backward_copy(z, to).wait_send()

        return 0

    lax.fori_loop(0, n, sent, 0)
    mixed_copy.wait()
    ig_out_copy.wait()
    pg_copy(0).wait()
    pg_copy(1).wait()
    res_copy.wait()
    skip_copy.wait()


def assemble_kernel(mixed, ig, pg, res, skips, mixed_o, ig_o, pg_o, res_o, skip_o, wide, sems):
    parts, rows = wide.shape[:2]
    stores = [pltpu.make_async_copy(wide.at[i], pg_o.at[pl.ds(i * rows, rows)], sems.at[i]) for i in range(parts)]
    for i, (src, dst) in enumerate(((mixed, mixed_o), (ig, ig_o), (res, res_o), (skips.at[pl.ds(0, 1)], skip_o))):
        stores.append(pltpu.make_async_copy(src, dst, sems.at[parts + i]))
        stores[-1].start()
    for i in range(parts):
        wide[i] = pg[pl.ds(i * rows, rows), :].astype(F32)
        stores[i].start()
    for copy in stores:
        copy.wait()


def shards(frames_in, in_proj, log_rates, angles, residues, skip_gain, lengths, grad_out):
    R, C = frames_in.shape[1:]
    D = in_proj.shape[1]
    M, H = log_rates.shape
    clips = lengths.shape[1]
    n, nt = lax.axis_size("tm"), lax.axis_size("tensor")
    nb = R // B
    norm = 1.0 / math.sqrt(R * n * lax.axis_size("dp"))
    half = D // 2
    nch = half // STEP
    share = D // nt
    resid = residues.reshape(2, M, H, 128).transpose(0, 2, 1, 3)
    skip = skip_gain.reshape(H, 1, 128)
    vm, dma = pltpu.VMEM, pltpu.SemaphoreType.DMA

    def chain_sems(steps, group):
        return [dma((steps,))] * 5 + [dma((steps // group,))] * 2

    scratch = [
        vm((R, D), BF16), vm((nb, D, B), BF16), vm((2, D, C), BF16), vm((R, C), BF16), vm((R, C), BF16),
        vm((H, B, 128), F32), vm((H, B, 128), F32), vm((H, B, 128), F32), vm((H, B, 128), F32),
        vm((H, B, 128), BF16), vm((H, B, 128), BF16), vm((H, B, 128), BF16),
        vm((H, R, 128), F32), vm((H, R, 128), F32), vm((R, C), BF16), vm((R, C), BF16), vm((R, C), BF16),
        vm((H, 144, 128), BF16), vm((H, 144, 128), BF16), vm((H, 128, 128), BF16), vm((H, 128, 128), BF16),
        vm((H, 128, 128), BF16), vm((H, 128, 128), BF16), vm((H, 128, 128), BF16),
        vm((H, 2, 8 * M, 128), F32), vm((H, 2, M, 128), F32), vm((H, 3, 2, M, 128), F32), vm((H, 2, M, 128), F32),
        vm((H, Q, 8, 128), F32), vm((H, M, 128), F32),
        vm((144, 128), BF16), vm((144, 128), BF16), vm((Q, 8, 128), F32), vm((8, 128), F32), vm((B, 128), F32),
        vm((B, 128), F32),
        vm((H, 2 * M, 128), F32), vm((H, 2 * M, 128), F32), vm((nb, H, 2 * M, 128), F32), vm((nb, H, 2 * M, 128), F32),
        vm((H, Q, 8, 128), F32), vm((H, 2 * M, 8, 128), F32), vm((H, 2 * M, 128), F32), vm((H, 2 * M, 128), F32),
        vm((n, H, 2 * M, 128), F32), vm((n, H, 2 * M, 128), F32),
        vm((2 * half, C), F32), vm((2 * half, C), BF16), vm((2 * half, C), BF16), vm((2 * half, C), BF16),
        vm((2 * half, C), BF16), vm((2 * half, C), BF16), vm((2 * D, C), BF16),
        vm((16, C), F32), vm((16, C), F32), vm((16, C), F32), vm((16, C), F32), vm((16, C), F32), vm((16, C), F32),
        vm((32, C), F32),
        vm((nt - 1, R, share), BF16), vm((nt - 1, R, share), BF16), vm((R, share), F32),
        dma((3,)), dma((nt - 1, nb)), dma((nt - 1, nb)), dma((n,)), dma((n,)), dma((n,)), dma((n,)),
        dma((2, 2)), dma((2, 2)), dma((nt - 1, nb)), dma((nt - 1, nb)), dma, dma, dma((6,)),
    ] + chain_sems(2 * nch, GROUP) + chain_sems(1, 1)
    vmem = pl.BlockSpec(memory_space=pltpu.VMEM)
    anywhere = pl.BlockSpec(memory_space=pl.ANY)
    mixed, ig, pg, res, skips = pl.pallas_call(
        functools.partial(layer_kernel, (clips, M, H, R, C, D, norm)),
        out_shape=[
            vm((R, C), BF16), vm((R, share), BF16), vm((2 * D, C), BF16), vm((2 * M, C), F32), vm((8, C), F32),
        ],
        in_specs=[pl.BlockSpec(memory_space=pltpu.SMEM)] + [vmem] * 4 + [anywhere] * 3,
        out_specs=[vmem] * 5,
        scratch_shapes=scratch,
        compiler_params=pltpu.CompilerParams(
            collective_id=0, has_side_effects=True, vmem_limit_bytes=56 << 20
        ),
        name="layer",
    )(lengths, log_rates.T, angles.T, resid, skip, frames_in[0], in_proj, grad_out[0])
    parts = 8
    mixed, ig, pg, res, skips = pl.pallas_call(
        assemble_kernel,
        out_shape=[
            jax.ShapeDtypeStruct((R, C), BF16), jax.ShapeDtypeStruct((R, share), BF16),
            jax.ShapeDtypeStruct((2 * D, C), F32), jax.ShapeDtypeStruct((2 * M, C), F32),
            jax.ShapeDtypeStruct((1, C), F32),
        ],
        in_specs=[vmem] * 5,
        out_specs=[anywhere] * 5,
        scratch_shapes=[vm((parts, 2 * D // parts, C), F32), dma((parts + 4,))],
        compiler_params=pltpu.CompilerParams(vmem_limit_bytes=20 << 20),
        name="assemble",
    )(mixed, ig, pg, res, skips)
    return mixed[None], ig[None], pg.reshape(2, D, C), res.reshape(2, M, C), skips[0]


def solution(mesh):
    in_specs = (
        P(("group", "dp"), "tm", "tensor"),
        P(None, None, "tensor"),
        P(None, "tensor"),
        P(None, "tensor"),
        P(None, None, "tensor"),
        P("tensor"),
        P(("group", "dp"), None),
        P(("group", "dp"), "tm", "tensor"),
    )
    out_specs = (
        P(("group", "dp"), "tm", "tensor"),
        P(("group", "dp"), "tm", "tensor"),
        P("group", None, "tensor"),
        P("group", None, "tensor"),
        P(("group", "tensor")),
    )
    return jax.shard_map(shards, mesh=mesh, in_specs=in_specs, out_specs=out_specs, check_vma=False)
```

```python
import functools
import math

import jax
import jax.numpy as jnp
from jax import lax
from jax.experimental import pallas as pl
from jax.experimental.pallas import tpu as pltpu
from jax.sharding import PartitionSpec as P

F32 = jnp.float32
BF16 = jnp.bfloat16
AXES = ("group", "tm", "tensor", "dp")
MESH = pl.DeviceIdType.MESH
Q = 16
B = 128
LAG = 2
GROUP = 4
EARLY = 3
STEP = 64


def dot(a, b):
    return jnp.dot(a, b, preferred_element_type=F32)


def dot_nt(a, b):
    return lax.dot_general(a, b, (((1,), (1,)), ((), ())), preferred_element_type=F32)


def flag(cond):
    return jnp.where(cond, 1.0, 0.0).astype(F32)


def rows_at(start, size, step=8):
    return pl.ds(pl.multiple_of(start, step), size)


class Place:
    def __init__(self):
        self.at = {axis: lax.axis_index(axis) for axis in AXES}

    def __call__(self, **moved):
        return tuple(moved.get(axis, self.at[axis]) for axis in AXES)


class Chain:
    def __init__(self, place, acc, also, snd, upb, inb, tot, sems, nch, size, half, tot_rows, group, core):
        n, z = lax.axis_size("tm"), place.at["tm"]
        left = z < n // 2
        self.inward = place(tm=jnp.where(left, z + 1, z - 1))
        self.outward = place(tm=jnp.clip(jnp.where(left, z - 1, z + 1), 0, n - 1))
        self.partner = place(dp=1 - core)
        depth = jnp.where(left, n // 2 - 1 - z, z - n // 2)
        self.root = depth == 0
        self.inner = depth > 0
        self.has_out = depth < n // 2 - 1
        self.no_out = depth == n // 2 - 1
        self.acc, self.also, self.snd, self.upb, self.inb, self.tot = acc, also, snd, upb, inb, tot
        (self.up_s, self.up_r, self.in_r, self.to_s, self.tot_r, self.dp_s, self.dp_r) = sems
        self.nch, self.size, self.half, self.tot_rows, self.group, self.core = nch, size, half, tot_rows, group, core
        self.wire = snd.dtype

    def row(self, s):
        return rows_at(s * self.size, self.size)

    def total_row(self, s, core, count=1):
        r = (s // self.nch) * self.tot_rows + core * self.half + (s % self.nch) * self.size
        return rows_at(r, self.size * count)

    def copy(self, src, dst, send, recv, to):
        return pltpu.make_async_remote_copy(
            src_ref=src, dst_ref=dst, send_sem=send, recv_sem=recv, device_id=to, device_id_type=MESH
        )

    def up_copy(self, s):
        r = self.row(s)
        return self.copy(self.snd.at[r], self.upb.at[r], self.up_s.at[s], self.up_r.at[s], self.inward)

    def in_copy(self, s):
        r = self.row(s)
        return self.copy(self.snd.at[r], self.inb.at[r], self.up_s.at[s], self.in_r.at[s], self.inward)

    def out_copy(self, s):
        r = self.total_row(s, self.core)
        return self.copy(self.tot.at[r], self.tot.at[r], self.to_s.at[s], self.tot_r.at[s], self.outward)

    def dp_copy(self, g, core):
        r = self.total_row(g * self.group, core, self.group)
        return self.copy(self.tot.at[r], self.tot.at[r], self.dp_s.at[g], self.dp_r.at[g], self.partner)

    def up(self, s):
        r = self.row(s)

        @pl.when(self.no_out)
        def _():
            self.snd[r] = (self.acc[r] + self.also[r].astype(F32)).astype(self.wire)

        @pl.when(self.has_out)
        def _():
            self.up_copy(s).wait_recv()
            self.snd[r] = (self.acc[r] + self.also[r].astype(F32) + self.upb[r].astype(F32)).astype(self.wire)

        @pl.when(self.inner)
        def _():
            self.up_copy(s).start()

        @pl.when(self.root)
        def _():
            self.in_copy(s).start()

    def down(self, s):
        @pl.when(self.root)
        def _():
            r = self.row(s)
            self.in_copy(s).wait_recv()
            self.tot[self.total_row(s, self.core)] = (self.snd[r].astype(F32) + self.inb[r].astype(F32)).astype(self.wire)

        @pl.when(self.inner)
        def _():
            self.out_copy(s).wait_recv()

        @pl.when(self.has_out)
        def _():
            self.out_copy(s).start()

        @pl.when(s % self.group == self.group - 1)
        def _():
            self.dp_copy(s // self.group, self.core).start()

    def finish(self, g):
        self.dp_copy(g, self.core).wait_send()
        self.dp_copy(g, 1 - self.core).wait_recv()
        for i in range(self.group):
            s = g * self.group + i

            @pl.when(self.has_out)
            def _():
                self.out_copy(s).wait_send()

            self.up_copy(s).wait_send()


def layer_kernel(
    cfg,
    lens_ref, rates_ref, angles_ref, resid_ref, skip_ref, frames_ref, proj_ref, up_hbm,
    mixed_out, ig_out, pg_out, res_out, skip_out,
    feat, feat_t, proj, up, q_s, x_scr, g_scr, y_scr, gx_scr, xb_s, gb_s, gm_s, y_loc, gx_loc, gq, gv, mixed_v,
    a1_s, a2_s, bt_s, b1_s, b2_s, colp_s, colh_s, pk_s, pos_s, pstep_s, w_s, k_s, wgt_s,
    ma1_s, ma2_s, keep_s, km_s, mb1_s, mb2_s,
    u_s, d_s, lead_s, g_end, r_s, rc_s, ent_s, lea_s, endf_r, endb_r,
    pacc, psnd, dpsnd, dprcv, upb, inb, tot, macc, msnd, mdps, mdpr, mupb, minb, mtot, igs, igr, iga,
    poles_mine, poles_r, reach_s, zsnd, zbuf, ue_s, e0_s, p_s, p_r, z_s, z_r,
    loc_sem, f_s, f_r, ef_s, ef_r, eb_s, eb_r, dps_s, dps_r, ig_s, ig_r, md_s, md_r, out_sem,
    *chain_sems,
):
    clips, M, H, R, C, D, norm = cfg
    nb = R // B
    place = Place()
    n, z = lax.axis_size("tm"), place.at["tm"]
    nt, t_me = lax.axis_size("tensor"), place.at["tensor"]
    core = place.at["dp"]
    first = z * R
    share = D // nt
    half = D // 2
    big_sems, small_sems = chain_sems[:7], chain_sems[7:]
    nch = half // STEP
    big = Chain(place, pacc, dprcv, psnd, upb, inb, tot, big_sems, nch, STEP, half, D, GROUP, core)
    small = Chain(place, macc, mdpr, msnd, mupb, minb, mtot, small_sems, 1, 16, 16, 32, 1, core)

    clip_starts = [jnp.int32(0)]
    for k in range(clips - 1):
        clip_starts.append(clip_starts[-1] + lens_ref[0, k])

    def seg(frame):
        total = jnp.where(frame >= clip_starts[0], 1, 0)
        for k in range(1, clips):
            total = total + jnp.where(frame >= clip_starts[k], 1, 0)
        return total

    mine = pl.ds(pl.multiple_of(t_me * C, 128), C)
    own_in = pltpu.make_async_copy(frames_ref, feat.at[:, mine], loc_sem.at[0])
    proj_in = pltpu.make_async_copy(proj_ref, proj, loc_sem.at[1])
    up_in = pltpu.make_async_copy(up_hbm, up, loc_sem.at[2])
    own_in.start()
    proj_in.start()
    up_in.start()

    barrier = pltpu.get_barrier_semaphore()
    for k in range(1, nt):
        pl.semaphore_signal(barrier, inc=1, device_id=place(tensor=lax.rem(t_me + k, nt)), device_id_type=MESH)
    pl.semaphore_signal(barrier, inc=1, device_id=place(dp=1 - core), device_id_type=MESH)
    for k in range(1, n):
        pl.semaphore_signal(barrier, inc=1, device_id=place(tm=lax.rem(z + k, n)), device_id_type=MESH)
    pl.semaphore_wait(barrier, nt + n - 1)

    def feature_copy(k, b, sender):
        rows = rows_at(b * B, B)
        cols = pl.ds(pl.multiple_of(sender * C, 128), C)
        return pltpu.make_async_remote_copy(
            src_ref=frames_ref.at[rows], dst_ref=feat.at[rows, cols], send_sem=f_s.at[k - 1, b],
            recv_sem=f_r.at[k - 1, b], device_id=place(tensor=lax.rem(t_me + k, nt)), device_id_type=MESH,
        )

    def pole_copy(k):
        return pltpu.make_async_remote_copy(
            src_ref=poles_mine, dst_ref=poles_r.at[k - 1], send_sem=p_s.at[k - 1], recv_sem=p_r.at[k - 1],
            device_id=place(tensor=lax.rem(t_me + k, nt)), device_id_type=MESH,
        )

    def z_copy(k, sender):
        cols = pl.ds(pl.multiple_of(sender * C, 128), C)
        return pltpu.make_async_remote_copy(
            src_ref=zsnd.at[k - 1], dst_ref=zbuf.at[:, cols], send_sem=z_s.at[k - 1], recv_sem=z_r.at[k - 1],
            device_id=place(tensor=lax.rem(t_me + k, nt)), device_id_type=MESH,
        )

    poles_mine[...] = jnp.zeros_like(poles_mine)
    poles_mine[:H, :M] = rates_ref[...]
    poles_mine[8 : 8 + H, :M] = angles_ref[...]
    for k in range(1, nt):
        pole_copy(k).start()
    for b in range(min(2, nb)):
        for k in range(1, nt):
            feature_copy(k, b, t_me).start()

    lane = lax.broadcasted_iota(jnp.int32, (8, 128), 1)
    sub = lax.broadcasted_iota(jnp.int32, (8, 128), 0)
    lanef = lane.astype(F32)
    in_chunk = lane % Q
    chunk = lane // Q
    square = lax.broadcasted_iota(jnp.int32, (M, M), 0) == lax.broadcasted_iota(jnp.int32, (M, M), 1)

    def upright(rates, turns):
        d = jnp.exp(jnp.sum(jnp.where(square, rates, 0.0), axis=1, keepdims=True))
        return d, jnp.sum(jnp.where(square, turns, 0.0), axis=1, keepdims=True)

    def powers_of(lag, d, a):
        size = jnp.exp(-d * lag)
        return size * jnp.cos(a * lag), size * jnp.sin(a * lag)

    def reach(ref):
        def one(h, _):
            d, a = upright(ref[pl.ds(h, 1), :][:, :M], ref[pl.ds(8 + h, 1), :][:, :M])
            re, im = powers_of(127.0 - lanef, d, a)
            step_re, step_im = powers_of(jnp.full((M, 128), float(B), F32), d, a)
            for b in reversed(range(nb)):
                kept = flag(seg(first + b * B + lane) == seg(first + R - 1))
                reach_s[rows_at(h * 16, 16, 16), b * B : b * B + B] = jnp.concatenate(
                    [re * kept, im * kept], axis=0
                ).astype(BF16)
                re, im = step_re * re - step_im * im, step_re * im + step_im * re
            return 0

        lax.fori_loop(0, H, one, 0)
        return dot(reach_s[...], feat[:, mine]).astype(BF16)

    own_in.wait()
    zbuf[:, mine] = reach(poles_mine)
    for k in range(1, nt):
        pole_copy(nt - k).wait_recv()
        zsnd[k - 1] = reach(poles_r.at[nt - k - 1])
        z_copy(k, t_me).start()
    for b in range(min(2, nb), nb):
        for k in range(1, nt):
            feature_copy(k, b, t_me).start()

    def tables(h, _):
        d, a = upright(rates_ref[pl.ds(h, 1), :], angles_ref[pl.ds(h, 1), :])

        def powers(lag, dd=d, aa=a):
            return powers_of(lag, dd, aa)

        pos_re, pos_im = powers(lanef)
        nxt_re, nxt_im = powers(lanef + 1.0)
        neg_re, neg_im = powers(-lanef - 1.0)
        end_re, end_im = powers(127.0 - lanef)
        far_re, far_im = powers(128.0 - lanef)
        b1_re, b1_im = powers((in_chunk + 1).astype(F32))
        b2_re, b2_im = powers((Q - in_chunk).astype(F32))
        pos_s[h, 0], pos_s[h, 1] = pos_re, pos_im
        for i, lag in enumerate((1.0, float(B), float(R))):
            pr, pi = powers(jnp.full((M, 128), lag, F32))
            pstep_s[h, i, 0], pstep_s[h, i, 1] = pr, pi
        y = 2.0 * d
        series = y * (1.0 - y / 2 * (1.0 - y / 3 * (1.0 - y / 4 * (1.0 - y / 5 * (1.0 - y / 6 * (1.0 - y / 7))))))
        wgt = jnp.sqrt(jnp.where(y < 0.25, series, 1.0 - jnp.exp(-y)))
        wgt = jnp.broadcast_to(wgt, (M, 128))
        wgt_s[h] = wgt
        wr, wi = resid_ref[0, h] * wgt, resid_ref[1, h] * wgt
        w_s[h, 0], w_s[h, 1] = wr, wi
        for k in range(Q):
            tap = jnp.sum(wr * pos_re[:, k : k + 1] - wi * pos_im[:, k : k + 1], axis=0, keepdims=True)
            if k == 0:
                tap = tap + skip_ref[h]
            k_s[h, k] = jnp.broadcast_to(tap, (8, 128))
        a1r, a1i, a2r, a2i, btr, bti, b2r, b2i = [], [], [], [], [], [], [], []
        subf = sub.astype(F32) * Q
        for m in range(M):
            one = slice(m, m + 1)
            pr, pi = powers(subf, d[one], a[one])
            pk_s[h, 0, m * 8 : m * 8 + 8], pk_s[h, 1, m * 8 : m * 8 + 8] = pr, pi
            back_re, back_im = powers(-subf - float(Q), d[one], a[one])
            fr, fi = neg_re[one], neg_im[one]
            past = lane < sub * Q
            a1r.append(jnp.where(past, pr * fr - pi * fi, 0.0))
            a1i.append(jnp.where(past, pr * fi + pi * fr, 0.0))
            fr, fi = pos_re[one], pos_im[one]
            later = lane >= (sub + 1) * Q
            a2r.append(jnp.where(later, back_re * fr - back_im * fi, 0.0))
            a2i.append(jnp.where(later, back_re * fi + back_im * fr, 0.0))
            here = chunk == sub
            btr.append(jnp.where(here, b1_re[one], 0.0))
            bti.append(jnp.where(here, b1_im[one], 0.0))
            b2r.append(jnp.where(here, b2_re[one], 0.0))
            b2i.append(jnp.where(here, b2_im[one], 0.0))
        a1_s[h] = jnp.concatenate(a1r + a1i + [end_re, end_im], axis=0).astype(BF16)
        a2_s[h] = jnp.concatenate(a2r + a2i + [pos_re, pos_im], axis=0).astype(BF16)
        bt = jnp.concatenate(btr + bti, axis=0)
        bt_s[h] = bt.astype(BF16)
        b1_s[h] = bt.T.astype(BF16)
        b2_s[h] = jnp.concatenate(b2r + b2i, axis=0).T.astype(BF16)
        pad = [jnp.zeros((128 - 2 * M, 128), F32)]
        colp_s[h] = jnp.concatenate([nxt_re, nxt_im] + pad, axis=0).T.astype(BF16)
        colh_s[h] = jnp.concatenate([far_re, far_im] + pad, axis=0).T.astype(BF16)
        return 0

    lax.fori_loop(0, H, tables, 0)
    u_s[...] = jnp.zeros_like(u_s)
    r_s[...] = jnp.zeros_like(r_s)
    rc_s[...] = jnp.zeros_like(rc_s)
    proj_in.wait()
    up_in.wait()

    def head(b, keep_block, h):
        rows = rows_at(b * B, B)
        xs = [x_scr[h, pl.ds(i, 8, stride=Q), :] for i in range(Q)]
        gs = [g_scr[h, pl.ds(i, 8, stride=Q), :] for i in range(Q)]
        held, corr = [], [None] * Q
        for i in range(Q):
            if i:
                kept = keep_s[i]
                held = [v * kept for v in held]
            held.append(xs[i])
            acc = None
            for s in range(i + 1):
                lag = i - s
                term = k_s[h, lag] * held[s]
                acc = term if acc is None else acc + term
                both = gs[i] * held[s]
                corr[lag] = both if corr[lag] is None else corr[lag] + both
            y_scr[h, pl.ds(i, 8, stride=Q), :] = acc
        for lag in range(Q):
            r_s[h, lag] += corr[lag]
        held = []
        for s in reversed(range(Q)):
            if s < Q - 1:
                kept = keep_s[s + 1]
                held = [v * kept for v in held]
            held = [gs[s]] + held
            acc = None
            for lag in range(Q - s):
                term = k_s[h, lag] * held[lag]
                acc = term if acc is None else acc + term
            gx_scr[h, pl.ds(s, 8, stride=Q), :] = acc

        states = dot(a1_s[h] * ma1_s[...], xb_s[h])
        leads = dot(bt_s[h], gm_s[h])
        adj = dot(a2_s[h] * ma2_s[...], gb_s[h])
        kept = km_s[...]
        vr, vi, ar, ai = [], [], [], []
        for m in range(M):
            re, im = slice(m * 8, m * 8 + 8), slice(64 + m * 8, 72 + m * 8)
            pr, pi = pk_s[h, 0, re] * kept, pk_s[h, 1, re] * kept
            ur, ui = u_s[h, m : m + 1, :], u_s[h, M + m : M + m + 1, :]
            sr = states[re] + (pr * ur - pi * ui)
            si = states[im] + (pr * ui + pi * ur)
            lr, li = leads[re], leads[im]
            rc_s[h, m] += sr * lr - si * li
            rc_s[h, M + m] += sr * li + si * lr
            wr, wi = w_s[h, 0, m : m + 1, :], w_s[h, 1, m : m + 1, :]
            vr.append(wr * sr - wi * si)
            vi.append(-(wr * si + wi * sr))
            ar.append(wr * adj[re] - wi * adj[im])
            ai.append(-(wr * adj[im] + wi * adj[re]))
        v = jnp.concatenate(vr + vi, axis=0).astype(BF16)
        y_loc[h, rows, :] = y_scr[h] + mb1_s[...] * dot(b1_s[h], v)
        v = jnp.concatenate(ar + ai, axis=0).astype(BF16)
        gx_loc[h, rows, :] = gx_scr[h] + mb2_s[...] * dot(b2_s[h], v)
        lead_s[b, h] = adj[128:]
        pr, pi = pstep_s[h, 1, 0] * keep_block, pstep_s[h, 1, 1] * keep_block
        ur, ui = u_s[h, :M, :], u_s[h, M:, :]
        u_s[h, :M, :] = states[128 : 128 + M] + (pr * ur - pi * ui)
        u_s[h, M:, :] = states[128 + M :] + (pr * ui + pi * ur)

    col = lax.broadcasted_iota(jnp.int32, (B, 128), 0)

    def block(b, _):
        begin = first + b * B
        rows = rows_at(b * B, B)
        seg_t = seg(begin + lane)
        same = flag(seg_t == seg(begin + sub * Q - 1))
        ma1_s[...] = jnp.concatenate([same] * 16 + [flag(seg_t == seg(begin + B - 1))] * 2, axis=0).astype(BF16)
        same = flag(seg_t == seg(begin + (sub + 1) * Q))
        ma2_s[...] = jnp.concatenate([same] * 16 + [flag(seg_t == seg(begin))] * 2, axis=0).astype(BF16)
        km_s[...] = flag(seg(begin + sub * Q - 1) == seg(begin - 1))
        for i in range(Q):
            at = begin + sub * Q + i
            keep_s[i] = flag(seg(at) == seg(at - 1))
        seg_c = seg(begin + col)
        mb1_s[...] = flag(seg_c == seg(begin + (col // Q) * Q - 1))
        mb2_s[...] = flag(seg_c == seg(begin + (col // Q + 1) * Q))
        keep_block = flag(seg(begin + B - 1) == seg(begin - 1))

        for k in range(1, nt):
            feature_copy(k, b, lax.rem(t_me - k + nt, nt)).wait_recv()
        fb = feat[rows, :]
        query = dot(fb, proj[0]).astype(BF16)
        signal = dot(fb, proj[1]).astype(BF16)
        q_s[rows, :] = query
        g = query.astype(F32) * up[rows, :].astype(F32)
        signal32 = signal.astype(F32)
        for h in range(H):
            cols = slice(h * 128, h * 128 + 128)
            x_scr[h] = signal32[:, cols]
            g_scr[h] = g[:, cols]
            xb_s[h] = signal[:, cols]
            gb_s[h] = g[:, cols].astype(BF16)
            gm_s[h] = (g[:, cols] * mb1_s[...]).astype(BF16)
        feat_t[b] = fb.T

        for h in range(H):
            head(b, keep_block, h)
        return 0

    def turned(h, which, re, im, kept):
        pr, pi = pstep_s[h, which, 0] * kept, pstep_s[h, which, 1] * kept
        return pr * re - pi * im, pr * im + pi * re

    def end_copy(src, dst, send, recv, slot, to):
        return pltpu.make_async_remote_copy(
            src_ref=src, dst_ref=dst.at[slot], send_sem=send.at[to], recv_sem=recv.at[slot],
            device_id=place(tm=to), device_id_type=MESH,
        )

    def forward_copy(slot, to):
        return end_copy(ue_s, endf_r, ef_s, ef_r, slot, to)

    def backward_copy(slot, to):
        return end_copy(d_s, endb_r, eb_s, eb_r, slot, to)

    def enter(src, _):
        @pl.when(src < z)
        def _():
            forward_copy(src, z).wait_recv()
            kept = flag(seg(src * R - 1) == seg(src * R + R - 1))
            for h in range(H):
                tr, ti = turned(h, 2, ent_s[h, :M, :], ent_s[h, M:, :], kept)
                ent_s[h, :M, :] = endf_r[src, h, :M, :] + tr
                ent_s[h, M:, :] = endf_r[src, h, M:, :] + ti

        return 0


    def weigh(h, re, im):
        wr, wi = w_s[h, 0], w_s[h, 1]
        pad = [jnp.zeros((128 - 2 * M, 128), F32)]
        return jnp.concatenate([wr * re - wi * im, -(wr * im + wi * re)] + pad, axis=0).astype(BF16)

    def enter_block(b, _):
        begin = first + b * B
        rows = rows_at(b * B, B)
        kept = flag(seg(begin + col) == seg(first - 1))
        for h in range(H):
            cols = slice(h * 128, h * 128 + 128)
            er, ei = ent_s[h, :M, :], ent_s[h, M:, :]
            y = y_loc[h, rows, :] + kept * dot(colp_s[h], weigh(h, er, ei))
            mixed_v[rows, cols] = (q_s[rows, cols].astype(F32) * y).astype(BF16)
            gq[rows, cols] = (up[rows, cols].astype(F32) * y).astype(BF16)
            ent_s[h, :M, :], ent_s[h, M:, :] = turned(h, 1, er, ei, 1.0)
        return 0

    def send_states():
        for k in range(1, nt):
            z_copy(k, lax.rem(t_me - k + nt, nt)).wait_recv()
        ends = dot(zbuf[...], proj[1])
        for h in range(H):
            ue_s[h] = ends[h * 16 : h * 16 + 16, h * 128 : h * 128 + 128]

        def go(to, _):
            @pl.when(to > z)
            def _():
                forward_copy(z, to).start()

            return 0

        lax.fori_loop(0, n, go, 0)

    def take_states():
        ent_s[...] = jnp.zeros_like(ent_s)
        lax.fori_loop(0, n, enter, 0)
        e0_s[...] = ent_s[...]
        lax.fori_loop(0, EARLY, enter_block, 0)

    def stream(b, _):
        pl.when(b == 1)(send_states)
        block(b, 0)
        pl.when(b == EARLY)(take_states)

        @pl.when(b >= EARLY)
        def _():
            enter_block(b, 0)

        return 0

    lax.fori_loop(0, nb, stream, 0)

    def reverse_scan(start, store):
        state = start
        for b in reversed(range(nb)):
            begin = first + b * B
            kept = flag(seg(begin) == seg(begin + B))
            following = []
            for h in range(H):
                re, im = state[h]
                if store:
                    g_end[b, h, :M, :], g_end[b, h, M:, :] = re, im
                tr, ti = turned(h, 1, re, im, kept)
                following.append((lead_s[b, h, :M, :] + tr, lead_s[b, h, M:, :] + ti))
            state = following
        return state

    mixed_copy = pltpu.make_async_copy(mixed_v, mixed_out, out_sem.at[0])
    mixed_copy.start()

    quarter = half // 2

    def partner_copy(k, i):
        r = rows_at(k * half + i * quarter, quarter)
        return pltpu.make_async_remote_copy(
            src_ref=dpsnd.at[r], dst_ref=dprcv.at[r], send_sem=dps_s.at[k, i], recv_sem=dps_r.at[k, i],
            device_id=place(dp=1 - core), device_id_type=MESH,
        )

    def transposed(start):
        return jnp.concatenate([feat_t[b, rows_at(start, quarter), :] for b in range(nb)], axis=1)

    def others_part(k, i, other):
        r = rows_at(k * half + i * quarter, quarter)
        dpsnd[r] = (dot(transposed((1 - core) * half + i * quarter), other[...]) * norm).astype(BF16)
        partner_copy(k, i).start()

    def own_part(k, i, other):
        r = rows_at(k * half + i * quarter, quarter)
        pacc[r] = dot(transposed(core * half + i * quarter), other[...]) * norm
        partner_copy(k, i).wait_recv()

        @pl.when(big.no_out)
        def _():
            def go(j, _):
                big.up(k * nch + i * (nch // 2) + j)
                return 0

            lax.fori_loop(0, nch // 2, go, 0)

    others_part(0, 0, gq)
    zero = jnp.zeros((M, 128), F32)
    ends = reverse_scan([(zero, zero)] * H, False)
    for h in range(H):
        d_s[h, :M, :], d_s[h, M:, :] = ends[h]

    def send_adjoint(to, _):
        @pl.when(to < z)
        def _():
            backward_copy(z, to).start()

        return 0

    lax.fori_loop(0, n, send_adjoint, 0)
    lea_s[...] = jnp.zeros_like(lea_s)

    others_part(0, 1, gq)
    own_part(0, 0, gq)
    own_part(0, 1, gq)
    kept_first = flag(seg(first) == seg(first - 1))
    for h in range(H):
        lr, li = turned(h, 0, d_s[h, :M, :], d_s[h, M:, :], kept_first)
        er, ei = e0_s[h, :M, :], e0_s[h, M:, :]
        re, im = [], []
        for m in range(M):
            re.append(jnp.sum(rc_s[h, m], axis=0, keepdims=True))
            im.append(jnp.sum(rc_s[h, M + m], axis=0, keepdims=True))
        re = jnp.concatenate(re, axis=0) + er * lr - ei * li
        im = jnp.concatenate(im, axis=0) + er * li + ei * lr
        for lag in range(Q):
            r = jnp.sum(r_s[h, lag], axis=0, keepdims=True)
            if lag == 0:
                skip_row = r
            re = re + pos_s[h, 0, :, lag : lag + 1] * r
            im = im + pos_s[h, 1, :, lag : lag + 1] * r
        cols = slice(h * 128, h * 128 + 128)
        scale = wgt_s[h] * norm
        terms = jnp.concatenate([re * scale, -im * scale, skip_row * norm, jnp.zeros((15, 128), F32)], axis=0)
        own = rows_at(core * 16, 16)
        mdps[:, cols] = jnp.where(core == 0, terms[16:], terms[:16])
        macc[:, cols] = jnp.where(core == 0, terms[:16], terms[16:])

    small_partner = pltpu.make_async_remote_copy(
        src_ref=mdps, dst_ref=mdpr, send_sem=md_s, recv_sem=md_r, device_id=place(dp=1 - core), device_id_type=MESH
    )
    small_partner.start()

    def leave(i, _):
        src = n - 1 - i

        @pl.when(src > z)
        def _():
            backward_copy(src, z).wait_recv()
            kept = flag(seg(src * R) == seg(src * R + R))
            for h in range(H):
                tr, ti = turned(h, 2, lea_s[h, :M, :], lea_s[h, M:, :], kept)
                lea_s[h, :M, :] = endb_r[src, h, :M, :] + tr
                lea_s[h, M:, :] = endb_r[src, h, M:, :] + ti

        return 0

    lax.fori_loop(0, n, leave, 0)
    reverse_scan([(lea_s[h, :M, :], lea_s[h, M:, :]) for h in range(H)], True)

    def ig_copy(k, b, sender):
        rows = rows_at(b * B, B)
        return pltpu.make_async_remote_copy(
            src_ref=igs.at[k - 1, rows], dst_ref=igr.at[k - 1, rows], send_sem=ig_s.at[k - 1, b],
            recv_sem=ig_r.at[k - 1, b], device_id=place(tensor=lax.rem(t_me + k, nt)), device_id_type=MESH,
        )

    def leave_block(b, _):
        begin = first + b * B
        rows = rows_at(b * B, B)
        kept = flag(seg(begin + col) == seg(begin + B))
        for h in range(H):
            cols = slice(h * 128, h * 128 + 128)
            gr, gi = g_end[b, h, :M, :], g_end[b, h, M:, :]
            gx = gx_loc[h, rows, :] + kept * dot(colh_s[h], weigh(h, gr, gi))
            gv[rows, cols] = gx.astype(BF16)
        for k in range(1, nt):
            to = lax.rem(t_me + k, nt)
            part = rows_at(to * share, share)
            igs[k - 1, rows, :] = (
                dot_nt(gq[rows, :], proj[0, part, :]) + dot_nt(gv[rows, :], proj[1, part, :])
            ).astype(BF16)
            ig_copy(k, b, t_me).start()
        return 0

    def ig_own(b, _):
        rows = rows_at(b * B, B)
        part = rows_at(t_me * share, share)
        iga[rows, :] = dot_nt(gq[rows, :], proj[0, part, :]) + dot_nt(gv[rows, :], proj[1, part, :])
        return 0

    steps = 2 * nch
    def middle_step(s, _=None):
        @pl.when(big.has_out & (s < steps))
        def _():
            big.up(s)

        @pl.when(big.has_out & (s >= LAG))
        def _():
            big.down(s - LAG)

        return 0

    def end_step(s, _):
        @pl.when(big.no_out)
        def _():
            big.down(s)

        return 0

    def ig_rest(b, _):
        rows = rows_at(b * B, B)
        total = iga[rows, :]
        for k in range(1, nt):
            ig_copy(k, b, t_me).wait_recv()
            total = total + igr[k - 1, rows, :].astype(F32)
        gv[rows, :share] = total.astype(BF16)
        return 0

    def finish(s, _):
        big.finish(s)
        return 0

    def pg_copy(k):
        r = pl.ds(k * D, D)
        return pltpu.make_async_copy(tot.at[r], pg_out.at[r], out_sem.at[2 + k])

    work = [functools.partial(lax.fori_loop, b, min(b + 2, nb), leave_block, 0) for b in range(1, nb, 2)]
    work += [functools.partial(others_part, 1, i, gv) for i in range(2)]
    work += [functools.partial(own_part, 1, i, gv) for i in range(2)]
    work += [functools.partial(lax.fori_loop, b, min(b + 3, nb), ig_own, 0) for b in range(0, nb, 3)]
    leave_block(0, 0)
    for s, item in enumerate(work):
        middle_step(s)
        item()
    lax.fori_loop(len(work), steps - 2, middle_step, 0)
    small_partner.wait_recv()
    pl.when(small.no_out)(lambda: small.up(0))
    lax.fori_loop(0, nch, end_step, 0)
    lax.fori_loop(0, nch // GROUP, finish, 0)
    pg_copy(0).start()
    pl.when(small.has_out)(lambda: small.up(0))
    lax.fori_loop(steps - 2, steps, middle_step, 0)
    small.down(0)
    lax.fori_loop(0, nb, ig_rest, 0)
    ig_out_copy = pltpu.make_async_copy(gv.at[:, :share], ig_out, out_sem.at[1])
    ig_out_copy.start()
    lax.fori_loop(steps, steps + LAG, middle_step, 0)
    lax.fori_loop(nch, steps, end_step, 0)
    small.finish(0)
    res_copy = pltpu.make_async_copy(mtot.at[pl.ds(0, 2 * M)], res_out, out_sem.at[4])
    skip_copy = pltpu.make_async_copy(mtot.at[pl.ds(2 * M, 8)], skip_out, out_sem.at[5])
    res_copy.start()
    skip_copy.start()
    lax.fori_loop(nch // GROUP, steps // GROUP, finish, 0)
    pg_copy(1).start()

    for b in range(nb):
        for k in range(1, nt):
            feature_copy(k, b, t_me).wait_send()
            ig_copy(k, b, t_me).wait_send()
    for k in range(1, nt):
        pole_copy(k).wait_send()
        z_copy(k, t_me).wait_send()
    for k in range(2):
        for i in range(2):
            partner_copy(k, i).wait_send()
    small_partner.wait_send()

    def sent(to, _):
        @pl.when(to > z)
        def _():
            forward_copy(z, to).wait_send()

        @pl.when(to < z)
        def _():
            backward_copy(z, to).wait_send()

        return 0

    lax.fori_loop(0, n, sent, 0)
    mixed_copy.wait()
    ig_out_copy.wait()
    pg_copy(0).wait()
    pg_copy(1).wait()
    res_copy.wait()
    skip_copy.wait()


def assemble_kernel(mixed, ig, pg, res, skips, mixed_o, ig_o, pg_o, res_o, skip_o, wide, sems):
    parts, rows = wide.shape[:2]
    stores = [pltpu.make_async_copy(wide.at[i], pg_o.at[pl.ds(i * rows, rows)], sems.at[i]) for i in range(parts)]
    for i, (src, dst) in enumerate(((mixed, mixed_o), (ig, ig_o), (res, res_o), (skips.at[pl.ds(0, 1)], skip_o))):
        stores.append(pltpu.make_async_copy(src, dst, sems.at[parts + i]))
        stores[-1].start()
    for i in range(parts):
        wide[i] = pg[pl.ds(i * rows, rows), :].astype(F32)
        stores[i].start()
    for copy in stores:
        copy.wait()


def shards(frames_in, in_proj, log_rates, angles, residues, skip_gain, lengths, grad_out):
    R, C = frames_in.shape[1:]
    D = in_proj.shape[1]
    M, H = log_rates.shape
    clips = lengths.shape[1]
    n, nt = lax.axis_size("tm"), lax.axis_size("tensor")
    nb = R // B
    norm = 1.0 / math.sqrt(R * n * lax.axis_size("dp"))
    half = D // 2
    nch = half // STEP
    share = D // nt
    resid = residues.reshape(2, M, H, 128).transpose(0, 2, 1, 3)
    skip = skip_gain.reshape(H, 1, 128)
    vm, dma = pltpu.VMEM, pltpu.SemaphoreType.DMA

    def chain_sems(steps, group):
        return [dma((steps,))] * 5 + [dma((steps // group,))] * 2

    scratch = [
        vm((R, D), BF16), vm((nb, D, B), BF16), vm((2, D, C), BF16), vm((R, C), BF16), vm((R, C), BF16),
        vm((H, B, 128), F32), vm((H, B, 128), F32), vm((H, B, 128), F32), vm((H, B, 128), F32),
        vm((H, B, 128), BF16), vm((H, B, 128), BF16), vm((H, B, 128), BF16),
        vm((H, R, 128), F32), vm((H, R, 128), F32), vm((R, C), BF16), vm((R, C), BF16), vm((R, C), BF16),
        vm((H, 144, 128), BF16), vm((H, 144, 128), BF16), vm((H, 128, 128), BF16), vm((H, 128, 128), BF16),
        vm((H, 128, 128), BF16), vm((H, 128, 128), BF16), vm((H, 128, 128), BF16),
        vm((H, 2, 8 * M, 128), F32), vm((H, 2, M, 128), F32), vm((H, 3, 2, M, 128), F32), vm((H, 2, M, 128), F32),
        vm((H, Q, 8, 128), F32), vm((H, M, 128), F32),
        vm((144, 128), BF16), vm((144, 128), BF16), vm((Q, 8, 128), F32), vm((8, 128), F32), vm((B, 128), F32),
        vm((B, 128), F32),
        vm((H, 2 * M, 128), F32), vm((H, 2 * M, 128), F32), vm((nb, H, 2 * M, 128), F32), vm((nb, H, 2 * M, 128), F32),
        vm((H, Q, 8, 128), F32), vm((H, 2 * M, 8, 128), F32), vm((H, 2 * M, 128), F32), vm((H, 2 * M, 128), F32),
        vm((n, H, 2 * M, 128), F32), vm((n, H, 2 * M, 128), F32),
        vm((2 * half, C), F32), vm((2 * half, C), BF16), vm((2 * half, C), BF16), vm((2 * half, C), BF16),
        vm((2 * half, C), BF16), vm((2 * half, C), BF16), vm((2 * D, C), BF16),
        vm((16, C), F32), vm((16, C), F32), vm((16, C), F32), vm((16, C), F32), vm((16, C), F32), vm((16, C), F32),
        vm((32, C), F32),
        vm((nt - 1, R, share), BF16), vm((nt - 1, R, share), BF16), vm((R, share), F32),
        vm((16, 128), F32), vm((nt - 1, 16, 128), F32), vm((16 * H, R), BF16), vm((nt - 1, 16 * H, C), BF16),
        vm((16 * H, D), BF16), vm((H, 2 * M, 128), F32), vm((H, 2 * M, 128), F32),
        dma((nt - 1,)), dma((nt - 1,)), dma((nt - 1,)), dma((nt - 1,)),
        dma((3,)), dma((nt - 1, nb)), dma((nt - 1, nb)), dma((n,)), dma((n,)), dma((n,)), dma((n,)),
        dma((2, 2)), dma((2, 2)), dma((nt - 1, nb)), dma((nt - 1, nb)), dma, dma, dma((6,)),
    ] + chain_sems(2 * nch, GROUP) + chain_sems(1, 1)
    vmem = pl.BlockSpec(memory_space=pltpu.VMEM)
    anywhere = pl.BlockSpec(memory_space=pl.ANY)
    mixed, ig, pg, res, skips = pl.pallas_call(
        functools.partial(layer_kernel, (clips, M, H, R, C, D, norm)),
        out_shape=[
            vm((R, C), BF16), vm((R, share), BF16), vm((2 * D, C), BF16), vm((2 * M, C), F32), vm((8, C), F32),
        ],
        in_specs=[pl.BlockSpec(memory_space=pltpu.SMEM)] + [vmem] * 4 + [anywhere] * 3,
        out_specs=[vmem] * 5,
        scratch_shapes=scratch,
        compiler_params=pltpu.CompilerParams(
            collective_id=0, has_side_effects=True, vmem_limit_bytes=56 << 20
        ),
        name="layer",
    )(lengths, log_rates.T, angles.T, resid, skip, frames_in[0], in_proj, grad_out[0])
    parts = 8
    mixed, ig, pg, res, skips = pl.pallas_call(
        assemble_kernel,
        out_shape=[
            jax.ShapeDtypeStruct((R, C), BF16), jax.ShapeDtypeStruct((R, share), BF16),
            jax.ShapeDtypeStruct((2 * D, C), F32), jax.ShapeDtypeStruct((2 * M, C), F32),
            jax.ShapeDtypeStruct((1, C), F32),
        ],
        in_specs=[vmem] * 5,
        out_specs=[anywhere] * 5,
        scratch_shapes=[vm((parts, 2 * D // parts, C), F32), dma((parts + 4,))],
        compiler_params=pltpu.CompilerParams(vmem_limit_bytes=20 << 20),
        name="assemble",
    )(mixed, ig, pg, res, skips)
    return mixed[None], ig[None], pg.reshape(2, D, C), res.reshape(2, M, C), skips[0]


def solution(mesh):
    in_specs = (
        P(("group", "dp"), "tm", "tensor"),
        P(None, None, "tensor"),
        P(None, "tensor"),
        P(None, "tensor"),
        P(None, None, "tensor"),
        P("tensor"),
        P(("group", "dp"), None),
        P(("group", "dp"), "tm", "tensor"),
    )
    out_specs = (
        P(("group", "dp"), "tm", "tensor"),
        P(("group", "dp"), "tm", "tensor"),
        P("group", None, "tensor"),
        P("group", None, "tensor"),
        P(("group", "tensor")),
    )
    return jax.shard_map(shards, mesh=mesh, in_specs=in_specs, out_specs=out_specs, check_vma=False)
```

```python
import functools
import math

import jax
import jax.numpy as jnp
from jax import lax
from jax.experimental import pallas as pl
from jax.experimental.pallas import tpu as pltpu
from jax.sharding import PartitionSpec as P

F32 = jnp.float32
BF16 = jnp.bfloat16
AXES = ("group", "tm", "tensor", "dp")
MESH = pl.DeviceIdType.MESH
Q = 16
B = 128
LAG = 2
GROUP = 4
EARLY = 2
STEP = 64


def dot(a, b):
    return jnp.dot(a, b, preferred_element_type=F32)


def dot_nt(a, b):
    return lax.dot_general(a, b, (((1,), (1,)), ((), ())), preferred_element_type=F32)


def flag(cond):
    return jnp.where(cond, 1.0, 0.0).astype(F32)


def rows_at(start, size, step=8):
    return pl.ds(pl.multiple_of(start, step), size)


class Place:
    def __init__(self):
        self.at = {axis: lax.axis_index(axis) for axis in AXES}

    def __call__(self, **moved):
        return tuple(moved.get(axis, self.at[axis]) for axis in AXES)


class Chain:
    def __init__(self, place, acc, also, snd, upb, inb, tot, sems, nch, size, half, tot_rows, group, core):
        n, z = lax.axis_size("tm"), place.at["tm"]
        left = z < n // 2
        self.inward = place(tm=jnp.where(left, z + 1, z - 1))
        self.outward = place(tm=jnp.clip(jnp.where(left, z - 1, z + 1), 0, n - 1))
        self.partner = place(dp=1 - core)
        depth = jnp.where(left, n // 2 - 1 - z, z - n // 2)
        self.root = depth == 0
        self.inner = depth > 0
        self.has_out = depth < n // 2 - 1
        self.no_out = depth == n // 2 - 1
        self.acc, self.also, self.snd, self.upb, self.inb, self.tot = acc, also, snd, upb, inb, tot
        (self.up_s, self.up_r, self.in_r, self.to_s, self.tot_r, self.dp_s, self.dp_r) = sems
        self.nch, self.size, self.half, self.tot_rows, self.group, self.core = nch, size, half, tot_rows, group, core
        self.wire = snd.dtype

    def row(self, s):
        return rows_at(s * self.size, self.size)

    def total_row(self, s, core, count=1):
        r = (s // self.nch) * self.tot_rows + core * self.half + (s % self.nch) * self.size
        return rows_at(r, self.size * count)

    def copy(self, src, dst, send, recv, to):
        return pltpu.make_async_remote_copy(
            src_ref=src, dst_ref=dst, send_sem=send, recv_sem=recv, device_id=to, device_id_type=MESH
        )

    def up_copy(self, s):
        r = self.row(s)
        return self.copy(self.snd.at[r], self.upb.at[r], self.up_s.at[s], self.up_r.at[s], self.inward)

    def in_copy(self, s):
        r = self.row(s)
        return self.copy(self.snd.at[r], self.inb.at[r], self.up_s.at[s], self.in_r.at[s], self.inward)

    def out_copy(self, s):
        r = self.total_row(s, self.core)
        return self.copy(self.tot.at[r], self.tot.at[r], self.to_s.at[s], self.tot_r.at[s], self.outward)

    def dp_copy(self, g, core):
        r = self.total_row(g * self.group, core, self.group)
        return self.copy(self.tot.at[r], self.tot.at[r], self.dp_s.at[g], self.dp_r.at[g], self.partner)

    def up(self, s):
        r = self.row(s)

        @pl.when(self.no_out)
        def _():
            self.snd[r] = (self.acc[r] + self.also[r].astype(F32)).astype(self.wire)

        @pl.when(self.has_out)
        def _():
            self.up_copy(s).wait_recv()
            self.snd[r] = (self.acc[r] + self.also[r].astype(F32) + self.upb[r].astype(F32)).astype(self.wire)

        @pl.when(self.inner)
        def _():
            self.up_copy(s).start()

        @pl.when(self.root)
        def _():
            self.in_copy(s).start()

    def down(self, s):
        @pl.when(self.root)
        def _():
            r = self.row(s)
            self.in_copy(s).wait_recv()
            self.tot[self.total_row(s, self.core)] = (self.snd[r].astype(F32) + self.inb[r].astype(F32)).astype(self.wire)

        @pl.when(self.inner)
        def _():
            self.out_copy(s).wait_recv()

        @pl.when(self.has_out)
        def _():
            self.out_copy(s).start()

        @pl.when(s % self.group == self.group - 1)
        def _():
            self.dp_copy(s // self.group, self.core).start()

    def finish(self, g):
        self.dp_copy(g, self.core).wait_send()
        self.dp_copy(g, 1 - self.core).wait_recv()
        for i in range(self.group):
            s = g * self.group + i

            @pl.when(self.has_out)
            def _():
                self.out_copy(s).wait_send()

            self.up_copy(s).wait_send()


def layer_kernel(
    cfg,
    lens_ref, rates_ref, angles_ref, resid_ref, skip_ref, frames_ref, proj_ref, up_hbm,
    mixed_out, ig_out, pg_out, res_out, skip_out,
    feat, feat_t, proj, up, q_s, x_scr, g_scr, y_scr, gx_scr, xb_s, gb_s, gm_s, y_loc, gx_loc, gq, gv, mixed_v,
    a1_s, a2_s, bt_s, b1_s, b2_s, colp_s, colh_s, pk_s, pos_s, pstep_s, w_s, k_s, wgt_s,
    ma1_s, ma2_s, keep_s, km_s, mb1_s, mb2_s,
    u_s, d_s, lead_s, g_end, r_s, rc_s, ent_s, lea_s, endf_r, endb_r,
    pacc, psnd, dpsnd, dprcv, upb, inb, tot, macc, msnd, mdps, mdpr, mupb, minb, mtot, igs, igr, iga,
    poles_mine, poles_r, reach_s, zsnd, zbuf, ue_s, e0_s, p_s, p_r, z_s, z_r,
    loc_sem, f_s, f_r, ef_s, ef_r, eb_s, eb_r, dps_s, dps_r, ig_s, ig_r, md_s, md_r, out_sem, pg_sem,
    *chain_sems,
):
    clips, M, H, R, C, D, norm = cfg
    nb = R // B
    place = Place()
    n, z = lax.axis_size("tm"), place.at["tm"]
    nt, t_me = lax.axis_size("tensor"), place.at["tensor"]
    core = place.at["dp"]
    first = z * R
    share = D // nt
    half = D // 2
    big_sems, small_sems = chain_sems[:7], chain_sems[7:]
    nch = half // STEP
    big = Chain(place, pacc, dprcv, psnd, upb, inb, tot, big_sems, nch, STEP, half, D, GROUP, core)
    small = Chain(place, macc, mdpr, msnd, mupb, minb, mtot, small_sems, 1, 16, 16, 32, 1, core)

    clip_starts = [jnp.int32(0)]
    for k in range(clips - 1):
        clip_starts.append(clip_starts[-1] + lens_ref[0, k])

    def seg(frame):
        total = jnp.where(frame >= clip_starts[0], 1, 0)
        for k in range(1, clips):
            total = total + jnp.where(frame >= clip_starts[k], 1, 0)
        return total

    mine = pl.ds(pl.multiple_of(t_me * C, 128), C)
    own_in = pltpu.make_async_copy(frames_ref, feat.at[:, mine], loc_sem.at[0])
    proj_in = pltpu.make_async_copy(proj_ref, proj, loc_sem.at[1])
    up_in = pltpu.make_async_copy(up_hbm, up, loc_sem.at[2])
    own_in.start()
    proj_in.start()
    up_in.start()

    barrier = pltpu.get_barrier_semaphore()
    for k in range(1, nt):
        pl.semaphore_signal(barrier, inc=1, device_id=place(tensor=lax.rem(t_me + k, nt)), device_id_type=MESH)
    pl.semaphore_signal(barrier, inc=1, device_id=place(dp=1 - core), device_id_type=MESH)
    for k in range(1, n):
        pl.semaphore_signal(barrier, inc=1, device_id=place(tm=lax.rem(z + k, n)), device_id_type=MESH)
    pl.semaphore_wait(barrier, nt + n - 1)

    def feature_copy(k, b, sender):
        rows = rows_at(b * B, B)
        cols = pl.ds(pl.multiple_of(sender * C, 128), C)
        return pltpu.make_async_remote_copy(
            src_ref=frames_ref.at[rows], dst_ref=feat.at[rows, cols], send_sem=f_s.at[k - 1, b],
            recv_sem=f_r.at[k - 1, b], device_id=place(tensor=lax.rem(t_me + k, nt)), device_id_type=MESH,
        )

    def pole_copy(k):
        return pltpu.make_async_remote_copy(
            src_ref=poles_mine, dst_ref=poles_r.at[k - 1], send_sem=p_s.at[k - 1], recv_sem=p_r.at[k - 1],
            device_id=place(tensor=lax.rem(t_me + k, nt)), device_id_type=MESH,
        )

    def z_copy(k, sender):
        cols = pl.ds(pl.multiple_of(sender * C, 128), C)
        return pltpu.make_async_remote_copy(
            src_ref=zsnd.at[k - 1], dst_ref=zbuf.at[:, cols], send_sem=z_s.at[k - 1], recv_sem=z_r.at[k - 1],
            device_id=place(tensor=lax.rem(t_me + k, nt)), device_id_type=MESH,
        )

    poles_mine[...] = jnp.zeros_like(poles_mine)
    poles_mine[:H, :M] = rates_ref[...]
    poles_mine[8 : 8 + H, :M] = angles_ref[...]
    for k in range(1, nt):
        pole_copy(k).start()
    for b in range(min(2, nb)):
        for k in range(1, nt):
            feature_copy(k, b, t_me).start()

    lane = lax.broadcasted_iota(jnp.int32, (8, 128), 1)
    sub = lax.broadcasted_iota(jnp.int32, (8, 128), 0)
    lanef = lane.astype(F32)
    in_chunk = lane % Q
    chunk = lane // Q
    square = lax.broadcasted_iota(jnp.int32, (M, M), 0) == lax.broadcasted_iota(jnp.int32, (M, M), 1)

    def upright(rates, turns):
        d = jnp.exp(jnp.sum(jnp.where(square, rates, 0.0), axis=1, keepdims=True))
        return d, jnp.sum(jnp.where(square, turns, 0.0), axis=1, keepdims=True)

    def powers_of(lag, d, a):
        size = jnp.exp(-d * lag)
        return size * jnp.cos(a * lag), size * jnp.sin(a * lag)

    def reach(ref):
        def one(h, _):
            d, a = upright(ref[pl.ds(h, 1), :][:, :M], ref[pl.ds(8 + h, 1), :][:, :M])
            re, im = powers_of(127.0 - lanef, d, a)
            step_re, step_im = powers_of(jnp.full((M, 128), float(B), F32), d, a)
            for b in reversed(range(nb)):
                kept = flag(seg(first + b * B + lane) == seg(first + R - 1))
                reach_s[rows_at(h * 16, 16, 16), b * B : b * B + B] = jnp.concatenate(
                    [re * kept, im * kept], axis=0
                ).astype(BF16)
                re, im = step_re * re - step_im * im, step_re * im + step_im * re
            return 0

        lax.fori_loop(0, H, one, 0)
        return dot(reach_s[...], feat[:, mine]).astype(BF16)

    own_in.wait()
    zbuf[:, mine] = reach(poles_mine)
    for k in range(1, nt):
        pole_copy(nt - k).wait_recv()
        zsnd[k - 1] = reach(poles_r.at[nt - k - 1])
        z_copy(k, t_me).start()
    for b in range(min(2, nb), nb):
        for k in range(1, nt):
            feature_copy(k, b, t_me).start()

    def tables(h, _):
        d, a = upright(rates_ref[pl.ds(h, 1), :], angles_ref[pl.ds(h, 1), :])

        def powers(lag, dd=d, aa=a):
            return powers_of(lag, dd, aa)

        pos_re, pos_im = powers(lanef)
        nxt_re, nxt_im = powers(lanef + 1.0)
        neg_re, neg_im = powers(-lanef - 1.0)
        end_re, end_im = powers(127.0 - lanef)
        far_re, far_im = powers(128.0 - lanef)
        b1_re, b1_im = powers((in_chunk + 1).astype(F32))
        b2_re, b2_im = powers((Q - in_chunk).astype(F32))
        pos_s[h, 0], pos_s[h, 1] = pos_re, pos_im
        for i, lag in enumerate((1.0, float(B), float(R))):
            pr, pi = powers(jnp.full((M, 128), lag, F32))
            pstep_s[h, i, 0], pstep_s[h, i, 1] = pr, pi
        y = 2.0 * d
        series = y * (1.0 - y / 2 * (1.0 - y / 3 * (1.0 - y / 4 * (1.0 - y / 5 * (1.0 - y / 6 * (1.0 - y / 7))))))
        wgt = jnp.sqrt(jnp.where(y < 0.25, series, 1.0 - jnp.exp(-y)))
        wgt = jnp.broadcast_to(wgt, (M, 128))
        wgt_s[h] = wgt
        wr, wi = resid_ref[0, h] * wgt, resid_ref[1, h] * wgt
        w_s[h, 0], w_s[h, 1] = wr, wi
        for k in range(Q):
            tap = jnp.sum(wr * pos_re[:, k : k + 1] - wi * pos_im[:, k : k + 1], axis=0, keepdims=True)
            if k == 0:
                tap = tap + skip_ref[h]
            k_s[h, k] = jnp.broadcast_to(tap, (8, 128))
        a1r, a1i, a2r, a2i, btr, bti, b2r, b2i = [], [], [], [], [], [], [], []
        subf = sub.astype(F32) * Q
        for m in range(M):
            one = slice(m, m + 1)
            pr, pi = powers(subf, d[one], a[one])
            pk_s[h, 0, m * 8 : m * 8 + 8], pk_s[h, 1, m * 8 : m * 8 + 8] = pr, pi
            back_re, back_im = powers(-subf - float(Q), d[one], a[one])
            fr, fi = neg_re[one], neg_im[one]
            past = lane < sub * Q
            a1r.append(jnp.where(past, pr * fr - pi * fi, 0.0))
            a1i.append(jnp.where(past, pr * fi + pi * fr, 0.0))
            fr, fi = pos_re[one], pos_im[one]
            later = lane >= (sub + 1) * Q
            a2r.append(jnp.where(later, back_re * fr - back_im * fi, 0.0))
            a2i.append(jnp.where(later, back_re * fi + back_im * fr, 0.0))
            here = chunk == sub
            btr.append(jnp.where(here, b1_re[one], 0.0))
            bti.append(jnp.where(here, b1_im[one], 0.0))
            b2r.append(jnp.where(here, b2_re[one], 0.0))
            b2i.append(jnp.where(here, b2_im[one], 0.0))
        a1_s[h] = jnp.concatenate(a1r + a1i + [end_re, end_im], axis=0).astype(BF16)
        a2_s[h] = jnp.concatenate(a2r + a2i + [pos_re, pos_im], axis=0).astype(BF16)
        bt = jnp.concatenate(btr + bti, axis=0)
        bt_s[h] = bt.astype(BF16)
        b1_s[h] = bt.T.astype(BF16)
        b2_s[h] = jnp.concatenate(b2r + b2i, axis=0).T.astype(BF16)
        pad = [jnp.zeros((128 - 2 * M, 128), F32)]
        colp_s[h] = jnp.concatenate([nxt_re, nxt_im] + pad, axis=0).T.astype(BF16)
        colh_s[h] = jnp.concatenate([far_re, far_im] + pad, axis=0).T.astype(BF16)
        return 0

    lax.fori_loop(0, H, tables, 0)
    u_s[...] = jnp.zeros_like(u_s)
    r_s[...] = jnp.zeros_like(r_s)
    rc_s[...] = jnp.zeros_like(rc_s)
    proj_in.wait()
    up_in.wait()

    def head(b, keep_block, h):
        rows = rows_at(b * B, B)
        xs = [x_scr[h, pl.ds(i, 8, stride=Q), :] for i in range(Q)]
        gs = [g_scr[h, pl.ds(i, 8, stride=Q), :] for i in range(Q)]
        held, corr = [], [None] * Q
        for i in range(Q):
            if i:
                kept = keep_s[i]
                held = [v * kept for v in held]
            held.append(xs[i])
            acc = None
            for s in range(i + 1):
                lag = i - s
                term = k_s[h, lag] * held[s]
                acc = term if acc is None else acc + term
                both = gs[i] * held[s]
                corr[lag] = both if corr[lag] is None else corr[lag] + both
            y_scr[h, pl.ds(i, 8, stride=Q), :] = acc
        for lag in range(Q):
            r_s[h, lag] += corr[lag]
        held = []
        for s in reversed(range(Q)):
            if s < Q - 1:
                kept = keep_s[s + 1]
                held = [v * kept for v in held]
            held = [gs[s]] + held
            acc = None
            for lag in range(Q - s):
                term = k_s[h, lag] * held[lag]
                acc = term if acc is None else acc + term
            gx_scr[h, pl.ds(s, 8, stride=Q), :] = acc

        states = dot(a1_s[h] * ma1_s[...], xb_s[h])
        leads = dot(bt_s[h], gm_s[h])
        adj = dot(a2_s[h] * ma2_s[...], gb_s[h])
        kept = km_s[...]
        vr, vi, ar, ai = [], [], [], []
        for m in range(M):
            re, im = slice(m * 8, m * 8 + 8), slice(64 + m * 8, 72 + m * 8)
            pr, pi = pk_s[h, 0, re] * kept, pk_s[h, 1, re] * kept
            ur, ui = u_s[h, m : m + 1, :], u_s[h, M + m : M + m + 1, :]
            sr = states[re] + (pr * ur - pi * ui)
            si = states[im] + (pr * ui + pi * ur)
            lr, li = leads[re], leads[im]
            rc_s[h, m] += sr * lr - si * li
            rc_s[h, M + m] += sr * li + si * lr
            wr, wi = w_s[h, 0, m : m + 1, :], w_s[h, 1, m : m + 1, :]
            vr.append(wr * sr - wi * si)
            vi.append(-(wr * si + wi * sr))
            ar.append(wr * adj[re] - wi * adj[im])
            ai.append(-(wr * adj[im] + wi * adj[re]))
        v = jnp.concatenate(vr + vi, axis=0).astype(BF16)
        y_loc[h, rows, :] = y_scr[h] + mb1_s[...] * dot(b1_s[h], v)
        v = jnp.concatenate(ar + ai, axis=0).astype(BF16)
        gx_loc[h, rows, :] = gx_scr[h] + mb2_s[...] * dot(b2_s[h], v)
        lead_s[b, h] = adj[128:]
        pr, pi = pstep_s[h, 1, 0] * keep_block, pstep_s[h, 1, 1] * keep_block
        ur, ui = u_s[h, :M, :], u_s[h, M:, :]
        u_s[h, :M, :] = states[128 : 128 + M] + (pr * ur - pi * ui)
        u_s[h, M:, :] = states[128 + M :] + (pr * ui + pi * ur)

    col = lax.broadcasted_iota(jnp.int32, (B, 128), 0)

    def block(b, _):
        begin = first + b * B
        rows = rows_at(b * B, B)
        seg_t = seg(begin + lane)
        same = flag(seg_t == seg(begin + sub * Q - 1))
        ma1_s[...] = jnp.concatenate([same] * 16 + [flag(seg_t == seg(begin + B - 1))] * 2, axis=0).astype(BF16)
        same = flag(seg_t == seg(begin + (sub + 1) * Q))
        ma2_s[...] = jnp.concatenate([same] * 16 + [flag(seg_t == seg(begin))] * 2, axis=0).astype(BF16)
        km_s[...] = flag(seg(begin + sub * Q - 1) == seg(begin - 1))
        for i in range(Q):
            at = begin + sub * Q + i
            keep_s[i] = flag(seg(at) == seg(at - 1))
        seg_c = seg(begin + col)
        mb1_s[...] = flag(seg_c == seg(begin + (col // Q) * Q - 1))
        mb2_s[...] = flag(seg_c == seg(begin + (col // Q + 1) * Q))
        keep_block = flag(seg(begin + B - 1) == seg(begin - 1))

        for k in range(1, nt):
            feature_copy(k, b, lax.rem(t_me - k + nt, nt)).wait_recv()
        fb = feat[rows, :]
        query = dot(fb, proj[0]).astype(BF16)
        signal = dot(fb, proj[1]).astype(BF16)
        q_s[rows, :] = query
        g = query.astype(F32) * up[rows, :].astype(F32)
        signal32 = signal.astype(F32)
        for h in range(H):
            cols = slice(h * 128, h * 128 + 128)
            x_scr[h] = signal32[:, cols]
            g_scr[h] = g[:, cols]
            xb_s[h] = signal[:, cols]
            gb_s[h] = g[:, cols].astype(BF16)
            gm_s[h] = (g[:, cols] * mb1_s[...]).astype(BF16)
        feat_t[b] = fb.T

        for h in range(H):
            head(b, keep_block, h)
        return 0

    def turned(h, which, re, im, kept):
        pr, pi = pstep_s[h, which, 0] * kept, pstep_s[h, which, 1] * kept
        return pr * re - pi * im, pr * im + pi * re

    def end_copy(src, dst, send, recv, slot, to):
        return pltpu.make_async_remote_copy(
            src_ref=src, dst_ref=dst.at[slot], send_sem=send.at[to], recv_sem=recv.at[slot],
            device_id=place(tm=to), device_id_type=MESH,
        )

    def forward_copy(slot, to):
        return end_copy(ue_s, endf_r, ef_s, ef_r, slot, to)

    def backward_copy(slot, to):
        return end_copy(d_s, endb_r, eb_s, eb_r, slot, to)

    def enter(src, _):
        @pl.when(src < z)
        def _():
            forward_copy(src, z).wait_recv()
            kept = flag(seg(src * R - 1) == seg(src * R + R - 1))
            for h in range(H):
                tr, ti = turned(h, 2, ent_s[h, :M, :], ent_s[h, M:, :], kept)
                ent_s[h, :M, :] = endf_r[src, h, :M, :] + tr
                ent_s[h, M:, :] = endf_r[src, h, M:, :] + ti

        return 0


    def weigh(h, re, im):
        wr, wi = w_s[h, 0], w_s[h, 1]
        pad = [jnp.zeros((128 - 2 * M, 128), F32)]
        return jnp.concatenate([wr * re - wi * im, -(wr * im + wi * re)] + pad, axis=0).astype(BF16)

    def enter_block(b, _):
        begin = first + b * B
        rows = rows_at(b * B, B)
        kept = flag(seg(begin + col) == seg(first - 1))
        for h in range(H):
            cols = slice(h * 128, h * 128 + 128)
            er, ei = ent_s[h, :M, :], ent_s[h, M:, :]
            y = y_loc[h, rows, :] + kept * dot(colp_s[h], weigh(h, er, ei))
            mixed_v[rows, cols] = (q_s[rows, cols].astype(F32) * y).astype(BF16)
            gq[rows, cols] = (up[rows, cols].astype(F32) * y).astype(BF16)
            ent_s[h, :M, :], ent_s[h, M:, :] = turned(h, 1, er, ei, 1.0)
        return 0

    def send_states():
        for k in range(1, nt):
            z_copy(k, lax.rem(t_me - k + nt, nt)).wait_recv()
        ends = dot(zbuf[...], proj[1])
        for h in range(H):
            ue_s[h] = ends[h * 16 : h * 16 + 16, h * 128 : h * 128 + 128]

        def go(to, _):
            @pl.when(to > z)
            def _():
                forward_copy(z, to).start()

            return 0

        lax.fori_loop(0, n, go, 0)

    def take_states():
        ent_s[...] = jnp.zeros_like(ent_s)
        lax.fori_loop(0, n, enter, 0)
        e0_s[...] = ent_s[...]
        lax.fori_loop(0, EARLY, enter_block, 0)

    def stream(b, _):
        pl.when(b == 1)(send_states)
        block(b, 0)
        pl.when(b == EARLY)(take_states)

        @pl.when(b >= EARLY)
        def _():
            enter_block(b, 0)

        return 0

    lax.fori_loop(0, nb, stream, 0)

    def reverse_scan(start, store):
        state = start
        for b in reversed(range(nb)):
            begin = first + b * B
            kept = flag(seg(begin) == seg(begin + B))
            following = []
            for h in range(H):
                re, im = state[h]
                if store:
                    g_end[b, h, :M, :], g_end[b, h, M:, :] = re, im
                tr, ti = turned(h, 1, re, im, kept)
                following.append((lead_s[b, h, :M, :] + tr, lead_s[b, h, M:, :] + ti))
            state = following
        return state

    mixed_copy = pltpu.make_async_copy(mixed_v, mixed_out, out_sem.at[0])
    mixed_copy.start()

    quarter = half // 2

    def partner_copy(k, i):
        r = rows_at(k * half + i * quarter, quarter)
        return pltpu.make_async_remote_copy(
            src_ref=dpsnd.at[r], dst_ref=dprcv.at[r], send_sem=dps_s.at[k, i], recv_sem=dps_r.at[k, i],
            device_id=place(dp=1 - core), device_id_type=MESH,
        )

    def transposed(start):
        return jnp.concatenate([feat_t[b, rows_at(start, quarter), :] for b in range(nb)], axis=1)

    def others_part(k, i, other):
        r = rows_at(k * half + i * quarter, quarter)
        dpsnd[r] = (dot(transposed((1 - core) * half + i * quarter), other[...]) * norm).astype(BF16)
        partner_copy(k, i).start()

    def own_part(k, i, other):
        r = rows_at(k * half + i * quarter, quarter)
        pacc[r] = dot(transposed(core * half + i * quarter), other[...]) * norm
        partner_copy(k, i).wait_recv()

        @pl.when(big.no_out)
        def _():
            def go(j, _):
                big.up(k * nch + i * (nch // 2) + j)
                return 0

            lax.fori_loop(0, nch // 2, go, 0)

    others_part(0, 0, gq)
    others_part(0, 1, gq)
    own_part(0, 0, gq)
    zero = jnp.zeros((M, 128), F32)
    ends = reverse_scan([(zero, zero)] * H, False)
    for h in range(H):
        d_s[h, :M, :], d_s[h, M:, :] = ends[h]

    def send_adjoint(to, _):
        @pl.when(to < z)
        def _():
            backward_copy(z, to).start()

        return 0

    lax.fori_loop(0, n, send_adjoint, 0)
    lea_s[...] = jnp.zeros_like(lea_s)

    own_part(0, 1, gq)
    kept_first = flag(seg(first) == seg(first - 1))
    for h in range(H):
        lr, li = turned(h, 0, d_s[h, :M, :], d_s[h, M:, :], kept_first)
        er, ei = e0_s[h, :M, :], e0_s[h, M:, :]
        re, im = [], []
        for m in range(M):
            re.append(jnp.sum(rc_s[h, m], axis=0, keepdims=True))
            im.append(jnp.sum(rc_s[h, M + m], axis=0, keepdims=True))
        re = jnp.concatenate(re, axis=0) + er * lr - ei * li
        im = jnp.concatenate(im, axis=0) + er * li + ei * lr
        for lag in range(Q):
            r = jnp.sum(r_s[h, lag], axis=0, keepdims=True)
            if lag == 0:
                skip_row = r
            re = re + pos_s[h, 0, :, lag : lag + 1] * r
            im = im + pos_s[h, 1, :, lag : lag + 1] * r
        cols = slice(h * 128, h * 128 + 128)
        scale = wgt_s[h] * norm
        terms = jnp.concatenate([re * scale, -im * scale, skip_row * norm, jnp.zeros((15, 128), F32)], axis=0)
        own = rows_at(core * 16, 16)
        mdps[:, cols] = jnp.where(core == 0, terms[16:], terms[:16])
        macc[:, cols] = jnp.where(core == 0, terms[:16], terms[16:])

    small_partner = pltpu.make_async_remote_copy(
        src_ref=mdps, dst_ref=mdpr, send_sem=md_s, recv_sem=md_r, device_id=place(dp=1 - core), device_id_type=MESH
    )
    small_partner.start()

    def leave(i, _):
        src = n - 1 - i

        @pl.when(src > z)
        def _():
            backward_copy(src, z).wait_recv()
            kept = flag(seg(src * R) == seg(src * R + R))
            for h in range(H):
                tr, ti = turned(h, 2, lea_s[h, :M, :], lea_s[h, M:, :], kept)
                lea_s[h, :M, :] = endb_r[src, h, :M, :] + tr
                lea_s[h, M:, :] = endb_r[src, h, M:, :] + ti

        return 0

    lax.fori_loop(0, n, leave, 0)
    reverse_scan([(lea_s[h, :M, :], lea_s[h, M:, :]) for h in range(H)], True)

    def ig_copy(k, b, sender):
        rows = rows_at(b * B, B)
        return pltpu.make_async_remote_copy(
            src_ref=igs.at[k - 1, rows], dst_ref=igr.at[k - 1, rows], send_sem=ig_s.at[k - 1, b],
            recv_sem=ig_r.at[k - 1, b], device_id=place(tensor=lax.rem(t_me + k, nt)), device_id_type=MESH,
        )

    def leave_block(b, _):
        begin = first + b * B
        rows = rows_at(b * B, B)
        kept = flag(seg(begin + col) == seg(begin + B))
        for h in range(H):
            cols = slice(h * 128, h * 128 + 128)
            gr, gi = g_end[b, h, :M, :], g_end[b, h, M:, :]
            gx = gx_loc[h, rows, :] + kept * dot(colh_s[h], weigh(h, gr, gi))
            gv[rows, cols] = gx.astype(BF16)
        for k in range(1, nt):
            to = lax.rem(t_me + k, nt)
            part = rows_at(to * share, share)
            igs[k - 1, rows, :] = (
                dot_nt(gq[rows, :], proj[0, part, :]) + dot_nt(gv[rows, :], proj[1, part, :])
            ).astype(BF16)
            ig_copy(k, b, t_me).start()
        return 0

    def ig_own(b, _):
        rows = rows_at(b * B, B)
        part = rows_at(t_me * share, share)
        iga[rows, :] = dot_nt(gq[rows, :], proj[0, part, :]) + dot_nt(gv[rows, :], proj[1, part, :])
        return 0

    steps = 2 * nch
    def middle_step(s, _=None):
        @pl.when(big.has_out & (s < steps))
        def _():
            big.up(s)

        @pl.when(big.has_out & (s >= LAG))
        def _():
            big.down(s - LAG)

        return 0

    def end_step(s, _):
        @pl.when(big.no_out)
        def _():
            big.down(s)

        return 0

    def ig_rest(b, _):
        rows = rows_at(b * B, B)
        total = iga[rows, :]
        for k in range(1, nt):
            ig_copy(k, b, t_me).wait_recv()
            total = total + igr[k - 1, rows, :].astype(F32)
        gv[rows, :share] = total.astype(BF16)
        return 0

    def pg_copy(g, c):
        r = big.total_row(g * GROUP, c, GROUP)
        return pltpu.make_async_copy(tot.at[r], pg_out.at[r], pg_sem.at[g, c])

    def finish(g, _):
        big.finish(g)
        pg_copy(g, 0).start()
        pg_copy(g, 1).start()
        return 0

    def written(g, _):
        pg_copy(g, 0).wait()
        pg_copy(g, 1).wait()
        return 0

    work = [functools.partial(lax.fori_loop, b, min(b + 2, nb), leave_block, 0) for b in range(1, nb, 2)]
    work += [functools.partial(others_part, 1, i, gv) for i in range(2)]
    work += [functools.partial(own_part, 1, i, gv) for i in range(2)]
    work += [functools.partial(lax.fori_loop, b, min(b + 3, nb), ig_own, 0) for b in range(0, nb, 3)]
    small_partner.wait_recv()
    pl.when(small.no_out)(lambda: small.up(0))
    leave_block(0, 0)
    for s, item in enumerate(work):
        middle_step(s)
        item()
        if s == len(work) - 2:
            pl.when(small.has_out)(lambda: small.up(0))
    rest = [functools.partial(lax.fori_loop, b, min(b + 2, nb), ig_rest, 0) for b in range(0, nb, 2)]
    last = steps - 1 - len(rest)
    lax.fori_loop(len(work), last, middle_step, 0)
    small.down(0)
    for s, item in enumerate(rest):
        middle_step(last + s)
        item()
    ig_out_copy = pltpu.make_async_copy(gv.at[:, :share], ig_out, out_sem.at[1])
    ig_out_copy.start()
    lax.fori_loop(0, nch, end_step, 0)
    middle_step(steps - 1)
    lax.fori_loop(0, nch // GROUP, finish, 0)
    lax.fori_loop(steps, steps + LAG, middle_step, 0)
    lax.fori_loop(nch, steps, end_step, 0)
    small.finish(0)
    res_copy = pltpu.make_async_copy(mtot.at[pl.ds(0, 2 * M)], res_out, out_sem.at[4])
    skip_copy = pltpu.make_async_copy(mtot.at[pl.ds(2 * M, 8)], skip_out, out_sem.at[5])
    res_copy.start()
    skip_copy.start()
    lax.fori_loop(nch // GROUP, steps // GROUP, finish, 0)

    for b in range(nb):
        for k in range(1, nt):
            feature_copy(k, b, t_me).wait_send()
            ig_copy(k, b, t_me).wait_send()
    for k in range(1, nt):
        pole_copy(k).wait_send()
        z_copy(k, t_me).wait_send()
    for k in range(2):
        for i in range(2):
            partner_copy(k, i).wait_send()
    small_partner.wait_send()

    def sent(to, _):
        @pl.when(to > z)
        def _():
            forward_copy(z, to).wait_send()

        @pl.when(to < z)
        def _():
            backward_copy(z, to).wait_send()

        return 0

    lax.fori_loop(0, n, sent, 0)
    mixed_copy.wait()
    ig_out_copy.wait()
    lax.fori_loop(0, steps // GROUP, written, 0)
    res_copy.wait()
    skip_copy.wait()


def assemble_kernel(mixed, ig, pg, res, skips, mixed_o, ig_o, pg_o, res_o, skip_o, wide, sems):
    parts, rows = wide.shape[:2]
    stores = [pltpu.make_async_copy(wide.at[i], pg_o.at[pl.ds(i * rows, rows)], sems.at[i]) for i in range(parts)]
    for i, (src, dst) in enumerate(((mixed, mixed_o), (ig, ig_o), (res, res_o), (skips.at[pl.ds(0, 1)], skip_o))):
        stores.append(pltpu.make_async_copy(src, dst, sems.at[parts + i]))
        stores[-1].start()
    for i in range(parts):
        wide[i] = pg[pl.ds(i * rows, rows), :].astype(F32)
        stores[i].start()
    for copy in stores:
        copy.wait()


def shards(frames_in, in_proj, log_rates, angles, residues, skip_gain, lengths, grad_out):
    R, C = frames_in.shape[1:]
    D = in_proj.shape[1]
    M, H = log_rates.shape
    clips = lengths.shape[1]
    n, nt = lax.axis_size("tm"), lax.axis_size("tensor")
    nb = R // B
    norm = 1.0 / math.sqrt(R * n * lax.axis_size("dp"))
    half = D // 2
    nch = half // STEP
    share = D // nt
    resid = residues.reshape(2, M, H, 128).transpose(0, 2, 1, 3)
    skip = skip_gain.reshape(H, 1, 128)
    vm, dma = pltpu.VMEM, pltpu.SemaphoreType.DMA

    def chain_sems(steps, group):
        return [dma((steps,))] * 5 + [dma((steps // group,))] * 2

    scratch = [
        vm((R, D), BF16), vm((nb, D, B), BF16), vm((2, D, C), BF16), vm((R, C), BF16), vm((R, C), BF16),
        vm((H, B, 128), F32), vm((H, B, 128), F32), vm((H, B, 128), F32), vm((H, B, 128), F32),
        vm((H, B, 128), BF16), vm((H, B, 128), BF16), vm((H, B, 128), BF16),
        vm((H, R, 128), F32), vm((H, R, 128), F32), vm((R, C), BF16), vm((R, C), BF16), vm((R, C), BF16),
        vm((H, 144, 128), BF16), vm((H, 144, 128), BF16), vm((H, 128, 128), BF16), vm((H, 128, 128), BF16),
        vm((H, 128, 128), BF16), vm((H, 128, 128), BF16), vm((H, 128, 128), BF16),
        vm((H, 2, 8 * M, 128), F32), vm((H, 2, M, 128), F32), vm((H, 3, 2, M, 128), F32), vm((H, 2, M, 128), F32),
        vm((H, Q, 8, 128), F32), vm((H, M, 128), F32),
        vm((144, 128), BF16), vm((144, 128), BF16), vm((Q, 8, 128), F32), vm((8, 128), F32), vm((B, 128), F32),
        vm((B, 128), F32),
        vm((H, 2 * M, 128), F32), vm((H, 2 * M, 128), F32), vm((nb, H, 2 * M, 128), F32), vm((nb, H, 2 * M, 128), F32),
        vm((H, Q, 8, 128), F32), vm((H, 2 * M, 8, 128), F32), vm((H, 2 * M, 128), F32), vm((H, 2 * M, 128), F32),
        vm((n, H, 2 * M, 128), F32), vm((n, H, 2 * M, 128), F32),
        vm((2 * half, C), F32), vm((2 * half, C), BF16), vm((2 * half, C), BF16), vm((2 * half, C), BF16),
        vm((2 * half, C), BF16), vm((2 * half, C), BF16), vm((2 * D, C), BF16),
        vm((16, C), F32), vm((16, C), F32), vm((16, C), F32), vm((16, C), F32), vm((16, C), F32), vm((16, C), F32),
        vm((32, C), F32),
        vm((nt - 1, R, share), BF16), vm((nt - 1, R, share), BF16), vm((R, share), F32),
        vm((16, 128), F32), vm((nt - 1, 16, 128), F32), vm((16 * H, R), BF16), vm((nt - 1, 16 * H, C), BF16),
        vm((16 * H, D), BF16), vm((H, 2 * M, 128), F32), vm((H, 2 * M, 128), F32),
        dma((nt - 1,)), dma((nt - 1,)), dma((nt - 1,)), dma((nt - 1,)),
        dma((3,)), dma((nt - 1, nb)), dma((nt - 1, nb)), dma((n,)), dma((n,)), dma((n,)), dma((n,)),
        dma((2, 2)), dma((2, 2)), dma((nt - 1, nb)), dma((nt - 1, nb)), dma, dma, dma((6,)), dma((2 * nch // GROUP, 2)),
    ] + chain_sems(2 * nch, GROUP) + chain_sems(1, 1)
    vmem = pl.BlockSpec(memory_space=pltpu.VMEM)
    anywhere = pl.BlockSpec(memory_space=pl.ANY)
    mixed, ig, pg, res, skips = pl.pallas_call(
        functools.partial(layer_kernel, (clips, M, H, R, C, D, norm)),
        out_shape=[
            vm((R, C), BF16), vm((R, share), BF16), vm((2 * D, C), BF16), vm((2 * M, C), F32), vm((8, C), F32),
        ],
        in_specs=[pl.BlockSpec(memory_space=pltpu.SMEM)] + [vmem] * 4 + [anywhere] * 3,
        out_specs=[vmem] * 5,
        scratch_shapes=scratch,
        compiler_params=pltpu.CompilerParams(
            collective_id=0, has_side_effects=True, vmem_limit_bytes=56 << 20
        ),
        name="layer",
    )(lengths, log_rates.T, angles.T, resid, skip, frames_in[0], in_proj, grad_out[0])
    parts = 8
    mixed, ig, pg, res, skips = pl.pallas_call(
        assemble_kernel,
        out_shape=[
            jax.ShapeDtypeStruct((R, C), BF16), jax.ShapeDtypeStruct((R, share), BF16),
            jax.ShapeDtypeStruct((2 * D, C), F32), jax.ShapeDtypeStruct((2 * M, C), F32),
            jax.ShapeDtypeStruct((1, C), F32),
        ],
        in_specs=[vmem] * 5,
        out_specs=[anywhere] * 5,
        scratch_shapes=[vm((parts, 2 * D // parts, C), F32), dma((parts + 4,))],
        compiler_params=pltpu.CompilerParams(vmem_limit_bytes=20 << 20),
        name="assemble",
    )(mixed, ig, pg, res, skips)
    return mixed[None], ig[None], pg.reshape(2, D, C), res.reshape(2, M, C), skips[0]


def solution(mesh):
    in_specs = (
        P(("group", "dp"), "tm", "tensor"),
        P(None, None, "tensor"),
        P(None, "tensor"),
        P(None, "tensor"),
        P(None, None, "tensor"),
        P("tensor"),
        P(("group", "dp"), None),
        P(("group", "dp"), "tm", "tensor"),
    )
    out_specs = (
        P(("group", "dp"), "tm", "tensor"),
        P(("group", "dp"), "tm", "tensor"),
        P("group", None, "tensor"),
        P("group", None, "tensor"),
        P(("group", "tensor")),
    )
    return jax.shard_map(shards, mesh=mesh, in_specs=in_specs, out_specs=out_specs, check_vma=False)
```

```python
import functools
import math

import jax
import jax.numpy as jnp
from jax import lax
from jax.experimental import pallas as pl
from jax.experimental.pallas import tpu as pltpu
from jax.sharding import PartitionSpec as P

F32 = jnp.float32
BF16 = jnp.bfloat16
AXES = ("group", "tm", "tensor", "dp")
MESH = pl.DeviceIdType.MESH
Q = 16
B = 128
LAG = 2
GROUP = 4
EARLY = 2
STEP = 64


def dot(a, b):
    return jnp.dot(a, b, preferred_element_type=F32)


def dot_nt(a, b):
    return lax.dot_general(a, b, (((1,), (1,)), ((), ())), preferred_element_type=F32)


def flag(cond):
    return jnp.where(cond, 1.0, 0.0).astype(F32)


def rows_at(start, size, step=8):
    return pl.ds(pl.multiple_of(start, step), size)


class Place:
    def __init__(self):
        self.at = {axis: lax.axis_index(axis) for axis in AXES}

    def __call__(self, **moved):
        return tuple(moved.get(axis, self.at[axis]) for axis in AXES)


class Chain:
    def __init__(self, place, acc, also, snd, upb, inb, tot, sems, nch, size, half, tot_rows, group, core):
        n, z = lax.axis_size("tm"), place.at["tm"]
        left = z < n // 2
        self.inward = place(tm=jnp.where(left, z + 1, z - 1))
        self.outward = place(tm=jnp.clip(jnp.where(left, z - 1, z + 1), 0, n - 1))
        self.partner = place(dp=1 - core)
        depth = jnp.where(left, n // 2 - 1 - z, z - n // 2)
        self.root = depth == 0
        self.inner = depth > 0
        self.has_out = depth < n // 2 - 1
        self.no_out = depth == n // 2 - 1
        self.acc, self.also, self.snd, self.upb, self.inb, self.tot = acc, also, snd, upb, inb, tot
        (self.up_s, self.up_r, self.in_r, self.to_s, self.tot_r, self.dp_s, self.dp_r) = sems
        self.nch, self.size, self.half, self.tot_rows, self.group, self.core = nch, size, half, tot_rows, group, core
        self.wire = snd.dtype

    def row(self, s):
        return rows_at(s * self.size, self.size)

    def total_row(self, s, core, count=1):
        r = (s // self.nch) * self.tot_rows + core * self.half + (s % self.nch) * self.size
        return rows_at(r, self.size * count)

    def copy(self, src, dst, send, recv, to):
        return pltpu.make_async_remote_copy(
            src_ref=src, dst_ref=dst, send_sem=send, recv_sem=recv, device_id=to, device_id_type=MESH
        )

    def up_copy(self, s):
        r = self.row(s)
        return self.copy(self.snd.at[r], self.upb.at[r], self.up_s.at[s], self.up_r.at[s], self.inward)

    def in_copy(self, s):
        r = self.row(s)
        return self.copy(self.snd.at[r], self.inb.at[r], self.up_s.at[s], self.in_r.at[s], self.inward)

    def out_copy(self, s):
        r = self.total_row(s, self.core)
        return self.copy(self.tot.at[r], self.tot.at[r], self.to_s.at[s], self.tot_r.at[s], self.outward)

    def dp_copy(self, g, core):
        r = self.total_row(g * self.group, core, self.group)
        return self.copy(self.tot.at[r], self.tot.at[r], self.dp_s.at[g], self.dp_r.at[g], self.partner)

    def up(self, s):
        r = self.row(s)

        @pl.when(self.no_out)
        def _():
            self.snd[r] = (self.acc[r] + self.also[r].astype(F32)).astype(self.wire)

        @pl.when(self.has_out)
        def _():
            self.up_copy(s).wait_recv()
            self.snd[r] = (self.acc[r] + self.also[r].astype(F32) + self.upb[r].astype(F32)).astype(self.wire)

        @pl.when(self.inner)
        def _():
            self.up_copy(s).start()

        @pl.when(self.root)
        def _():
            self.in_copy(s).start()

    def down(self, s):
        @pl.when(self.root)
        def _():
            r = self.row(s)
            self.in_copy(s).wait_recv()
            self.tot[self.total_row(s, self.core)] = (self.snd[r].astype(F32) + self.inb[r].astype(F32)).astype(self.wire)

        @pl.when(self.inner)
        def _():
            self.out_copy(s).wait_recv()

        @pl.when(self.has_out)
        def _():
            self.out_copy(s).start()

        @pl.when(s % self.group == self.group - 1)
        def _():
            self.dp_copy(s // self.group, self.core).start()

    def finish(self, g):
        self.dp_copy(g, self.core).wait_send()
        self.dp_copy(g, 1 - self.core).wait_recv()
        for i in range(self.group):
            s = g * self.group + i

            @pl.when(self.has_out)
            def _():
                self.out_copy(s).wait_send()

            self.up_copy(s).wait_send()


def layer_kernel(
    cfg,
    lens_ref, rates_ref, angles_ref, resid_ref, skip_ref, frames_ref, proj_ref, up_hbm,
    mixed_out, ig_out, pg_out, res_out, skip_out,
    feat, feat_t, proj, up, q_s, x_scr, g_scr, y_scr, gx_scr, xb_s, gb_s, gm_s, y_loc, gx_loc, gq, gv, mixed_v,
    a1_s, a2_s, bt_s, b1_s, b2_s, colp_s, colh_s, pk_s, pos_s, pstep_s, w_s, k_s, wgt_s,
    ma1_s, ma2_s, keep_s, km_s, mb1_s, mb2_s,
    u_s, d_s, lead_s, g_end, r_s, rc_s, ent_s, lea_s, endf_r, endb_r,
    pacc, psnd, dpsnd, dprcv, upb, inb, tot, macc, msnd, mdps, mdpr, mupb, minb, mtot, igs, igr, iga,
    poles_mine, poles_r, reach_s, zsnd, zbuf, ue_s, e0_s, p_s, p_r, z_s, z_r,
    loc_sem, f_s, f_r, ef_s, ef_r, eb_s, eb_r, dps_s, dps_r, ig_s, ig_r, md_s, md_r, out_sem, pg_sem,
    *chain_sems,
):
    clips, M, H, R, C, D, norm = cfg
    nb = R // B
    place = Place()
    n, z = lax.axis_size("tm"), place.at["tm"]
    nt, t_me = lax.axis_size("tensor"), place.at["tensor"]
    core = place.at["dp"]
    first = z * R
    share = D // nt
    half = D // 2
    big_sems, small_sems = chain_sems[:7], chain_sems[7:]
    nch = half // STEP
    big = Chain(place, pacc, dprcv, psnd, upb, inb, tot, big_sems, nch, STEP, half, D, GROUP, core)
    small = Chain(place, macc, mdpr, msnd, mupb, minb, mtot, small_sems, 1, 16, 16, 32, 1, core)

    clip_starts = [jnp.int32(0)]
    for k in range(clips - 1):
        clip_starts.append(clip_starts[-1] + lens_ref[0, k])

    def seg(frame):
        total = jnp.where(frame >= clip_starts[0], 1, 0)
        for k in range(1, clips):
            total = total + jnp.where(frame >= clip_starts[k], 1, 0)
        return total

    mine = pl.ds(pl.multiple_of(t_me * C, 128), C)
    own_in = pltpu.make_async_copy(frames_ref, feat.at[:, mine], loc_sem.at[0])
    proj_in = pltpu.make_async_copy(proj_ref, proj, loc_sem.at[1])
    up_in = pltpu.make_async_copy(up_hbm, up, loc_sem.at[2])
    own_in.start()
    proj_in.start()
    up_in.start()

    barrier = pltpu.get_barrier_semaphore()
    for k in range(1, nt):
        pl.semaphore_signal(barrier, inc=1, device_id=place(tensor=lax.rem(t_me + k, nt)), device_id_type=MESH)
    pl.semaphore_signal(barrier, inc=1, device_id=place(dp=1 - core), device_id_type=MESH)
    for k in range(1, n):
        pl.semaphore_signal(barrier, inc=1, device_id=place(tm=lax.rem(z + k, n)), device_id_type=MESH)
    pl.semaphore_wait(barrier, nt + n - 1)

    def feature_copy(k, b, sender):
        rows = rows_at(b * B, B)
        cols = pl.ds(pl.multiple_of(sender * C, 128), C)
        return pltpu.make_async_remote_copy(
            src_ref=frames_ref.at[rows], dst_ref=feat.at[rows, cols], send_sem=f_s.at[k - 1, b],
            recv_sem=f_r.at[k - 1, b], device_id=place(tensor=lax.rem(t_me + k, nt)), device_id_type=MESH,
        )

    def pole_copy(k):
        return pltpu.make_async_remote_copy(
            src_ref=poles_mine, dst_ref=poles_r.at[k - 1], send_sem=p_s.at[k - 1], recv_sem=p_r.at[k - 1],
            device_id=place(tensor=lax.rem(t_me + k, nt)), device_id_type=MESH,
        )

    def z_copy(k, sender):
        cols = pl.ds(pl.multiple_of(sender * C, 128), C)
        return pltpu.make_async_remote_copy(
            src_ref=zsnd.at[k - 1], dst_ref=zbuf.at[:, cols], send_sem=z_s.at[k - 1], recv_sem=z_r.at[k - 1],
            device_id=place(tensor=lax.rem(t_me + k, nt)), device_id_type=MESH,
        )

    poles_mine[...] = jnp.zeros_like(poles_mine)
    poles_mine[:H, :M] = rates_ref[...]
    poles_mine[8 : 8 + H, :M] = angles_ref[...]
    for k in range(1, nt):
        pole_copy(k).start()
    for b in range(min(2, nb)):
        for k in range(1, nt):
            feature_copy(k, b, t_me).start()

    lane = lax.broadcasted_iota(jnp.int32, (8, 128), 1)
    sub = lax.broadcasted_iota(jnp.int32, (8, 128), 0)
    lanef = lane.astype(F32)
    in_chunk = lane % Q
    chunk = lane // Q
    square = lax.broadcasted_iota(jnp.int32, (M, M), 0) == lax.broadcasted_iota(jnp.int32, (M, M), 1)

    def upright(rates, turns):
        d = jnp.exp(jnp.sum(jnp.where(square, rates, 0.0), axis=1, keepdims=True))
        return d, jnp.sum(jnp.where(square, turns, 0.0), axis=1, keepdims=True)

    def powers_of(lag, d, a):
        size = jnp.exp(-d * lag)
        return size * jnp.cos(a * lag), size * jnp.sin(a * lag)

    def reach(ref):
        def one(h, _):
            d, a = upright(ref[pl.ds(h, 1), :][:, :M], ref[pl.ds(8 + h, 1), :][:, :M])
            re, im = powers_of(127.0 - lanef, d, a)
            step_re, step_im = powers_of(jnp.full((M, 128), float(B), F32), d, a)
            for b in reversed(range(nb)):
                kept = flag(seg(first + b * B + lane) == seg(first + R - 1))
                reach_s[rows_at(h * 16, 16, 16), b * B : b * B + B] = jnp.concatenate(
                    [re * kept, im * kept], axis=0
                ).astype(BF16)
                re, im = step_re * re - step_im * im, step_re * im + step_im * re
            return 0

        lax.fori_loop(0, H, one, 0)
        return dot(reach_s[...], feat[:, mine]).astype(BF16)

    own_in.wait()
    zbuf[:, mine] = reach(poles_mine)
    for k in range(1, nt):
        pole_copy(nt - k).wait_recv()
        zsnd[k - 1] = reach(poles_r.at[nt - k - 1])
        z_copy(k, t_me).start()
    for b in range(min(2, nb), nb):
        for k in range(1, nt):
            feature_copy(k, b, t_me).start()

    def tables(h, _):
        d, a = upright(rates_ref[pl.ds(h, 1), :], angles_ref[pl.ds(h, 1), :])

        def powers(lag, dd=d, aa=a):
            return powers_of(lag, dd, aa)

        pos_re, pos_im = powers(lanef)
        nxt_re, nxt_im = powers(lanef + 1.0)
        neg_re, neg_im = powers(-lanef - 1.0)
        end_re, end_im = powers(127.0 - lanef)
        far_re, far_im = powers(128.0 - lanef)
        b1_re, b1_im = powers((in_chunk + 1).astype(F32))
        b2_re, b2_im = powers((Q - in_chunk).astype(F32))
        pos_s[h, 0], pos_s[h, 1] = pos_re, pos_im
        for i, lag in enumerate((1.0, float(B), float(R))):
            pr, pi = powers(jnp.full((M, 128), lag, F32))
            pstep_s[h, i, 0], pstep_s[h, i, 1] = pr, pi
        y = 2.0 * d
        series = y * (1.0 - y / 2 * (1.0 - y / 3 * (1.0 - y / 4 * (1.0 - y / 5 * (1.0 - y / 6 * (1.0 - y / 7))))))
        wgt = jnp.sqrt(jnp.where(y < 0.25, series, 1.0 - jnp.exp(-y)))
        wgt = jnp.broadcast_to(wgt, (M, 128))
        wgt_s[h] = wgt
        wr, wi = resid_ref[0, h] * wgt, resid_ref[1, h] * wgt
        w_s[h, 0], w_s[h, 1] = wr, wi
        for k in range(Q):
            tap = jnp.sum(wr * pos_re[:, k : k + 1] - wi * pos_im[:, k : k + 1], axis=0, keepdims=True)
            if k == 0:
                tap = tap + skip_ref[h]
            k_s[h, k] = jnp.broadcast_to(tap, (8, 128))
        a1r, a1i, a2r, a2i, btr, bti, b2r, b2i = [], [], [], [], [], [], [], []
        subf = sub.astype(F32) * Q
        for m in range(M):
            one = slice(m, m + 1)
            pr, pi = powers(subf, d[one], a[one])
            pk_s[h, 0, m * 8 : m * 8 + 8], pk_s[h, 1, m * 8 : m * 8 + 8] = pr, pi
            back_re, back_im = powers(-subf - float(Q), d[one], a[one])
            fr, fi = neg_re[one], neg_im[one]
            past = lane < sub * Q
            a1r.append(jnp.where(past, pr * fr - pi * fi, 0.0))
            a1i.append(jnp.where(past, pr * fi + pi * fr, 0.0))
            fr, fi = pos_re[one], pos_im[one]
            later = lane >= (sub + 1) * Q
            a2r.append(jnp.where(later, back_re * fr - back_im * fi, 0.0))
            a2i.append(jnp.where(later, back_re * fi + back_im * fr, 0.0))
            here = chunk == sub
            btr.append(jnp.where(here, b1_re[one], 0.0))
            bti.append(jnp.where(here, b1_im[one], 0.0))
            b2r.append(jnp.where(here, b2_re[one], 0.0))
            b2i.append(jnp.where(here, b2_im[one], 0.0))
        a1_s[h] = jnp.concatenate(a1r + a1i + [end_re, end_im], axis=0).astype(BF16)
        a2_s[h] = jnp.concatenate(a2r + a2i + [pos_re, pos_im], axis=0).astype(BF16)
        bt = jnp.concatenate(btr + bti, axis=0)
        bt_s[h] = bt.astype(BF16)
        b1_s[h] = bt.T.astype(BF16)
        b2_s[h] = jnp.concatenate(b2r + b2i, axis=0).T.astype(BF16)
        pad = [jnp.zeros((128 - 2 * M, 128), F32)]
        colp_s[h] = jnp.concatenate([nxt_re, nxt_im] + pad, axis=0).T.astype(BF16)
        colh_s[h] = jnp.concatenate([far_re, far_im] + pad, axis=0).T.astype(BF16)
        return 0

    lax.fori_loop(0, H, tables, 0)
    u_s[...] = jnp.zeros_like(u_s)
    r_s[...] = jnp.zeros_like(r_s)
    rc_s[...] = jnp.zeros_like(rc_s)
    proj_in.wait()
    up_in.wait()

    def head(b, keep_block, h):
        rows = rows_at(b * B, B)
        xs = [x_scr[h, pl.ds(i, 8, stride=Q), :] for i in range(Q)]
        gs = [g_scr[h, pl.ds(i, 8, stride=Q), :] for i in range(Q)]
        held, corr = [], [None] * Q
        for i in range(Q):
            if i:
                kept = keep_s[i]
                held = [v * kept for v in held]
            held.append(xs[i])
            acc = None
            for s in range(i + 1):
                lag = i - s
                term = k_s[h, lag] * held[s]
                acc = term if acc is None else acc + term
                both = gs[i] * held[s]
                corr[lag] = both if corr[lag] is None else corr[lag] + both
            y_scr[h, pl.ds(i, 8, stride=Q), :] = acc
        for lag in range(Q):
            r_s[h, lag] += corr[lag]
        held = []
        for s in reversed(range(Q)):
            if s < Q - 1:
                kept = keep_s[s + 1]
                held = [v * kept for v in held]
            held = [gs[s]] + held
            acc = None
            for lag in range(Q - s):
                term = k_s[h, lag] * held[lag]
                acc = term if acc is None else acc + term
            gx_scr[h, pl.ds(s, 8, stride=Q), :] = acc

        states = dot(a1_s[h] * ma1_s[...], xb_s[h])
        leads = dot(bt_s[h], gm_s[h])
        adj = dot(a2_s[h] * ma2_s[...], gb_s[h])
        kept = km_s[...]
        vr, vi, ar, ai = [], [], [], []
        for m in range(M):
            re, im = slice(m * 8, m * 8 + 8), slice(64 + m * 8, 72 + m * 8)
            pr, pi = pk_s[h, 0, re] * kept, pk_s[h, 1, re] * kept
            ur, ui = u_s[h, m : m + 1, :], u_s[h, M + m : M + m + 1, :]
            sr = states[re] + (pr * ur - pi * ui)
            si = states[im] + (pr * ui + pi * ur)
            lr, li = leads[re], leads[im]
            rc_s[h, m] += sr * lr - si * li
            rc_s[h, M + m] += sr * li + si * lr
            wr, wi = w_s[h, 0, m : m + 1, :], w_s[h, 1, m : m + 1, :]
            vr.append(wr * sr - wi * si)
            vi.append(-(wr * si + wi * sr))
            ar.append(wr * adj[re] - wi * adj[im])
            ai.append(-(wr * adj[im] + wi * adj[re]))
        v = jnp.concatenate(vr + vi, axis=0).astype(BF16)
        y_loc[h, rows, :] = y_scr[h] + mb1_s[...] * dot(b1_s[h], v)
        v = jnp.concatenate(ar + ai, axis=0).astype(BF16)
        gx_loc[h, rows, :] = gx_scr[h] + mb2_s[...] * dot(b2_s[h], v)
        lead_s[b, h] = adj[128:]
        pr, pi = pstep_s[h, 1, 0] * keep_block, pstep_s[h, 1, 1] * keep_block
        ur, ui = u_s[h, :M, :], u_s[h, M:, :]
        u_s[h, :M, :] = states[128 : 128 + M] + (pr * ur - pi * ui)
        u_s[h, M:, :] = states[128 + M :] + (pr * ui + pi * ur)

    col = lax.broadcasted_iota(jnp.int32, (B, 128), 0)

    def block(b, _):
        begin = first + b * B
        rows = rows_at(b * B, B)
        seg_t = seg(begin + lane)
        same = flag(seg_t == seg(begin + sub * Q - 1))
        ma1_s[...] = jnp.concatenate([same] * 16 + [flag(seg_t == seg(begin + B - 1))] * 2, axis=0).astype(BF16)
        same = flag(seg_t == seg(begin + (sub + 1) * Q))
        ma2_s[...] = jnp.concatenate([same] * 16 + [flag(seg_t == seg(begin))] * 2, axis=0).astype(BF16)
        km_s[...] = flag(seg(begin + sub * Q - 1) == seg(begin - 1))
        for i in range(Q):
            at = begin + sub * Q + i
            keep_s[i] = flag(seg(at) == seg(at - 1))
        seg_c = seg(begin + col)
        mb1_s[...] = flag(seg_c == seg(begin + (col // Q) * Q - 1))
        mb2_s[...] = flag(seg_c == seg(begin + (col // Q + 1) * Q))
        keep_block = flag(seg(begin + B - 1) == seg(begin - 1))

        for k in range(1, nt):
            feature_copy(k, b, lax.rem(t_me - k + nt, nt)).wait_recv()
        fb = feat[rows, :]
        query = dot(fb, proj[0]).astype(BF16)
        signal = dot(fb, proj[1]).astype(BF16)
        q_s[rows, :] = query
        g = query.astype(F32) * up[rows, :].astype(F32)
        signal32 = signal.astype(F32)
        for h in range(H):
            cols = slice(h * 128, h * 128 + 128)
            x_scr[h] = signal32[:, cols]
            g_scr[h] = g[:, cols]
            xb_s[h] = signal[:, cols]
            gb_s[h] = g[:, cols].astype(BF16)
            gm_s[h] = (g[:, cols] * mb1_s[...]).astype(BF16)
        feat_t[b] = fb.T

        for h in range(H):
            head(b, keep_block, h)
        return 0

    def turned(h, which, re, im, kept):
        pr, pi = pstep_s[h, which, 0] * kept, pstep_s[h, which, 1] * kept
        return pr * re - pi * im, pr * im + pi * re

    def end_copy(src, dst, send, recv, slot, to):
        return pltpu.make_async_remote_copy(
            src_ref=src, dst_ref=dst.at[slot], send_sem=send.at[to], recv_sem=recv.at[slot],
            device_id=place(tm=to), device_id_type=MESH,
        )

    def forward_copy(slot, to):
        return end_copy(ue_s, endf_r, ef_s, ef_r, slot, to)

    def backward_copy(slot, to):
        return end_copy(d_s, endb_r, eb_s, eb_r, slot, to)

    def enter(src, _):
        @pl.when(src < z)
        def _():
            forward_copy(src, z).wait_recv()
            kept = flag(seg(src * R - 1) == seg(src * R + R - 1))
            for h in range(H):
                tr, ti = turned(h, 2, ent_s[h, :M, :], ent_s[h, M:, :], kept)
                ent_s[h, :M, :] = endf_r[src, h, :M, :] + tr
                ent_s[h, M:, :] = endf_r[src, h, M:, :] + ti

        return 0


    def weigh(h, re, im):
        wr, wi = w_s[h, 0], w_s[h, 1]
        pad = [jnp.zeros((128 - 2 * M, 128), F32)]
        return jnp.concatenate([wr * re - wi * im, -(wr * im + wi * re)] + pad, axis=0).astype(BF16)

    def enter_block(b, _):
        begin = first + b * B
        rows = rows_at(b * B, B)
        kept = flag(seg(begin + col) == seg(first - 1))
        for h in range(H):
            cols = slice(h * 128, h * 128 + 128)
            er, ei = ent_s[h, :M, :], ent_s[h, M:, :]
            y = y_loc[h, rows, :] + kept * dot(colp_s[h], weigh(h, er, ei))
            mixed_v[rows, cols] = (q_s[rows, cols].astype(F32) * y).astype(BF16)
            gq[rows, cols] = (up[rows, cols].astype(F32) * y).astype(BF16)
            ent_s[h, :M, :], ent_s[h, M:, :] = turned(h, 1, er, ei, 1.0)
        return 0

    def send_states():
        for k in range(1, nt):
            z_copy(k, lax.rem(t_me - k + nt, nt)).wait_recv()
        ends = dot(zbuf[...], proj[1])
        for h in range(H):
            ue_s[h] = ends[h * 16 : h * 16 + 16, h * 128 : h * 128 + 128]

        def go(to, _):
            @pl.when(to > z)
            def _():
                forward_copy(z, to).start()

            return 0

        lax.fori_loop(0, n, go, 0)

    def take_states():
        ent_s[...] = jnp.zeros_like(ent_s)
        lax.fori_loop(0, n, enter, 0)
        e0_s[...] = ent_s[...]
        lax.fori_loop(0, EARLY, enter_block, 0)

    def stream(b, _):
        pl.when(b == 1)(send_states)
        block(b, 0)
        pl.when(b == EARLY)(take_states)

        @pl.when(b >= EARLY)
        def _():
            enter_block(b, 0)

        return 0

    lax.fori_loop(0, nb, stream, 0)

    def reverse_scan(start, store):
        state = start
        for b in reversed(range(nb)):
            begin = first + b * B
            kept = flag(seg(begin) == seg(begin + B))
            following = []
            for h in range(H):
                re, im = state[h]
                if store:
                    g_end[b, h, :M, :], g_end[b, h, M:, :] = re, im
                tr, ti = turned(h, 1, re, im, kept)
                following.append((lead_s[b, h, :M, :] + tr, lead_s[b, h, M:, :] + ti))
            state = following
        return state

    mixed_copy = pltpu.make_async_copy(mixed_v, mixed_out, out_sem.at[0])
    mixed_copy.start()

    quarter = half // 2

    def partner_copy(k, i):
        r = rows_at(k * half + i * quarter, quarter)
        return pltpu.make_async_remote_copy(
            src_ref=dpsnd.at[r], dst_ref=dprcv.at[r], send_sem=dps_s.at[k, i], recv_sem=dps_r.at[k, i],
            device_id=place(dp=1 - core), device_id_type=MESH,
        )

    def transposed(start):
        return jnp.concatenate([feat_t[b, rows_at(start, quarter), :] for b in range(nb)], axis=1)

    def others_part(k, i, other):
        r = rows_at(k * half + i * quarter, quarter)
        dpsnd[r] = (dot(transposed((1 - core) * half + i * quarter), other[...]) * norm).astype(BF16)
        partner_copy(k, i).start()

    def own_part(k, i, other):
        r = rows_at(k * half + i * quarter, quarter)
        pacc[r] = dot(transposed(core * half + i * quarter), other[...]) * norm
        partner_copy(k, i).wait_recv()

        @pl.when(big.no_out)
        def _():
            def go(j, _):
                big.up(k * nch + i * (nch // 2) + j)
                return 0

            lax.fori_loop(0, nch // 2, go, 0)

    others_part(0, 0, gq)
    zero = jnp.zeros((M, 128), F32)
    ends = reverse_scan([(zero, zero)] * H, False)
    for h in range(H):
        d_s[h, :M, :], d_s[h, M:, :] = ends[h]

    def send_adjoint(to, _):
        @pl.when(to < z)
        def _():
            backward_copy(z, to).start()

        return 0

    lax.fori_loop(0, n, send_adjoint, 0)
    lea_s[...] = jnp.zeros_like(lea_s)

    others_part(0, 1, gq)
    own_part(0, 0, gq)
    own_part(0, 1, gq)
    kept_first = flag(seg(first) == seg(first - 1))
    for h in range(H):
        lr, li = turned(h, 0, d_s[h, :M, :], d_s[h, M:, :], kept_first)
        er, ei = e0_s[h, :M, :], e0_s[h, M:, :]
        re, im = [], []
        for m in range(M):
            re.append(jnp.sum(rc_s[h, m], axis=0, keepdims=True))
            im.append(jnp.sum(rc_s[h, M + m], axis=0, keepdims=True))
        re = jnp.concatenate(re, axis=0) + er * lr - ei * li
        im = jnp.concatenate(im, axis=0) + er * li + ei * lr
        for lag in range(Q):
            r = jnp.sum(r_s[h, lag], axis=0, keepdims=True)
            if lag == 0:
                skip_row = r
            re = re + pos_s[h, 0, :, lag : lag + 1] * r
            im = im + pos_s[h, 1, :, lag : lag + 1] * r
        cols = slice(h * 128, h * 128 + 128)
        scale = wgt_s[h] * norm
        terms = jnp.concatenate([re * scale, -im * scale, skip_row * norm, jnp.zeros((15, 128), F32)], axis=0)
        own = rows_at(core * 16, 16)
        mdps[:, cols] = jnp.where(core == 0, terms[16:], terms[:16])
        macc[:, cols] = jnp.where(core == 0, terms[:16], terms[16:])

    small_partner = pltpu.make_async_remote_copy(
        src_ref=mdps, dst_ref=mdpr, send_sem=md_s, recv_sem=md_r, device_id=place(dp=1 - core), device_id_type=MESH
    )
    small_partner.start()

    def leave(i, _):
        src = n - 1 - i

        @pl.when(src > z)
        def _():
            backward_copy(src, z).wait_recv()
            kept = flag(seg(src * R) == seg(src * R + R))
            for h in range(H):
                tr, ti = turned(h, 2, lea_s[h, :M, :], lea_s[h, M:, :], kept)
                lea_s[h, :M, :] = endb_r[src, h, :M, :] + tr
                lea_s[h, M:, :] = endb_r[src, h, M:, :] + ti

        return 0

    lax.fori_loop(0, n, leave, 0)
    reverse_scan([(lea_s[h, :M, :], lea_s[h, M:, :]) for h in range(H)], True)

    def ig_copy(k, b, sender):
        rows = rows_at(b * B, B)
        return pltpu.make_async_remote_copy(
            src_ref=igs.at[k - 1, rows], dst_ref=igr.at[k - 1, rows], send_sem=ig_s.at[k - 1, b],
            recv_sem=ig_r.at[k - 1, b], device_id=place(tensor=lax.rem(t_me + k, nt)), device_id_type=MESH,
        )

    def leave_block(b, _):
        begin = first + b * B
        rows = rows_at(b * B, B)
        kept = flag(seg(begin + col) == seg(begin + B))
        for h in range(H):
            cols = slice(h * 128, h * 128 + 128)
            gr, gi = g_end[b, h, :M, :], g_end[b, h, M:, :]
            gx = gx_loc[h, rows, :] + kept * dot(colh_s[h], weigh(h, gr, gi))
            gv[rows, cols] = gx.astype(BF16)
        for k in range(1, nt):
            to = lax.rem(t_me + k, nt)
            part = rows_at(to * share, share)
            igs[k - 1, rows, :] = (
                dot_nt(gq[rows, :], proj[0, part, :]) + dot_nt(gv[rows, :], proj[1, part, :])
            ).astype(BF16)
            ig_copy(k, b, t_me).start()
        return 0

    def ig_own(b, _):
        rows = rows_at(b * B, B)
        part = rows_at(t_me * share, share)
        iga[rows, :] = dot_nt(gq[rows, :], proj[0, part, :]) + dot_nt(gv[rows, :], proj[1, part, :])
        return 0

    steps = 2 * nch
    def middle_step(s, _=None):
        @pl.when(big.has_out & (s < steps))
        def _():
            big.up(s)

        @pl.when(big.has_out & (s >= LAG))
        def _():
            big.down(s - LAG)

        return 0

    def end_step(s, _):
        @pl.when(big.no_out)
        def _():
            big.down(s)

        return 0

    def ig_rest(b, _):
        rows = rows_at(b * B, B)
        total = iga[rows, :]
        for k in range(1, nt):
            ig_copy(k, b, t_me).wait_recv()
            total = total + igr[k - 1, rows, :].astype(F32)
        gv[rows, :share] = total.astype(BF16)
        return 0

    def pg_copy(g, c):
        r = big.total_row(g * GROUP, c, GROUP)
        return pltpu.make_async_copy(tot.at[r], pg_out.at[r], pg_sem.at[g, c])

    def finish(g, _):
        big.finish(g)
        pg_copy(g, 0).start()
        pg_copy(g, 1).start()
        return 0

    def written(g, _):
        pg_copy(g, 0).wait()
        pg_copy(g, 1).wait()
        return 0

    work = [functools.partial(lax.fori_loop, b, min(b + 2, nb), leave_block, 0) for b in range(1, nb, 2)]
    work += [functools.partial(others_part, 1, i, gv) for i in range(2)]
    work += [functools.partial(own_part, 1, i, gv) for i in range(2)]
    work += [functools.partial(lax.fori_loop, b, min(b + 3, nb), ig_own, 0) for b in range(0, nb, 3)]
    small_partner.wait_recv()
    pl.when(small.no_out)(lambda: small.up(0))
    leave_block(0, 0)
    for s, item in enumerate(work):
        middle_step(s)
        item()
        if s == len(work) - 2:
            pl.when(small.has_out)(lambda: small.up(0))
    rest = [functools.partial(lax.fori_loop, b, min(b + 2, nb), ig_rest, 0) for b in range(0, nb, 2)]
    last = steps - 1 - len(rest)
    lax.fori_loop(len(work), last, middle_step, 0)
    small.down(0)
    for s, item in enumerate(rest):
        middle_step(last + s)
        item()
    ig_out_copy = pltpu.make_async_copy(gv.at[:, :share], ig_out, out_sem.at[1])
    ig_out_copy.start()
    lax.fori_loop(0, nch, end_step, 0)
    middle_step(steps - 1)
    lax.fori_loop(0, nch // GROUP, finish, 0)
    lax.fori_loop(steps, steps + LAG, middle_step, 0)
    lax.fori_loop(nch, steps, end_step, 0)
    small.finish(0)
    res_copy = pltpu.make_async_copy(mtot.at[pl.ds(0, 2 * M)], res_out, out_sem.at[4])
    skip_copy = pltpu.make_async_copy(mtot.at[pl.ds(2 * M, 8)], skip_out, out_sem.at[5])
    res_copy.start()
    skip_copy.start()
    lax.fori_loop(nch // GROUP, steps // GROUP, finish, 0)

    for b in range(nb):
        for k in range(1, nt):
            feature_copy(k, b, t_me).wait_send()
            ig_copy(k, b, t_me).wait_send()
    for k in range(1, nt):
        pole_copy(k).wait_send()
        z_copy(k, t_me).wait_send()
    for k in range(2):
        for i in range(2):
            partner_copy(k, i).wait_send()
    small_partner.wait_send()

    def sent(to, _):
        @pl.when(to > z)
        def _():
            forward_copy(z, to).wait_send()

        @pl.when(to < z)
        def _():
            backward_copy(z, to).wait_send()

        return 0

    lax.fori_loop(0, n, sent, 0)
    mixed_copy.wait()
    ig_out_copy.wait()
    lax.fori_loop(0, steps // GROUP, written, 0)
    res_copy.wait()
    skip_copy.wait()


def assemble_kernel(mixed, ig, pg, res, skips, mixed_o, ig_o, pg_o, res_o, skip_o, wide, sems):
    parts, rows = wide.shape[:2]
    stores = [pltpu.make_async_copy(wide.at[i], pg_o.at[pl.ds(i * rows, rows)], sems.at[i]) for i in range(parts)]
    for i, (src, dst) in enumerate(((mixed, mixed_o), (ig, ig_o), (res, res_o), (skips.at[pl.ds(0, 1)], skip_o))):
        stores.append(pltpu.make_async_copy(src, dst, sems.at[parts + i]))
        stores[-1].start()
    for i in range(parts):
        wide[i] = pg[pl.ds(i * rows, rows), :].astype(F32)
        stores[i].start()
    for copy in stores:
        copy.wait()


def shards(frames_in, in_proj, log_rates, angles, residues, skip_gain, lengths, grad_out):
    R, C = frames_in.shape[1:]
    D = in_proj.shape[1]
    M, H = log_rates.shape
    clips = lengths.shape[1]
    n, nt = lax.axis_size("tm"), lax.axis_size("tensor")
    nb = R // B
    norm = 1.0 / math.sqrt(R * n * lax.axis_size("dp"))
    half = D // 2
    nch = half // STEP
    share = D // nt
    resid = residues.reshape(2, M, H, 128).transpose(0, 2, 1, 3)
    skip = skip_gain.reshape(H, 1, 128)
    vm, dma = pltpu.VMEM, pltpu.SemaphoreType.DMA

    def chain_sems(steps, group):
        return [dma((steps,))] * 5 + [dma((steps // group,))] * 2

    scratch = [
        vm((R, D), BF16), vm((nb, D, B), BF16), vm((2, D, C), BF16), vm((R, C), BF16), vm((R, C), BF16),
        vm((H, B, 128), F32), vm((H, B, 128), F32), vm((H, B, 128), F32), vm((H, B, 128), F32),
        vm((H, B, 128), BF16), vm((H, B, 128), BF16), vm((H, B, 128), BF16),
        vm((H, R, 128), F32), vm((H, R, 128), F32), vm((R, C), BF16), vm((R, C), BF16), vm((R, C), BF16),
        vm((H, 144, 128), BF16), vm((H, 144, 128), BF16), vm((H, 128, 128), BF16), vm((H, 128, 128), BF16),
        vm((H, 128, 128), BF16), vm((H, 128, 128), BF16), vm((H, 128, 128), BF16),
        vm((H, 2, 8 * M, 128), F32), vm((H, 2, M, 128), F32), vm((H, 3, 2, M, 128), F32), vm((H, 2, M, 128), F32),
        vm((H, Q, 8, 128), F32), vm((H, M, 128), F32),
        vm((144, 128), BF16), vm((144, 128), BF16), vm((Q, 8, 128), F32), vm((8, 128), F32), vm((B, 128), F32),
        vm((B, 128), F32),
        vm((H, 2 * M, 128), F32), vm((H, 2 * M, 128), F32), vm((nb, H, 2 * M, 128), F32), vm((nb, H, 2 * M, 128), F32),
        vm((H, Q, 8, 128), F32), vm((H, 2 * M, 8, 128), F32), vm((H, 2 * M, 128), F32), vm((H, 2 * M, 128), F32),
        vm((n, H, 2 * M, 128), F32), vm((n, H, 2 * M, 128), F32),
        vm((2 * half, C), F32), vm((2 * half, C), BF16), vm((2 * half, C), BF16), vm((2 * half, C), BF16),
        vm((2 * half, C), BF16), vm((2 * half, C), BF16), vm((2 * D, C), BF16),
        vm((16, C), F32), vm((16, C), F32), vm((16, C), F32), vm((16, C), F32), vm((16, C), F32), vm((16, C), F32),
        vm((32, C), F32),
        vm((nt - 1, R, share), BF16), vm((nt - 1, R, share), BF16), vm((R, share), F32),
        vm((16, 128), F32), vm((nt - 1, 16, 128), F32), vm((16 * H, R), BF16), vm((nt - 1, 16 * H, C), BF16),
        vm((16 * H, D), BF16), vm((H, 2 * M, 128), F32), vm((H, 2 * M, 128), F32),
        dma((nt - 1,)), dma((nt - 1,)), dma((nt - 1,)), dma((nt - 1,)),
        dma((3,)), dma((nt - 1, nb)), dma((nt - 1, nb)), dma((n,)), dma((n,)), dma((n,)), dma((n,)),
        dma((2, 2)), dma((2, 2)), dma((nt - 1, nb)), dma((nt - 1, nb)), dma, dma, dma((6,)), dma((2 * nch // GROUP, 2)),
    ] + chain_sems(2 * nch, GROUP) + chain_sems(1, 1)
    vmem = pl.BlockSpec(memory_space=pltpu.VMEM)
    anywhere = pl.BlockSpec(memory_space=pl.ANY)
    mixed, ig, pg, res, skips = pl.pallas_call(
        functools.partial(layer_kernel, (clips, M, H, R, C, D, norm)),
        out_shape=[
            vm((R, C), BF16), vm((R, share), BF16), vm((2 * D, C), BF16), vm((2 * M, C), F32), vm((8, C), F32),
        ],
        in_specs=[pl.BlockSpec(memory_space=pltpu.SMEM)] + [vmem] * 4 + [anywhere] * 3,
        out_specs=[vmem] * 5,
        scratch_shapes=scratch,
        compiler_params=pltpu.CompilerParams(
            collective_id=0, has_side_effects=True, vmem_limit_bytes=56 << 20
        ),
        name="layer",
    )(lengths, log_rates.T, angles.T, resid, skip, frames_in[0], in_proj, grad_out[0])
    parts = 8
    mixed, ig, pg, res, skips = pl.pallas_call(
        assemble_kernel,
        out_shape=[
            jax.ShapeDtypeStruct((R, C), BF16), jax.ShapeDtypeStruct((R, share), BF16),
            jax.ShapeDtypeStruct((2 * D, C), F32), jax.ShapeDtypeStruct((2 * M, C), F32),
            jax.ShapeDtypeStruct((1, C), F32),
        ],
        in_specs=[vmem] * 5,
        out_specs=[anywhere] * 5,
        scratch_shapes=[vm((parts, 2 * D // parts, C), F32), dma((parts + 4,))],
        compiler_params=pltpu.CompilerParams(vmem_limit_bytes=20 << 20),
        name="assemble",
    )(mixed, ig, pg, res, skips)
    return mixed[None], ig[None], pg.reshape(2, D, C), res.reshape(2, M, C), skips[0]


def solution(mesh):
    in_specs = (
        P(("group", "dp"), "tm", "tensor"),
        P(None, None, "tensor"),
        P(None, "tensor"),
        P(None, "tensor"),
        P(None, None, "tensor"),
        P("tensor"),
        P(("group", "dp"), None),
        P(("group", "dp"), "tm", "tensor"),
    )
    out_specs = (
        P(("group", "dp"), "tm", "tensor"),
        P(("group", "dp"), "tm", "tensor"),
        P("group", None, "tensor"),
        P("group", None, "tensor"),
        P(("group", "tensor")),
    )
    return jax.shard_map(shards, mesh=mesh, in_specs=in_specs, out_specs=out_specs, check_vma=False)
```

```python
import functools
import math

import jax
import jax.numpy as jnp
from jax import lax
from jax.experimental import pallas as pl
from jax.experimental.pallas import tpu as pltpu
from jax.sharding import PartitionSpec as P

F32 = jnp.float32
BF16 = jnp.bfloat16
AXES = ("group", "tm", "tensor", "dp")
MESH = pl.DeviceIdType.MESH
Q = 16
B = 128
LAG = 2
GROUP = 4
EARLY = 2
STEP = 64


def dot(a, b):
    return jnp.dot(a, b, preferred_element_type=F32)


def dot_nt(a, b):
    return lax.dot_general(a, b, (((1,), (1,)), ((), ())), preferred_element_type=F32)


def flag(cond):
    return jnp.where(cond, 1.0, 0.0).astype(F32)


def rows_at(start, size, step=8):
    return pl.ds(pl.multiple_of(start, step), size)


class Place:
    def __init__(self):
        self.at = {axis: lax.axis_index(axis) for axis in AXES}

    def __call__(self, **moved):
        return tuple(moved.get(axis, self.at[axis]) for axis in AXES)


class Chain:
    def __init__(self, place, acc, also, snd, upb, inb, tot, sems, nch, size, half, tot_rows, group, core):
        n, z = lax.axis_size("tm"), place.at["tm"]
        left = z < n // 2
        self.inward = place(tm=jnp.where(left, z + 1, z - 1))
        self.outward = place(tm=jnp.clip(jnp.where(left, z - 1, z + 1), 0, n - 1))
        self.partner = place(dp=1 - core)
        depth = jnp.where(left, n // 2 - 1 - z, z - n // 2)
        self.root = depth == 0
        self.inner = depth > 0
        self.has_out = depth < n // 2 - 1
        self.no_out = depth == n // 2 - 1
        self.acc, self.also, self.snd, self.upb, self.inb, self.tot = acc, also, snd, upb, inb, tot
        (self.up_s, self.up_r, self.in_r, self.to_s, self.tot_r, self.dp_s, self.dp_r) = sems
        self.nch, self.size, self.half, self.tot_rows, self.group, self.core = nch, size, half, tot_rows, group, core
        self.wire = snd.dtype

    def row(self, s):
        return rows_at(s * self.size, self.size)

    def total_row(self, s, core, count=1):
        r = (s // self.nch) * self.tot_rows + core * self.half + (s % self.nch) * self.size
        return rows_at(r, self.size * count)

    def copy(self, src, dst, send, recv, to):
        return pltpu.make_async_remote_copy(
            src_ref=src, dst_ref=dst, send_sem=send, recv_sem=recv, device_id=to, device_id_type=MESH
        )

    def up_copy(self, s):
        r = self.row(s)
        return self.copy(self.snd.at[r], self.upb.at[r], self.up_s.at[s], self.up_r.at[s], self.inward)

    def in_copy(self, s):
        r = self.row(s)
        return self.copy(self.snd.at[r], self.inb.at[r], self.up_s.at[s], self.in_r.at[s], self.inward)

    def out_copy(self, s):
        r = self.total_row(s, self.core)
        return self.copy(self.tot.at[r], self.tot.at[r], self.to_s.at[s], self.tot_r.at[s], self.outward)

    def dp_copy(self, g, core):
        r = self.total_row(g * self.group, core, self.group)
        return self.copy(self.tot.at[r], self.tot.at[r], self.dp_s.at[g], self.dp_r.at[g], self.partner)

    def up(self, s):
        r = self.row(s)

        @pl.when(self.no_out)
        def _():
            self.snd[r] = (self.acc[r] + self.also[r].astype(F32)).astype(self.wire)

        @pl.when(self.has_out)
        def _():
            self.up_copy(s).wait_recv()
            self.snd[r] = (self.acc[r] + self.also[r].astype(F32) + self.upb[r].astype(F32)).astype(self.wire)

        @pl.when(self.inner)
        def _():
            self.up_copy(s).start()

        @pl.when(self.root)
        def _():
            self.in_copy(s).start()

    def down(self, s):
        @pl.when(self.root)
        def _():
            r = self.row(s)
            self.in_copy(s).wait_recv()
            self.tot[self.total_row(s, self.core)] = (self.snd[r].astype(F32) + self.inb[r].astype(F32)).astype(self.wire)

        @pl.when(self.inner)
        def _():
            self.out_copy(s).wait_recv()

        @pl.when(self.has_out)
        def _():
            self.out_copy(s).start()

        @pl.when(s % self.group == self.group - 1)
        def _():
            self.dp_copy(s // self.group, self.core).start()

    def finish(self, g):
        self.dp_copy(g, self.core).wait_send()
        self.dp_copy(g, 1 - self.core).wait_recv()
        for i in range(self.group):
            s = g * self.group + i

            @pl.when(self.has_out)
            def _():
                self.out_copy(s).wait_send()

            self.up_copy(s).wait_send()


def layer_kernel(
    cfg,
    lens_ref, rates_ref, angles_ref, resid_ref, skip_ref, frames_ref, proj_ref, up_hbm,
    mixed_out, ig_out, pg_out, res_out, skip_out,
    feat, feat_t, proj, up, q_s, x_scr, g_scr, y_scr, gx_scr, xb_s, gb_s, gm_s, y_loc, gx_loc, gq, gv, mixed_v,
    a1_s, a2_s, bt_s, b1_s, b2_s, colp_s, colh_s, pk_s, pos_s, pstep_s, w_s, k_s, wgt_s,
    ma1_s, ma2_s, keep_s, km_s, mb1_s, mb2_s,
    u_s, d_s, lead_s, g_end, r_s, rc_s, ent_s, lea_s, endf_r, endb_r,
    pacc, psnd, dpsnd, dprcv, upb, inb, tot, macc, msnd, mdps, mdpr, mupb, minb, mtot, igs, igr, iga,
    poles_mine, poles_r, reach_s, zsnd, zbuf, ue_s, e0_s, p_s, p_r, z_s, z_r,
    loc_sem, f_s, f_r, ef_s, ef_r, eb_s, eb_r, dps_s, dps_r, ig_s, ig_r, md_s, md_r, out_sem, pg_sem,
    *chain_sems,
):
    clips, M, H, R, C, D, norm = cfg
    nb = R // B
    place = Place()
    n, z = lax.axis_size("tm"), place.at["tm"]
    nt, t_me = lax.axis_size("tensor"), place.at["tensor"]
    core = place.at["dp"]
    first = z * R
    share = D // nt
    half = D // 2
    big_sems, small_sems = chain_sems[:7], chain_sems[7:]
    nch = half // STEP
    big = Chain(place, pacc, dprcv, psnd, upb, inb, tot, big_sems, nch, STEP, half, D, GROUP, core)
    small = Chain(place, macc, mdpr, msnd, mupb, minb, mtot, small_sems, 1, 16, 16, 32, 1, core)

    clip_starts = [jnp.int32(0)]
    for k in range(clips - 1):
        clip_starts.append(clip_starts[-1] + lens_ref[0, k])

    def seg(frame):
        total = jnp.where(frame >= clip_starts[0], 1, 0)
        for k in range(1, clips):
            total = total + jnp.where(frame >= clip_starts[k], 1, 0)
        return total

    mine = pl.ds(pl.multiple_of(t_me * C, 128), C)
    own_in = pltpu.make_async_copy(frames_ref, feat.at[:, mine], loc_sem.at[0])
    proj_in = pltpu.make_async_copy(proj_ref, proj, loc_sem.at[1])
    up_in = pltpu.make_async_copy(up_hbm, up, loc_sem.at[2])
    own_in.start()
    proj_in.start()
    up_in.start()

    barrier = pltpu.get_barrier_semaphore()
    for k in range(1, nt):
        pl.semaphore_signal(barrier, inc=1, device_id=place(tensor=lax.rem(t_me + k, nt)), device_id_type=MESH)
    pl.semaphore_signal(barrier, inc=1, device_id=place(dp=1 - core), device_id_type=MESH)
    for k in range(1, n):
        pl.semaphore_signal(barrier, inc=1, device_id=place(tm=lax.rem(z + k, n)), device_id_type=MESH)
    pl.semaphore_wait(barrier, nt + n - 1)

    def feature_copy(k, b, sender):
        rows = rows_at(b * B, B)
        cols = pl.ds(pl.multiple_of(sender * C, 128), C)
        return pltpu.make_async_remote_copy(
            src_ref=frames_ref.at[rows], dst_ref=feat.at[rows, cols], send_sem=f_s.at[k - 1, b],
            recv_sem=f_r.at[k - 1, b], device_id=place(tensor=lax.rem(t_me + k, nt)), device_id_type=MESH,
        )

    def pole_copy(k):
        return pltpu.make_async_remote_copy(
            src_ref=poles_mine, dst_ref=poles_r.at[k - 1], send_sem=p_s.at[k - 1], recv_sem=p_r.at[k - 1],
            device_id=place(tensor=lax.rem(t_me + k, nt)), device_id_type=MESH,
        )

    def z_copy(k, sender):
        cols = pl.ds(pl.multiple_of(sender * C, 128), C)
        return pltpu.make_async_remote_copy(
            src_ref=zsnd.at[k - 1], dst_ref=zbuf.at[:, cols], send_sem=z_s.at[k - 1], recv_sem=z_r.at[k - 1],
            device_id=place(tensor=lax.rem(t_me + k, nt)), device_id_type=MESH,
        )

    poles_mine[...] = jnp.zeros_like(poles_mine)
    poles_mine[:H, :M] = rates_ref[...]
    poles_mine[8 : 8 + H, :M] = angles_ref[...]
    for k in range(1, nt):
        pole_copy(k).start()
    for b in range(min(2, nb)):
        for k in range(1, nt):
            feature_copy(k, b, t_me).start()

    lane = lax.broadcasted_iota(jnp.int32, (8, 128), 1)
    sub = lax.broadcasted_iota(jnp.int32, (8, 128), 0)
    lanef = lane.astype(F32)
    in_chunk = lane % Q
    chunk = lane // Q
    square = lax.broadcasted_iota(jnp.int32, (M, M), 0) == lax.broadcasted_iota(jnp.int32, (M, M), 1)

    def upright(rates, turns):
        d = jnp.exp(jnp.sum(jnp.where(square, rates, 0.0), axis=1, keepdims=True))
        return d, jnp.sum(jnp.where(square, turns, 0.0), axis=1, keepdims=True)

    def powers_of(lag, d, a):
        size = jnp.exp(-d * lag)
        return size * jnp.cos(a * lag), size * jnp.sin(a * lag)

    def reach(ref):
        def one(h, _):
            d, a = upright(ref[pl.ds(h, 1), :][:, :M], ref[pl.ds(8 + h, 1), :][:, :M])
            re, im = powers_of(127.0 - lanef, d, a)
            step_re, step_im = powers_of(jnp.full((M, 128), float(B), F32), d, a)
            for b in reversed(range(nb)):
                kept = flag(seg(first + b * B + lane) == seg(first + R - 1))
                reach_s[rows_at(h * 16, 16, 16), b * B : b * B + B] = jnp.concatenate(
                    [re * kept, im * kept], axis=0
                ).astype(BF16)
                re, im = step_re * re - step_im * im, step_re * im + step_im * re
            return 0

        lax.fori_loop(0, H, one, 0)
        return dot(reach_s[...], feat[:, mine]).astype(BF16)

    own_in.wait()
    zbuf[:, mine] = reach(poles_mine)
    for k in range(1, nt):
        pole_copy(nt - k).wait_recv()
        zsnd[k - 1] = reach(poles_r.at[nt - k - 1])
        z_copy(k, t_me).start()
    for b in range(min(2, nb), nb):
        for k in range(1, nt):
            feature_copy(k, b, t_me).start()

    def tables(h, _):
        d, a = upright(rates_ref[pl.ds(h, 1), :], angles_ref[pl.ds(h, 1), :])

        def powers(lag, dd=d, aa=a):
            return powers_of(lag, dd, aa)

        pos_re, pos_im = powers(lanef)
        nxt_re, nxt_im = powers(lanef + 1.0)
        neg_re, neg_im = powers(-lanef - 1.0)
        end_re, end_im = powers(127.0 - lanef)
        far_re, far_im = powers(128.0 - lanef)
        b1_re, b1_im = powers((in_chunk + 1).astype(F32))
        b2_re, b2_im = powers((Q - in_chunk).astype(F32))
        pos_s[h, 0], pos_s[h, 1] = pos_re, pos_im
        for i, lag in enumerate((1.0, float(B), float(R))):
            pr, pi = powers(jnp.full((M, 128), lag, F32))
            pstep_s[h, i, 0], pstep_s[h, i, 1] = pr, pi
        y = 2.0 * d
        series = y * (1.0 - y / 2 * (1.0 - y / 3 * (1.0 - y / 4 * (1.0 - y / 5 * (1.0 - y / 6 * (1.0 - y / 7))))))
        wgt = jnp.sqrt(jnp.where(y < 0.25, series, 1.0 - jnp.exp(-y)))
        wgt = jnp.broadcast_to(wgt, (M, 128))
        wgt_s[h] = wgt
        wr, wi = resid_ref[0, h] * wgt, resid_ref[1, h] * wgt
        w_s[h, 0], w_s[h, 1] = wr, wi
        for k in range(Q):
            tap = jnp.sum(wr * pos_re[:, k : k + 1] - wi * pos_im[:, k : k + 1], axis=0, keepdims=True)
            if k == 0:
                tap = tap + skip_ref[h]
            k_s[h, k] = jnp.broadcast_to(tap, (8, 128))
        a1r, a1i, a2r, a2i, btr, bti, b2r, b2i = [], [], [], [], [], [], [], []
        subf = sub.astype(F32) * Q
        for m in range(M):
            one = slice(m, m + 1)
            pr, pi = powers(subf, d[one], a[one])
            pk_s[h, 0, m * 8 : m * 8 + 8], pk_s[h, 1, m * 8 : m * 8 + 8] = pr, pi
            back_re, back_im = powers(-subf - float(Q), d[one], a[one])
            fr, fi = neg_re[one], neg_im[one]
            past = lane < sub * Q
            a1r.append(jnp.where(past, pr * fr - pi * fi, 0.0))
            a1i.append(jnp.where(past, pr * fi + pi * fr, 0.0))
            fr, fi = pos_re[one], pos_im[one]
            later = lane >= (sub + 1) * Q
            a2r.append(jnp.where(later, back_re * fr - back_im * fi, 0.0))
            a2i.append(jnp.where(later, back_re * fi + back_im * fr, 0.0))
            here = chunk == sub
            btr.append(jnp.where(here, b1_re[one], 0.0))
            bti.append(jnp.where(here, b1_im[one], 0.0))
            b2r.append(jnp.where(here, b2_re[one], 0.0))
            b2i.append(jnp.where(here, b2_im[one], 0.0))
        a1_s[h] = jnp.concatenate(a1r + a1i + [end_re, end_im], axis=0).astype(BF16)
        a2_s[h] = jnp.concatenate(a2r + a2i + [pos_re, pos_im], axis=0).astype(BF16)
        bt = jnp.concatenate(btr + bti, axis=0)
        bt_s[h] = bt.astype(BF16)
        b1_s[h] = bt.T.astype(BF16)
        b2_s[h] = jnp.concatenate(b2r + b2i, axis=0).T.astype(BF16)
        pad = [jnp.zeros((128 - 2 * M, 128), F32)]
        colp_s[h] = jnp.concatenate([nxt_re, nxt_im] + pad, axis=0).T.astype(BF16)
        colh_s[h] = jnp.concatenate([far_re, far_im] + pad, axis=0).T.astype(BF16)
        return 0

    lax.fori_loop(0, H, tables, 0)
    u_s[...] = jnp.zeros_like(u_s)
    r_s[...] = jnp.zeros_like(r_s)
    rc_s[...] = jnp.zeros_like(rc_s)
    proj_in.wait()
    up_in.wait()

    def head(b, keep_block, h):
        rows = rows_at(b * B, B)
        xs = [x_scr[h, pl.ds(i, 8, stride=Q), :] for i in range(Q)]
        gs = [g_scr[h, pl.ds(i, 8, stride=Q), :] for i in range(Q)]
        held, corr = [], [None] * Q
        for i in range(Q):
            if i:
                kept = keep_s[i]
                held = [v * kept for v in held]
            held.append(xs[i])
            acc = None
            for s in range(i + 1):
                lag = i - s
                term = k_s[h, lag] * held[s]
                acc = term if acc is None else acc + term
                both = gs[i] * held[s]
                corr[lag] = both if corr[lag] is None else corr[lag] + both
            y_scr[h, pl.ds(i, 8, stride=Q), :] = acc
        for lag in range(Q):
            r_s[h, lag] += corr[lag]
        held = []
        for s in reversed(range(Q)):
            if s < Q - 1:
                kept = keep_s[s + 1]
                held = [v * kept for v in held]
            held = [gs[s]] + held
            acc = None
            for lag in range(Q - s):
                term = k_s[h, lag] * held[lag]
                acc = term if acc is None else acc + term
            gx_scr[h, pl.ds(s, 8, stride=Q), :] = acc

        states = dot(a1_s[h] * ma1_s[...], xb_s[h])
        leads = dot(bt_s[h], gm_s[h])
        adj = dot(a2_s[h] * ma2_s[...], gb_s[h])
        kept = km_s[...]
        vr, vi, ar, ai = [], [], [], []
        for m in range(M):
            re, im = slice(m * 8, m * 8 + 8), slice(64 + m * 8, 72 + m * 8)
            pr, pi = pk_s[h, 0, re] * kept, pk_s[h, 1, re] * kept
            ur, ui = u_s[h, m : m + 1, :], u_s[h, M + m : M + m + 1, :]
            sr = states[re] + (pr * ur - pi * ui)
            si = states[im] + (pr * ui + pi * ur)
            lr, li = leads[re], leads[im]
            rc_s[h, m] += sr * lr - si * li
            rc_s[h, M + m] += sr * li + si * lr
            wr, wi = w_s[h, 0, m : m + 1, :], w_s[h, 1, m : m + 1, :]
            vr.append(wr * sr - wi * si)
            vi.append(-(wr * si + wi * sr))
            ar.append(wr * adj[re] - wi * adj[im])
            ai.append(-(wr * adj[im] + wi * adj[re]))
        v = jnp.concatenate(vr + vi, axis=0).astype(BF16)
        y_loc[h, rows, :] = y_scr[h] + mb1_s[...] * dot(b1_s[h], v)
        v = jnp.concatenate(ar + ai, axis=0).astype(BF16)
        gx_loc[h, rows, :] = gx_scr[h] + mb2_s[...] * dot(b2_s[h], v)
        lead_s[b, h] = adj[128:]
        pr, pi = pstep_s[h, 1, 0] * keep_block, pstep_s[h, 1, 1] * keep_block
        ur, ui = u_s[h, :M, :], u_s[h, M:, :]
        u_s[h, :M, :] = states[128 : 128 + M] + (pr * ur - pi * ui)
        u_s[h, M:, :] = states[128 + M :] + (pr * ui + pi * ur)

    col = lax.broadcasted_iota(jnp.int32, (B, 128), 0)

    def block(b, _):
        begin = first + b * B
        rows = rows_at(b * B, B)
        seg_t = seg(begin + lane)
        same = flag(seg_t == seg(begin + sub * Q - 1))
        ma1_s[...] = jnp.concatenate([same] * 16 + [flag(seg_t == seg(begin + B - 1))] * 2, axis=0).astype(BF16)
        same = flag(seg_t == seg(begin + (sub + 1) * Q))
        ma2_s[...] = jnp.concatenate([same] * 16 + [flag(seg_t == seg(begin))] * 2, axis=0).astype(BF16)
        km_s[...] = flag(seg(begin + sub * Q - 1) == seg(begin - 1))
        for i in range(Q):
            at = begin + sub * Q + i
            keep_s[i] = flag(seg(at) == seg(at - 1))
        seg_c = seg(begin + col)
        mb1_s[...] = flag(seg_c == seg(begin + (col // Q) * Q - 1))
        mb2_s[...] = flag(seg_c == seg(begin + (col // Q + 1) * Q))
        keep_block = flag(seg(begin + B - 1) == seg(begin - 1))

        for k in range(1, nt):
            feature_copy(k, b, lax.rem(t_me - k + nt, nt)).wait_recv()
        fb = feat[rows, :]
        query = dot(fb, proj[0]).astype(BF16)
        signal = dot(fb, proj[1]).astype(BF16)
        q_s[rows, :] = query
        g = query.astype(F32) * up[rows, :].astype(F32)
        signal32 = signal.astype(F32)
        for h in range(H):
            cols = slice(h * 128, h * 128 + 128)
            x_scr[h] = signal32[:, cols]
            g_scr[h] = g[:, cols]
            xb_s[h] = signal[:, cols]
            gb_s[h] = g[:, cols].astype(BF16)
            gm_s[h] = (g[:, cols] * mb1_s[...]).astype(BF16)
        feat_t[b] = fb.T

        for h in range(H):
            head(b, keep_block, h)
        return 0

    def turned(h, which, re, im, kept):
        pr, pi = pstep_s[h, which, 0] * kept, pstep_s[h, which, 1] * kept
        return pr * re - pi * im, pr * im + pi * re

    def end_copy(src, dst, send, recv, slot, to):
        return pltpu.make_async_remote_copy(
            src_ref=src, dst_ref=dst.at[slot], send_sem=send.at[to], recv_sem=recv.at[slot],
            device_id=place(tm=to), device_id_type=MESH,
        )

    def forward_copy(slot, to):
        return end_copy(ue_s, endf_r, ef_s, ef_r, slot, to)

    def backward_copy(slot, to):
        return end_copy(d_s, endb_r, eb_s, eb_r, slot, to)

    def enter(src, _):
        @pl.when(src < z)
        def _():
            forward_copy(src, z).wait_recv()
            kept = flag(seg(src * R - 1) == seg(src * R + R - 1))
            for h in range(H):
                tr, ti = turned(h, 2, ent_s[h, :M, :], ent_s[h, M:, :], kept)
                ent_s[h, :M, :] = endf_r[src, h, :M, :] + tr
                ent_s[h, M:, :] = endf_r[src, h, M:, :] + ti

        return 0


    def weigh(h, re, im):
        wr, wi = w_s[h, 0], w_s[h, 1]
        pad = [jnp.zeros((128 - 2 * M, 128), F32)]
        return jnp.concatenate([wr * re - wi * im, -(wr * im + wi * re)] + pad, axis=0).astype(BF16)

    def enter_block(b, _):
        begin = first + b * B
        rows = rows_at(b * B, B)
        kept = flag(seg(begin + col) == seg(first - 1))
        for h in range(H):
            cols = slice(h * 128, h * 128 + 128)
            er, ei = ent_s[h, :M, :], ent_s[h, M:, :]
            y = y_loc[h, rows, :] + kept * dot(colp_s[h], weigh(h, er, ei))
            mixed_v[rows, cols] = (q_s[rows, cols].astype(F32) * y).astype(BF16)
            gq[rows, cols] = (up[rows, cols].astype(F32) * y).astype(BF16)
            ent_s[h, :M, :], ent_s[h, M:, :] = turned(h, 1, er, ei, 1.0)
        return 0

    def send_states():
        for k in range(1, nt):
            z_copy(k, lax.rem(t_me - k + nt, nt)).wait_recv()
        ends = dot(zbuf[...], proj[1])
        for h in range(H):
            ue_s[h] = ends[h * 16 : h * 16 + 16, h * 128 : h * 128 + 128]

        def go(to, _):
            @pl.when(to > z)
            def _():
                forward_copy(z, to).start()

            return 0

        lax.fori_loop(0, n, go, 0)

    def take_states():
        ent_s[...] = jnp.zeros_like(ent_s)
        lax.fori_loop(0, n, enter, 0)
        e0_s[...] = ent_s[...]
        lax.fori_loop(0, EARLY, enter_block, 0)

    def stream(b, _):
        pl.when(b == 1)(send_states)
        block(b, 0)
        pl.when(b == EARLY)(take_states)

        @pl.when(b >= EARLY)
        def _():
            enter_block(b, 0)

        return 0

    lax.fori_loop(0, nb, stream, 0)

    def reverse_scan(start, store):
        state = start
        for b in reversed(range(nb)):
            begin = first + b * B
            kept = flag(seg(begin) == seg(begin + B))
            following = []
            for h in range(H):
                re, im = state[h]
                if store:
                    g_end[b, h, :M, :], g_end[b, h, M:, :] = re, im
                tr, ti = turned(h, 1, re, im, kept)
                following.append((lead_s[b, h, :M, :] + tr, lead_s[b, h, M:, :] + ti))
            state = following
        return state

    mixed_copy = pltpu.make_async_copy(mixed_v, mixed_out, out_sem.at[0])
    mixed_copy.start()

    quarter = half // 2

    def partner_copy(k, i):
        r = rows_at(k * half + i * quarter, quarter)
        return pltpu.make_async_remote_copy(
            src_ref=dpsnd.at[r], dst_ref=dprcv.at[r], send_sem=dps_s.at[k, i], recv_sem=dps_r.at[k, i],
            device_id=place(dp=1 - core), device_id_type=MESH,
        )

    def transposed(start):
        return jnp.concatenate([feat_t[b, rows_at(start, quarter), :] for b in range(nb)], axis=1)

    def others_part(k, i, other):
        r = rows_at(k * half + i * quarter, quarter)
        dpsnd[r] = (dot(transposed((1 - core) * half + i * quarter), other[...]) * norm).astype(BF16)
        partner_copy(k, i).start()

    def own_part(k, i, other):
        r = rows_at(k * half + i * quarter, quarter)
        pacc[r] = dot(transposed(core * half + i * quarter), other[...]) * norm
        partner_copy(k, i).wait_recv()

        @pl.when(big.no_out)
        def _():
            def go(j, _):
                big.up(k * nch + i * (nch // 2) + j)
                return 0

            lax.fori_loop(0, nch // 2, go, 0)

    zero = jnp.zeros((M, 128), F32)
    ends = reverse_scan([(zero, zero)] * H, False)
    for h in range(H):
        d_s[h, :M, :], d_s[h, M:, :] = ends[h]

    def send_adjoint(to, _):
        @pl.when(to < z)
        def _():
            backward_copy(z, to).start()

        return 0

    lax.fori_loop(0, n, send_adjoint, 0)
    lea_s[...] = jnp.zeros_like(lea_s)

    others_part(0, 0, gq)
    others_part(0, 1, gq)
    own_part(0, 0, gq)
    own_part(0, 1, gq)
    kept_first = flag(seg(first) == seg(first - 1))
    for h in range(H):
        lr, li = turned(h, 0, d_s[h, :M, :], d_s[h, M:, :], kept_first)
        er, ei = e0_s[h, :M, :], e0_s[h, M:, :]
        re, im = [], []
        for m in range(M):
            re.append(jnp.sum(rc_s[h, m], axis=0, keepdims=True))
            im.append(jnp.sum(rc_s[h, M + m], axis=0, keepdims=True))
        re = jnp.concatenate(re, axis=0) + er * lr - ei * li
        im = jnp.concatenate(im, axis=0) + er * li + ei * lr
        for lag in range(Q):
            r = jnp.sum(r_s[h, lag], axis=0, keepdims=True)
            if lag == 0:
                skip_row = r
            re = re + pos_s[h, 0, :, lag : lag + 1] * r
            im = im + pos_s[h, 1, :, lag : lag + 1] * r
        cols = slice(h * 128, h * 128 + 128)
        scale = wgt_s[h] * norm
        terms = jnp.concatenate([re * scale, -im * scale, skip_row * norm, jnp.zeros((15, 128), F32)], axis=0)
        own = rows_at(core * 16, 16)
        mdps[:, cols] = jnp.where(core == 0, terms[16:], terms[:16])
        macc[:, cols] = jnp.where(core == 0, terms[:16], terms[16:])

    small_partner = pltpu.make_async_remote_copy(
        src_ref=mdps, dst_ref=mdpr, send_sem=md_s, recv_sem=md_r, device_id=place(dp=1 - core), device_id_type=MESH
    )
    small_partner.start()

    def leave(i, _):
        src = n - 1 - i

        @pl.when(src > z)
        def _():
            backward_copy(src, z).wait_recv()
            kept = flag(seg(src * R) == seg(src * R + R))
            for h in range(H):
                tr, ti = turned(h, 2, lea_s[h, :M, :], lea_s[h, M:, :], kept)
                lea_s[h, :M, :] = endb_r[src, h, :M, :] + tr
                lea_s[h, M:, :] = endb_r[src, h, M:, :] + ti

        return 0

    lax.fori_loop(0, n, leave, 0)
    reverse_scan([(lea_s[h, :M, :], lea_s[h, M:, :]) for h in range(H)], True)

    def ig_copy(k, b, sender):
        rows = rows_at(b * B, B)
        return pltpu.make_async_remote_copy(
            src_ref=igs.at[k - 1, rows], dst_ref=igr.at[k - 1, rows], send_sem=ig_s.at[k - 1, b],
            recv_sem=ig_r.at[k - 1, b], device_id=place(tensor=lax.rem(t_me + k, nt)), device_id_type=MESH,
        )

    def leave_block(b, _):
        begin = first + b * B
        rows = rows_at(b * B, B)
        kept = flag(seg(begin + col) == seg(begin + B))
        for h in range(H):
            cols = slice(h * 128, h * 128 + 128)
            gr, gi = g_end[b, h, :M, :], g_end[b, h, M:, :]
            gx = gx_loc[h, rows, :] + kept * dot(colh_s[h], weigh(h, gr, gi))
            gv[rows, cols] = gx.astype(BF16)
        for k in range(1, nt):
            to = lax.rem(t_me + k, nt)
            part = rows_at(to * share, share)
            igs[k - 1, rows, :] = (
                dot_nt(gq[rows, :], proj[0, part, :]) + dot_nt(gv[rows, :], proj[1, part, :])
            ).astype(BF16)
            ig_copy(k, b, t_me).start()
        return 0

    def ig_own(b, _):
        rows = rows_at(b * B, B)
        part = rows_at(t_me * share, share)
        iga[rows, :] = dot_nt(gq[rows, :], proj[0, part, :]) + dot_nt(gv[rows, :], proj[1, part, :])
        return 0

    steps = 2 * nch
    def middle_step(s, _=None):
        @pl.when(big.has_out & (s < steps))
        def _():
            big.up(s)

        @pl.when(big.has_out & (s >= LAG))
        def _():
            big.down(s - LAG)

        return 0

    def end_step(s, _):
        @pl.when(big.no_out)
        def _():
            big.down(s)

        return 0

    def ig_rest(b, _):
        rows = rows_at(b * B, B)
        total = iga[rows, :]
        for k in range(1, nt):
            ig_copy(k, b, t_me).wait_recv()
            total = total + igr[k - 1, rows, :].astype(F32)
        gv[rows, :share] = total.astype(BF16)
        return 0

    def pg_copy(g, c):
        r = big.total_row(g * GROUP, c, GROUP)
        return pltpu.make_async_copy(tot.at[r], pg_out.at[r], pg_sem.at[g, c])

    def finish(g, _):
        big.finish(g)
        pg_copy(g, 0).start()
        pg_copy(g, 1).start()
        return 0

    def written(g, _):
        pg_copy(g, 0).wait()
        pg_copy(g, 1).wait()
        return 0

    work = [functools.partial(lax.fori_loop, b, min(b + 2, nb), leave_block, 0) for b in range(1, nb, 2)]
    work += [functools.partial(others_part, 1, i, gv) for i in range(2)]
    work += [functools.partial(own_part, 1, i, gv) for i in range(2)]
    work += [functools.partial(lax.fori_loop, b, min(b + 3, nb), ig_own, 0) for b in range(0, nb, 3)]
    small_partner.wait_recv()
    pl.when(small.no_out)(lambda: small.up(0))
    leave_block(0, 0)
    for s, item in enumerate(work):
        middle_step(s)
        item()
        if s == len(work) - 2:
            pl.when(small.has_out)(lambda: small.up(0))
    rest = [functools.partial(lax.fori_loop, b, min(b + 2, nb), ig_rest, 0) for b in range(0, nb, 2)]
    last = steps - 1 - len(rest)
    lax.fori_loop(len(work), last, middle_step, 0)
    small.down(0)
    for s, item in enumerate(rest):
        middle_step(last + s)
        item()
    ig_out_copy = pltpu.make_async_copy(gv.at[:, :share], ig_out, out_sem.at[1])
    ig_out_copy.start()
    lax.fori_loop(0, nch, end_step, 0)
    middle_step(steps - 1)
    lax.fori_loop(0, nch // GROUP, finish, 0)
    lax.fori_loop(steps, steps + LAG, middle_step, 0)
    lax.fori_loop(nch, steps, end_step, 0)
    small.finish(0)
    res_copy = pltpu.make_async_copy(mtot.at[pl.ds(0, 2 * M)], res_out, out_sem.at[4])
    skip_copy = pltpu.make_async_copy(mtot.at[pl.ds(2 * M, 8)], skip_out, out_sem.at[5])
    res_copy.start()
    skip_copy.start()
    lax.fori_loop(nch // GROUP, steps // GROUP, finish, 0)

    for b in range(nb):
        for k in range(1, nt):
            feature_copy(k, b, t_me).wait_send()
            ig_copy(k, b, t_me).wait_send()
    for k in range(1, nt):
        pole_copy(k).wait_send()
        z_copy(k, t_me).wait_send()
    for k in range(2):
        for i in range(2):
            partner_copy(k, i).wait_send()
    small_partner.wait_send()

    def sent(to, _):
        @pl.when(to > z)
        def _():
            forward_copy(z, to).wait_send()

        @pl.when(to < z)
        def _():
            backward_copy(z, to).wait_send()

        return 0

    lax.fori_loop(0, n, sent, 0)
    mixed_copy.wait()
    ig_out_copy.wait()
    lax.fori_loop(0, steps // GROUP, written, 0)
    res_copy.wait()
    skip_copy.wait()


def assemble_kernel(mixed, ig, pg, res, skips, mixed_o, ig_o, pg_o, res_o, skip_o, wide, sems):
    parts, rows = wide.shape[:2]
    stores = [pltpu.make_async_copy(wide.at[i], pg_o.at[pl.ds(i * rows, rows)], sems.at[i]) for i in range(parts)]
    for i, (src, dst) in enumerate(((mixed, mixed_o), (ig, ig_o), (res, res_o), (skips.at[pl.ds(0, 1)], skip_o))):
        stores.append(pltpu.make_async_copy(src, dst, sems.at[parts + i]))
        stores[-1].start()
    for i in range(parts):
        wide[i] = pg[pl.ds(i * rows, rows), :].astype(F32)
        stores[i].start()
    for copy in stores:
        copy.wait()


def shards(frames_in, in_proj, log_rates, angles, residues, skip_gain, lengths, grad_out):
    R, C = frames_in.shape[1:]
    D = in_proj.shape[1]
    M, H = log_rates.shape
    clips = lengths.shape[1]
    n, nt = lax.axis_size("tm"), lax.axis_size("tensor")
    nb = R // B
    norm = 1.0 / math.sqrt(R * n * lax.axis_size("dp"))
    half = D // 2
    nch = half // STEP
    share = D // nt
    resid = residues.reshape(2, M, H, 128).transpose(0, 2, 1, 3)
    skip = skip_gain.reshape(H, 1, 128)
    vm, dma = pltpu.VMEM, pltpu.SemaphoreType.DMA

    def chain_sems(steps, group):
        return [dma((steps,))] * 5 + [dma((steps // group,))] * 2

    scratch = [
        vm((R, D), BF16), vm((nb, D, B), BF16), vm((2, D, C), BF16), vm((R, C), BF16), vm((R, C), BF16),
        vm((H, B, 128), F32), vm((H, B, 128), F32), vm((H, B, 128), F32), vm((H, B, 128), F32),
        vm((H, B, 128), BF16), vm((H, B, 128), BF16), vm((H, B, 128), BF16),
        vm((H, R, 128), F32), vm((H, R, 128), F32), vm((R, C), BF16), vm((R, C), BF16), vm((R, C), BF16),
        vm((H, 144, 128), BF16), vm((H, 144, 128), BF16), vm((H, 128, 128), BF16), vm((H, 128, 128), BF16),
        vm((H, 128, 128), BF16), vm((H, 128, 128), BF16), vm((H, 128, 128), BF16),
        vm((H, 2, 8 * M, 128), F32), vm((H, 2, M, 128), F32), vm((H, 3, 2, M, 128), F32), vm((H, 2, M, 128), F32),
        vm((H, Q, 8, 128), F32), vm((H, M, 128), F32),
        vm((144, 128), BF16), vm((144, 128), BF16), vm((Q, 8, 128), F32), vm((8, 128), F32), vm((B, 128), F32),
        vm((B, 128), F32),
        vm((H, 2 * M, 128), F32), vm((H, 2 * M, 128), F32), vm((nb, H, 2 * M, 128), F32), vm((nb, H, 2 * M, 128), F32),
        vm((H, Q, 8, 128), F32), vm((H, 2 * M, 8, 128), F32), vm((H, 2 * M, 128), F32), vm((H, 2 * M, 128), F32),
        vm((n, H, 2 * M, 128), F32), vm((n, H, 2 * M, 128), F32),
        vm((2 * half, C), F32), vm((2 * half, C), BF16), vm((2 * half, C), BF16), vm((2 * half, C), BF16),
        vm((2 * half, C), BF16), vm((2 * half, C), BF16), vm((2 * D, C), BF16),
        vm((16, C), F32), vm((16, C), F32), vm((16, C), F32), vm((16, C), F32), vm((16, C), F32), vm((16, C), F32),
        vm((32, C), F32),
        vm((nt - 1, R, share), BF16), vm((nt - 1, R, share), BF16), vm((R, share), F32),
        vm((16, 128), F32), vm((nt - 1, 16, 128), F32), vm((16 * H, R), BF16), vm((nt - 1, 16 * H, C), BF16),
        vm((16 * H, D), BF16), vm((H, 2 * M, 128), F32), vm((H, 2 * M, 128), F32),
        dma((nt - 1,)), dma((nt - 1,)), dma((nt - 1,)), dma((nt - 1,)),
        dma((3,)), dma((nt - 1, nb)), dma((nt - 1, nb)), dma((n,)), dma((n,)), dma((n,)), dma((n,)),
        dma((2, 2)), dma((2, 2)), dma((nt - 1, nb)), dma((nt - 1, nb)), dma, dma, dma((6,)), dma((2 * nch // GROUP, 2)),
    ] + chain_sems(2 * nch, GROUP) + chain_sems(1, 1)
    vmem = pl.BlockSpec(memory_space=pltpu.VMEM)
    anywhere = pl.BlockSpec(memory_space=pl.ANY)
    mixed, ig, pg, res, skips = pl.pallas_call(
        functools.partial(layer_kernel, (clips, M, H, R, C, D, norm)),
        out_shape=[
            vm((R, C), BF16), vm((R, share), BF16), vm((2 * D, C), BF16), vm((2 * M, C), F32), vm((8, C), F32),
        ],
        in_specs=[pl.BlockSpec(memory_space=pltpu.SMEM)] + [vmem] * 4 + [anywhere] * 3,
        out_specs=[vmem] * 5,
        scratch_shapes=scratch,
        compiler_params=pltpu.CompilerParams(
            collective_id=0, has_side_effects=True, vmem_limit_bytes=56 << 20
        ),
        name="layer",
    )(lengths, log_rates.T, angles.T, resid, skip, frames_in[0], in_proj, grad_out[0])
    parts = 8
    mixed, ig, pg, res, skips = pl.pallas_call(
        assemble_kernel,
        out_shape=[
            jax.ShapeDtypeStruct((R, C), BF16), jax.ShapeDtypeStruct((R, share), BF16),
            jax.ShapeDtypeStruct((2 * D, C), F32), jax.ShapeDtypeStruct((2 * M, C), F32),
            jax.ShapeDtypeStruct((1, C), F32),
        ],
        in_specs=[vmem] * 5,
        out_specs=[anywhere] * 5,
        scratch_shapes=[vm((parts, 2 * D // parts, C), F32), dma((parts + 4,))],
        compiler_params=pltpu.CompilerParams(vmem_limit_bytes=20 << 20),
        name="assemble",
    )(mixed, ig, pg, res, skips)
    return mixed[None], ig[None], pg.reshape(2, D, C), res.reshape(2, M, C), skips[0]


def solution(mesh):
    in_specs = (
        P(("group", "dp"), "tm", "tensor"),
        P(None, None, "tensor"),
        P(None, "tensor"),
        P(None, "tensor"),
        P(None, None, "tensor"),
        P("tensor"),
        P(("group", "dp"), None),
        P(("group", "dp"), "tm", "tensor"),
    )
    out_specs = (
        P(("group", "dp"), "tm", "tensor"),
        P(("group", "dp"), "tm", "tensor"),
        P("group", None, "tensor"),
        P("group", None, "tensor"),
        P(("group", "tensor")),
    )
    return jax.shard_map(shards, mesh=mesh, in_specs=in_specs, out_specs=out_specs, check_vma=False)
```
